32 devices in a mesh: dp: 8 (over y, x, core), group: 4 (over z).
Axes of the slice: x: 2, y: 2, z: 4, core: 2. Of those that a mesh axis runs over, the one named last changes fastest.
Arguments:
- tokens: bfloat16 [4096, 768], P(('dp', 'group')), may hold values from -6 to 6
- grad_out: bfloat16 [4096, 768], P(('dp', 'group')), may hold values from -6 to 6
- segment_ids: int32 [4096], P(('dp', 'group')), may hold values from 0 to 1023, as said below
- positions: int32 [4096], P(('dp', 'group')), may hold values from 0 to 511, as said below
- counts: int32 [32], P(('dp', 'group')), may hold values from 64 to 128, as said below
- master: float32 [7090176], P(('dp', 'group'))
- moment_one: float32 [7090176], P(('dp', 'group')), may hold values from -0.00021362305 to 0.00021362305
- moment_two: float32 [7090176], P(('dp', 'group')), may hold values from 2.8208045e-09 to 2.8208044e-08
Outputs:
- block_out: bfloat16 [4096, 768], P(('dp', 'group'))
- grad_in: bfloat16 [4096, 768], P(('dp', 'group'))
- weight_grads: float32 [7090176], P(('dp', 'group'))
- new_master: float32 [7090176], P(('dp', 'group'))
- new_moment_one: float32 [7090176], P(('dp', 'group'))
- new_moment_two: float32 [7090176], P(('dp', 'group'))
The draws below stay inside these ranges and needn't reach their ends.
Inputs may be any that keep to these rules, and one draw needn't show every extreme that they name: `counts`: in every batch of 4 devices at least one device uses all 128 slots; a device's used slots come first. The first batch uses all its slots; in the last batch the last device uses 128 // 2. `segment_ids`: used slots of a batch carry sequence numbers that never fall along the batch; the unused slot j of a batch carries 512 + j. A sequence may run over several devices of its batch; the first batch holds one sequence. `positions`: used slots carry their position counted from 0 within their sequence in slot order; unused slots carry 0.
All inputs are finite; a program needn't handle non-finite values.
Results may differ from the reference program's by a relative error of at most 0.019.
Values may be sent and summed in bfloat16 or wider, within the bound.
A program may use at most 192 MiB of HBM per device.

```python
import math
import jax
import jax.numpy as jnp
from jax import lax

D = 768
FF = 3072
HEAD = 64
ROT = 16
STEP = 3
TOK_DEV = 128
GROUP_SIZE = 4
BATCHES = 8
GROUP_ROWS = 512
TOKENS = 4096
NPAR = 7090176
DEVICES = 32


start_odds = 384


def param_layout_drawn(model_width, hidden):
    return [('weight_qkv', (model_width, 3 * model_width)), ('bias_qkv', (3 * model_width,)), ('weight_out', (model_width, model_width)), ('bias_out', (model_width,)), ('weight_up', (model_width, hidden)), ('bias_up', (hidden,)), ('weight_down', (hidden, model_width)), ('bias_down', (model_width,)), ('gain_attn', (model_width,)), ('shift_attn', (model_width,)), ('gain_mlp', (model_width,)), ('shift_mlp', (model_width,))]


def packing(key):
    base_key = jax.random.fold_in(key, 11)
    key_counts, key_full, key_coin = jax.random.split(base_key, 3)
    counts = jax.random.randint(key_counts, (BATCHES, GROUP_SIZE), TOK_DEV // 2, TOK_DEV + 1)
    full_device = jax.random.randint(key_full, (BATCHES,), 0, GROUP_SIZE)
    batch_index = jnp.arange(BATCHES)[:, None]
    device_index = jnp.arange(GROUP_SIZE)[None, :]
    full_device = jnp.where(jnp.arange(BATCHES) == BATCHES - 1, 0, full_device)
    counts = jnp.where(device_index == full_device[:, None], TOK_DEV, counts)
    counts = jnp.where(batch_index == 0, TOK_DEV, counts)
    counts = jnp.where((batch_index == BATCHES - 1) & (device_index == GROUP_SIZE - 1), TOK_DEV // 2, counts)
    counts = counts.astype(jnp.int32)
    valid_rows = (jnp.arange(TOK_DEV)[None, None, :] < counts[:, :, None]).reshape(BATCHES, GROUP_ROWS)
    valid_rank = jnp.cumsum(valid_rows.astype(jnp.int32), 1) - 1
    coin_draw = jax.random.randint(key_coin, (BATCHES, GROUP_ROWS), 0, start_odds)
    coin_start = (coin_draw == 0) & (batch_index > 0)
    starts = valid_rows & (coin_start | (valid_rank == 0))
    segment = jnp.cumsum(starts.astype(jnp.int32), 1) - 1
    slot_index = jnp.arange(GROUP_ROWS, dtype=jnp.int32)[None, :]
    segment = jnp.where(valid_rows, segment, GROUP_ROWS + slot_index)
    start_rank = lax.cummax(jnp.where(starts, valid_rank, -1), axis=1)
    position = jnp.where(valid_rows, valid_rank - start_rank, 0)
    return (counts.reshape(DEVICES), segment.reshape(TOKENS).astype(jnp.int32), position.reshape(TOKENS).astype(jnp.int32))


def draw_counts(key, part):
    return packing(key)[0]


def draw_segment_ids(key, part):
    return packing(key)[1]


def draw_positions(key, part):
    return packing(key)[2]


def draw_master(key, part):
    flat_index = jnp.arange(NPAR)
    raw_values = jax.random.normal(key, (NPAR,), jnp.float32)
    scale_table = {'weight_qkv': D ** (-0.5), 'bias_qkv': 0.1, 'weight_out': 3.0 * D ** (-0.5), 'bias_out': 0.1, 'weight_up': D ** (-0.5), 'bias_up': 0.1, 'weight_down': FF ** (-0.5), 'bias_down': 0.1, 'gain_attn': 0.1, 'shift_attn': 0.1, 'gain_mlp': 0.1, 'shift_mlp': 0.1}
    scale_vec = jnp.full((NPAR,), 0.02, jnp.float32)
    shift_vec = jnp.zeros((NPAR,), jnp.float32)
    offset = 0
    for entry_name, entry_shape in param_layout_drawn(D, FF):
        length = 1
        for extent in entry_shape:
            length = length * extent
        inside = (flat_index >= offset) & (flat_index < offset + length)
        scale_vec = jnp.where(inside, scale_table[entry_name], scale_vec)
        if entry_name in ('gain_attn', 'gain_mlp'):
            shift_vec = jnp.where(inside, 1.0, shift_vec)
        offset = offset + length
    return raw_values * scale_vec + shift_vec


def levels(key, shape, cuts, least, top_value):
    gain, own = 1.0, jax.random.fold_in(key, 6)
    for axis_at, parts in cuts:
        steps = jnp.exp(jax.random.uniform(jax.random.fold_in(own, axis_at), (parts,), jnp.float32, least / len(cuts), top_value / len(cuts)))
        gain = gain * jnp.repeat(steps, shape[axis_at] // parts).reshape([-1 if axis == axis_at else 1 for axis in range(len(shape))])
    return gain


def bell_draw(key, shape, width, limit, cuts=(), kind=jnp.bfloat16):
    loudness = levels(key, shape, cuts, -0.22, 0.18) if cuts else 1.0
    values = jax.random.normal(key, shape, jnp.float32) * width * loudness
    return jnp.minimum(jnp.maximum(values, -limit), limit).astype(kind)


def setup_inputs(seed: int = 0) -> dict:
    splits = jax.random.split(jax.random.key(seed), 9)
    return {
        "tokens": bell_draw(splits[0], (TOKENS, D), 1.0, 6.0, ((0, 32),)),
        "grad_out": bell_draw(splits[1], (TOKENS, D), 1.0, 6.0, ((0, 32),)),
        "segment_ids": draw_segment_ids(jax.random.fold_in(splits[8], 71), 0),
        "positions": draw_positions(jax.random.fold_in(splits[8], 71), 0),
        "counts": draw_counts(jax.random.fold_in(splits[8], 71), 0),
        "master": draw_master(jax.random.fold_in(splits[8], 71), 0),
        "moment_one": bell_draw(splits[6], (NPAR,), (0.1 / NPAR ** 0.5), 0.00021362305, ((0, 32),), jnp.float32),
        "moment_two": jnp.clip(jnp.exp(math.log(2.8208043900690427e-08) - 2.3025851 * jax.random.uniform(splits[7], (NPAR,), jnp.float32) ** levels(splits[7], (NPAR,), ((0, 32),), -0.2, 0.2)), 2.8208044788868847e-09, 2.8208043900690427e-08),
    }


BETA_ONE = 0.9
BETA_TWO = 0.95
LEARN_RATE = 0.01
DECAY_RATE = 0.1
ADAM_EPS = 1e-08
NORM_EPS = 1e-05
SCORE_SCALE = 0.125
MASKED = -1e+30

def param_layout(model_width, hidden):
    return [('weight_qkv', (model_width, 3 * model_width)), ('bias_qkv', (3 * model_width,)), ('weight_out', (model_width, model_width)), ('bias_out', (model_width,)), ('weight_up', (model_width, hidden)), ('bias_up', (hidden,)), ('weight_down', (hidden, model_width)), ('bias_down', (model_width,)), ('gain_attn', (model_width,)), ('shift_attn', (model_width,)), ('gain_mlp', (model_width,)), ('shift_mlp', (model_width,))]

def unpack_params(flat_params, model_width, hidden):
    result = {}
    offset = 0
    for entry_name, entry_shape in param_layout(model_width, hidden):
        length = 1
        for extent in entry_shape:
            length = length * extent
        result[entry_name] = flat_params[offset:offset + length].reshape(entry_shape)
        offset = offset + length
    return result

def pack_grads(grad_dict, model_width, hidden, total_len):
    pieces = []
    used_count = 0
    for entry_name, entry_shape in param_layout(model_width, hidden):
        flat_grad = grad_dict[entry_name].reshape(-1)
        pieces.append(flat_grad)
        used_count = used_count + flat_grad.shape[0]
    pieces.append(jnp.zeros((total_len - used_count,), jnp.float32))
    return jnp.concatenate(pieces)

def rotary_tables(pos_ids):
    half_rot = ROT // 2
    inverse_freq = 10000.0 ** (-jnp.arange(half_rot, dtype=jnp.float32) * 2.0 / ROT)
    angles = pos_ids.astype(jnp.float32)[:, None] * inverse_freq[None, :]
    return (jnp.cos(angles), jnp.sin(angles))

def rotate(values, cosine, sine_rows):
    half_rot = ROT // 2
    lower_part = values[..., :half_rot]
    upper_part = values[..., half_rot:ROT]
    cos_rows = cosine[:, None, :]
    sin_rows = sine_rows[:, None, :]
    return jnp.concatenate([lower_part * cos_rows - upper_part * sin_rows, upper_part * cos_rows + lower_part * sin_rows, values[..., ROT:]], -1)

def rotate_back(values, cosine, sine_rows):
    half_rot = ROT // 2
    lower_part = values[..., :half_rot]
    upper_part = values[..., half_rot:ROT]
    cos_rows = cosine[:, None, :]
    sin_rows = sine_rows[:, None, :]
    return jnp.concatenate([lower_part * cos_rows + upper_part * sin_rows, upper_part * cos_rows - lower_part * sin_rows, values[..., ROT:]], -1)

def layer_stats(block_in):
    centred = block_in - lax.optimization_barrier(jnp.mean(block_in, -1, keepdims=True))
    inv_std = lax.rsqrt(lax.optimization_barrier(jnp.mean(centred * centred, -1, keepdims=True)) + NORM_EPS)
    return (centred * inv_std, inv_std)

def norm_backward(grad_normed, normed, inv_std):
    return inv_std * (grad_normed - lax.optimization_barrier(jnp.mean(grad_normed, -1, keepdims=True)) - normed * lax.optimization_barrier(jnp.mean(grad_normed * normed, -1, keepdims=True)))

def gelu_slope(up_pre):
    return 0.5 * (1.0 + lax.erf(up_pre * 0.7071067811865476)) + up_pre * jnp.exp(-0.5 * up_pre * up_pre) * 0.3989422804014327

def group_pass(block_tokens, cotangent, seg_ids, pos_ids, valid_rows, params):
    rows_here = block_tokens.shape[0]
    head_count = D // HEAD
    block_in = block_tokens.astype(jnp.float32)
    normed, inv_std = layer_stats(block_in)
    gain_attn = params['gain_attn'].astype(jnp.float32)
    gain_mlp = params['gain_mlp'].astype(jnp.float32)
    attn_in = (normed * gain_attn + params['shift_attn'].astype(jnp.float32)).astype(jnp.bfloat16)
    mlp_in = (normed * gain_mlp + params['shift_mlp'].astype(jnp.float32)).astype(jnp.bfloat16)
    qkv_pre = (jnp.dot(attn_in, params['weight_qkv'], preferred_element_type=jnp.float32) + params['bias_qkv'].astype(jnp.float32)).reshape(rows_here, 3, head_count, HEAD)
    cosine, sine_rows = rotary_tables(pos_ids)
    queries = rotate(qkv_pre[:, 0], cosine, sine_rows).astype(jnp.bfloat16)
    keys_rot = rotate(qkv_pre[:, 1], cosine, sine_rows).astype(jnp.bfloat16)
    values = qkv_pre[:, 2].astype(jnp.bfloat16)
    slot_index = jnp.arange(rows_here)
    allowed = (seg_ids[:, None] == seg_ids[None, :]) & (slot_index[None, :] <= slot_index[:, None])
    scores = jnp.einsum('qhd,khd->hqk', queries.astype(jnp.float32), keys_rot.astype(jnp.float32)) * SCORE_SCALE
    scores = jnp.where(allowed[None], scores, MASKED)
    row_max = lax.optimization_barrier(jnp.max(scores, -1, keepdims=True))
    log_total = row_max + jnp.log(lax.optimization_barrier(jnp.sum(jnp.exp(scores - row_max), -1, keepdims=True)))
    attn_probs = jnp.exp(scores - log_total)
    probs_low = attn_probs.astype(jnp.bfloat16)
    context = jnp.einsum('hqk,khd->qhd', probs_low.astype(jnp.float32), values.astype(jnp.float32)).astype(jnp.bfloat16)
    context_flat = context.reshape(rows_here, D)
    attn_out = jnp.dot(context_flat, params['weight_out'], preferred_element_type=jnp.float32) + params['bias_out'].astype(jnp.float32)
    up_pre = jnp.dot(mlp_in, params['weight_up'], preferred_element_type=jnp.float32) + params['bias_up'].astype(jnp.float32)
    up_act = jax.nn.gelu(up_pre, approximate=False).astype(jnp.bfloat16)
    mlp_out = jnp.dot(up_act, params['weight_down'], preferred_element_type=jnp.float32) + params['bias_down'].astype(jnp.float32)
    block_out = (block_in + attn_out + mlp_out).astype(jnp.bfloat16)
    grad_rows = cotangent.astype(jnp.float32) * valid_rows[:, None]
    grad_low = grad_rows.astype(jnp.bfloat16)
    bias_grad = lax.optimization_barrier(jnp.sum(grad_rows, 0))
    grad_dict = {}
    grad_dict['weight_down'] = jnp.dot(up_act.T, grad_low, preferred_element_type=jnp.float32)
    grad_dict['bias_down'] = bias_grad
    grad_dict['weight_out'] = jnp.dot(context_flat.T, grad_low, preferred_element_type=jnp.float32)
    grad_dict['bias_out'] = bias_grad
    grad_act = jnp.dot(grad_low, params['weight_down'].T, preferred_element_type=jnp.float32)
    grad_pre = (grad_act * gelu_slope(up_pre)).astype(jnp.bfloat16)
    grad_dict['weight_up'] = jnp.dot(mlp_in.T, grad_pre, preferred_element_type=jnp.float32)
    grad_dict['bias_up'] = lax.optimization_barrier(jnp.sum(grad_pre.astype(jnp.float32), 0))
    grad_mlp_in = jnp.dot(grad_pre, params['weight_up'].T, preferred_element_type=jnp.float32)
    grad_context = jnp.dot(grad_low, params['weight_out'].T, preferred_element_type=jnp.float32).astype(jnp.bfloat16)
    grad_context = grad_context.reshape(rows_here, head_count, HEAD)
    row_delta = jnp.einsum('qhd,qhd->hq', grad_context.astype(jnp.float32), context.astype(jnp.float32))
    grad_probs = jnp.einsum('qhd,khd->hqk', grad_context.astype(jnp.float32), values.astype(jnp.float32))
    grad_scores = (attn_probs * (grad_probs - row_delta[..., None]) * SCORE_SCALE).astype(jnp.bfloat16)
    grad_queries = jnp.einsum('hqk,khd->qhd', grad_scores.astype(jnp.float32), keys_rot.astype(jnp.float32))
    grad_keys = jnp.einsum('hqk,qhd->khd', grad_scores.astype(jnp.float32), queries.astype(jnp.float32))
    grad_values = jnp.einsum('hqk,qhd->khd', probs_low.astype(jnp.float32), grad_context.astype(jnp.float32))
    grad_qkv = jnp.stack([rotate_back(grad_queries, cosine, sine_rows), rotate_back(grad_keys, cosine, sine_rows), grad_values], 1).reshape(rows_here, 3 * D).astype(jnp.bfloat16)
    grad_dict['weight_qkv'] = jnp.dot(attn_in.T, grad_qkv, preferred_element_type=jnp.float32)
    grad_dict['bias_qkv'] = lax.optimization_barrier(jnp.sum(grad_qkv.astype(jnp.float32), 0))
    grad_attn_in = jnp.dot(grad_qkv, params['weight_qkv'].T, preferred_element_type=jnp.float32)
    grad_dict['gain_attn'] = lax.optimization_barrier(jnp.sum(grad_attn_in * normed, 0))
    grad_dict['shift_attn'] = lax.optimization_barrier(jnp.sum(grad_attn_in, 0))
    grad_dict['gain_mlp'] = lax.optimization_barrier(jnp.sum(grad_mlp_in * normed, 0))
    grad_dict['shift_mlp'] = lax.optimization_barrier(jnp.sum(grad_mlp_in, 0))
    grad_normed = grad_attn_in * gain_attn + grad_mlp_in * gain_mlp
    grad_in = (grad_rows + norm_backward(grad_normed, normed, inv_std)).astype(jnp.bfloat16)
    return (block_out, grad_in, grad_dict)

def reference(tokens, grad_out, segment_ids, positions, counts, master, moment_one, moment_two):
    params = unpack_params(master.astype(jnp.bfloat16), D, FF)
    valid_rows = (jnp.arange(TOK_DEV)[None, :] < counts[:, None]).astype(jnp.float32).reshape(BATCHES, GROUP_ROWS)
    inputs_all = (tokens.reshape(BATCHES, GROUP_ROWS, D), grad_out.reshape(BATCHES, GROUP_ROWS, D), segment_ids.reshape(BATCHES, GROUP_ROWS), positions.reshape(BATCHES, GROUP_ROWS), valid_rows)
    zero_grads = {}
    for entry_name, entry_shape in param_layout(D, FF):
        zero_grads[entry_name] = jnp.zeros(entry_shape, jnp.float32)

    def scan_group(totals, group_inputs):
        block_tokens, cotangent, seg_ids, pos_ids, valid_here = group_inputs
        block_out, grad_in, grad_dict = group_pass(block_tokens, cotangent, seg_ids, pos_ids, valid_here, params)
        summed = jax.tree.map(lambda running, addend: running + addend, totals, grad_dict)
        return (summed, (block_out, grad_in))
    totals, (outs_all, grads_all) = lax.scan(scan_group, zero_grads, inputs_all)
    flat_grads = pack_grads(totals, D, FF, NPAR)
    square_sum = jnp.sum(flat_grads * flat_grads)
    grad_scale = 1.0 / (jnp.sqrt(square_sum) + 1e-06)
    scaled = flat_grads * grad_scale
    new_one = BETA_ONE * moment_one + (1.0 - BETA_ONE) * scaled
    new_two = BETA_TWO * moment_two + (1.0 - BETA_TWO) * scaled * scaled
    correct_one = 1.0 - BETA_ONE ** STEP
    correct_two = 1.0 - BETA_TWO ** STEP
    new_master = master - LEARN_RATE * (new_one / correct_one / (jnp.sqrt(new_two / correct_two) + ADAM_EPS) + DECAY_RATE * master)
    return (outs_all.reshape(TOKENS, D), grads_all.reshape(TOKENS, D), flat_grads, new_master, new_one, new_two)
```

```python
import functools

import jax
import jax.numpy as jnp
import numpy as np
from jax import lax
from jax.experimental import pallas as pl
from jax.experimental.pallas import tpu as pltpu
from jax.sharding import PartitionSpec as P

FF = 3072
HEAD = 64
ROT = 16
STEP = 3


BETA_ONE = 0.9
BETA_TWO = 0.95
LEARN_RATE = 0.01
DECAY_RATE = 0.1
ADAM_EPS = 1e-08
NORM_EPS = 1e-05
SCORE_SCALE = 0.125
MASKED = -1e30
TILE_ROWS = 16
MESH = pl.DeviceIdType.MESH
DMA = pltpu.SemaphoreType.DMA
ANY = pl.BlockSpec(memory_space=pl.ANY)
INVMEM = pl.BlockSpec(memory_space=pltpu.VMEM)


def param_layout(model_width, hidden):
    return [
        ("weight_qkv", (model_width, 3 * model_width)),
        ("bias_qkv", (3 * model_width,)),
        ("weight_out", (model_width, model_width)),
        ("bias_out", (model_width,)),
        ("weight_up", (model_width, hidden)),
        ("bias_up", (hidden,)),
        ("weight_down", (hidden, model_width)),
        ("bias_down", (model_width,)),
        ("gain_attn", (model_width,)),
        ("shift_attn", (model_width,)),
        ("gain_mlp", (model_width,)),
        ("shift_mlp", (model_width,)),
    ]


def unpack_params(flat_params, model_width, hidden):
    result = {}
    offset = 0
    for entry_name, entry_shape in param_layout(model_width, hidden):
        length = 1
        for extent in entry_shape:
            length = length * extent
        result[entry_name] = flat_params[offset : offset + length].reshape(entry_shape)
        offset = offset + length
    return result


def pack_grads(grad_dict, model_width, hidden, total_len):
    pieces = []
    used_count = 0
    for entry_name, entry_shape in param_layout(model_width, hidden):
        flat_grad = grad_dict[entry_name].reshape(-1)
        pieces.append(flat_grad)
        used_count = used_count + flat_grad.shape[0]
    pieces.append(jnp.zeros((total_len - used_count,), jnp.float32))
    return jnp.concatenate(pieces)


def rotary_tables(pos_ids):
    half_rot = ROT // 2
    inverse_freq = 10000.0 ** (-jnp.arange(half_rot, dtype=jnp.float32) * 2.0 / ROT)
    angles = pos_ids.astype(jnp.float32)[:, None] * inverse_freq[None, :]
    return (jnp.cos(angles), jnp.sin(angles))


def rotate(values, cosine, sine_rows):
    half_rot = ROT // 2
    lower_part = values[..., :half_rot]
    upper_part = values[..., half_rot:ROT]
    cos_rows = cosine[:, None, :]
    sin_rows = sine_rows[:, None, :]
    return jnp.concatenate(
        [
            lower_part * cos_rows - upper_part * sin_rows,
            upper_part * cos_rows + lower_part * sin_rows,
            values[..., ROT:],
        ],
        -1,
    )


def rotate_back(values, cosine, sine_rows):
    half_rot = ROT // 2
    lower_part = values[..., :half_rot]
    upper_part = values[..., half_rot:ROT]
    cos_rows = cosine[:, None, :]
    sin_rows = sine_rows[:, None, :]
    return jnp.concatenate(
        [
            lower_part * cos_rows + upper_part * sin_rows,
            upper_part * cos_rows - lower_part * sin_rows,
            values[..., ROT:],
        ],
        -1,
    )


def layer_stats(block_in):
    centred = block_in - jnp.mean(block_in, -1, keepdims=True)
    inv_std = lax.rsqrt(jnp.mean(centred * centred, -1, keepdims=True) + NORM_EPS)
    return (centred * inv_std, inv_std)


def norm_backward(grad_normed, normed, inv_std):
    return inv_std * (
        grad_normed
        - jnp.mean(grad_normed, -1, keepdims=True)
        - normed * jnp.mean(grad_normed * normed, -1, keepdims=True)
    )


def gelu_slope(up_pre):
    return (
        0.5 * (1.0 + lax.erf(up_pre * 0.7071067811865476))
        + up_pre * jnp.exp(-0.5 * up_pre * up_pre) * 0.3989422804014327
    )


def masked_scores(query_part, key_part, query_seg, key_seg, query_slot, key_slot):
    scores = (
        jnp.einsum("qhd,khd->hqk", query_part, key_part, preferred_element_type=jnp.float32)
        * SCORE_SCALE
    )
    allowed = (query_seg[:, None] == key_seg[None, :]) & (key_slot[None, :] <= query_slot[:, None])
    return (jnp.where(allowed[None], scores, MASKED), allowed)


def score_grads(scores, allowed, log_total, row_delta, grad_context, value_part):
    attn_probs = jnp.where(allowed[None], jnp.exp(scores - log_total[..., None]), 0.0)
    grad_probs = jnp.einsum(
        "qhd,khd->hqk", grad_context, value_part, preferred_element_type=jnp.float32
    )
    grad_scores = (attn_probs * (grad_probs - row_delta[..., None]) * SCORE_SCALE).astype(
        jnp.bfloat16
    )
    return (attn_probs.astype(jnp.bfloat16), grad_scores)


def on_device_gathered(tokens, grad_out, segment_ids, positions, counts, master, moment_one, moment_two):
    local_rows = tokens.shape[0]
    model_width = tokens.shape[1]
    head_count = model_width // HEAD
    local_master = master.astype(jnp.bfloat16)
    sectioned = lax.all_gather(local_master.reshape(1, 1, -1), "group", axis=1, tiled=True)
    sectioned = lax.all_gather(sectioned, "dp", axis=0, tiled=True)
    flat_params = sectioned.reshape(-1)
    params = unpack_params(flat_params, model_width, FF)
    block_in = tokens.astype(jnp.float32)
    normed, inv_std = layer_stats(block_in)
    gain_attn = params["gain_attn"].astype(jnp.float32)
    gain_mlp = params["gain_mlp"].astype(jnp.float32)
    attn_in = (normed * gain_attn + params["shift_attn"].astype(jnp.float32)).astype(jnp.bfloat16)
    mlp_in = (normed * gain_mlp + params["shift_mlp"].astype(jnp.float32)).astype(jnp.bfloat16)
    qkv_pre = (
        jnp.dot(attn_in, params["weight_qkv"], preferred_element_type=jnp.float32)
        + params["bias_qkv"].astype(jnp.float32)
    ).reshape(local_rows, 3, head_count, HEAD)
    cosine, sine_rows = rotary_tables(positions)
    queries = rotate(qkv_pre[:, 0], cosine, sine_rows).astype(jnp.bfloat16)
    keys_own = rotate(qkv_pre[:, 1], cosine, sine_rows).astype(jnp.bfloat16)
    values_own = qkv_pre[:, 2].astype(jnp.bfloat16)
    key_vals = jnp.stack(
        [keys_own.reshape(local_rows, model_width), values_own.reshape(local_rows, model_width)], 1
    )
    query_slot = lax.axis_index("group") * local_rows + jnp.arange(local_rows, dtype=jnp.int32)

    def split_keys(piece_kv):
        count_keys = piece_kv.shape[0]
        return (
            piece_kv[:, 0].reshape(count_keys, head_count, HEAD),
            piece_kv[:, 1].reshape(count_keys, head_count, HEAD),
        )

    run_max = jnp.full((head_count, local_rows), MASKED, jnp.float32)
    piece_kv = lax.all_gather(key_vals, "group", axis=0, tiled=True)
    piece_seg = lax.all_gather(segment_ids, "group", axis=0, tiled=True)
    piece_keys, piece_values = split_keys(piece_kv)
    key_slot = jnp.arange(piece_seg.shape[0], dtype=jnp.int32)
    scores, allowed = masked_scores(
        queries, piece_keys, segment_ids, piece_seg, query_slot, key_slot
    )
    new_max = jnp.maximum(run_max, jnp.max(scores, -1))
    weights = jnp.where(allowed[None], jnp.exp(scores - new_max[..., None]), 0.0)
    run_sum = jnp.sum(weights, -1)
    run_acc = jnp.einsum(
        "hqk,khd->hqd",
        weights.astype(jnp.bfloat16),
        piece_values,
        preferred_element_type=jnp.float32,
    )
    run_max, run_sum, run_acc = (new_max, run_sum, run_acc)
    log_total = run_max + jnp.log(run_sum)
    context = jnp.transpose(run_acc / run_sum[..., None], (1, 0, 2)).astype(jnp.bfloat16)
    context_flat = context.reshape(local_rows, model_width)
    attn_out = jnp.dot(
        context_flat, params["weight_out"], preferred_element_type=jnp.float32
    ) + params["bias_out"].astype(jnp.float32)
    up_pre = jnp.dot(mlp_in, params["weight_up"], preferred_element_type=jnp.float32) + params[
        "bias_up"
    ].astype(jnp.float32)
    up_act = jax.nn.gelu(up_pre, approximate=False).astype(jnp.bfloat16)
    mlp_out = jnp.dot(up_act, params["weight_down"], preferred_element_type=jnp.float32) + params[
        "bias_down"
    ].astype(jnp.float32)
    block_out = (block_in + attn_out + mlp_out).astype(jnp.bfloat16)
    valid_rows = (jnp.arange(local_rows) < counts[0]).astype(jnp.float32)
    grad_rows = grad_out.astype(jnp.float32) * valid_rows[:, None]
    grad_low = grad_rows.astype(jnp.bfloat16)
    bias_grad = jnp.sum(grad_rows, 0)
    grad_dict = {}
    grad_dict["weight_down"] = jnp.dot(up_act.T, grad_low, preferred_element_type=jnp.float32)
    grad_dict["bias_down"] = bias_grad
    grad_dict["weight_out"] = jnp.dot(context_flat.T, grad_low, preferred_element_type=jnp.float32)
    grad_dict["bias_out"] = bias_grad
    grad_act = jnp.dot(grad_low, params["weight_down"].T, preferred_element_type=jnp.float32)
    grad_pre = (grad_act * gelu_slope(up_pre)).astype(jnp.bfloat16)
    grad_dict["weight_up"] = jnp.dot(mlp_in.T, grad_pre, preferred_element_type=jnp.float32)
    grad_dict["bias_up"] = jnp.sum(grad_pre.astype(jnp.float32), 0)
    grad_mlp_in = jnp.dot(grad_pre, params["weight_up"].T, preferred_element_type=jnp.float32)
    grad_context = jnp.dot(
        grad_low, params["weight_out"].T, preferred_element_type=jnp.float32
    ).astype(jnp.bfloat16)
    grad_context = grad_context.reshape(local_rows, head_count, HEAD)
    row_delta = jnp.einsum(
        "qhd,qhd->hq", grad_context.astype(jnp.float32), context.astype(jnp.float32)
    )
    piece_kv = lax.all_gather(key_vals, "group", axis=0, tiled=True)
    piece_seg = lax.all_gather(segment_ids, "group", axis=0, tiled=True)
    piece_keys, piece_values = split_keys(piece_kv)
    count_keys = piece_seg.shape[0]
    key_slot = jnp.arange(count_keys, dtype=jnp.int32)
    scores, allowed = masked_scores(
        queries, piece_keys, segment_ids, piece_seg, query_slot, key_slot
    )
    probs_low, grad_scores = score_grads(
        scores, allowed, log_total, row_delta, grad_context, piece_values
    )
    grad_queries = jnp.einsum(
        "hqk,khd->qhd", grad_scores, piece_keys, preferred_element_type=jnp.float32
    )
    part_keys = jnp.einsum("hqk,qhd->khd", grad_scores, queries, preferred_element_type=jnp.float32)
    part_values = jnp.einsum(
        "hqk,qhd->khd", probs_low, grad_context, preferred_element_type=jnp.float32
    )
    addition = jnp.stack(
        [part_keys.reshape(count_keys, model_width), part_values.reshape(count_keys, model_width)],
        1,
    )
    grad_kv = addition
    grad_queries, batch_kv = (grad_queries, grad_kv)
    grad_kv = lax.psum_scatter(
        batch_kv.astype(jnp.bfloat16), "group", scatter_dimension=0, tiled=True
    ).astype(jnp.float32)
    grad_keys = grad_kv[:, 0].reshape(local_rows, head_count, HEAD)
    grad_values = grad_kv[:, 1].reshape(local_rows, head_count, HEAD)
    grad_qkv = (
        jnp.stack(
            [
                rotate_back(grad_queries, cosine, sine_rows),
                rotate_back(grad_keys, cosine, sine_rows),
                grad_values,
            ],
            1,
        )
        .reshape(local_rows, 3 * model_width)
        .astype(jnp.bfloat16)
    )
    grad_dict["weight_qkv"] = jnp.dot(attn_in.T, grad_qkv, preferred_element_type=jnp.float32)
    grad_dict["bias_qkv"] = jnp.sum(grad_qkv.astype(jnp.float32), 0)
    grad_attn_in = jnp.dot(grad_qkv, params["weight_qkv"].T, preferred_element_type=jnp.float32)
    grad_dict["gain_attn"] = jnp.sum(grad_attn_in * normed, 0)
    grad_dict["shift_attn"] = jnp.sum(grad_attn_in, 0)
    grad_dict["gain_mlp"] = jnp.sum(grad_mlp_in * normed, 0)
    grad_dict["shift_mlp"] = jnp.sum(grad_mlp_in, 0)
    grad_normed = grad_attn_in * gain_attn + grad_mlp_in * gain_mlp
    grad_in = (grad_rows + norm_backward(grad_normed, normed, inv_std)).astype(jnp.bfloat16)
    dp_count = lax.axis_size("dp")
    group_count = lax.axis_size("group")
    partial_value = pack_grads(grad_dict, model_width, FF, master.shape[0] * dp_count * group_count)
    sectioned_grad = lax.psum_scatter(
        partial_value.reshape(dp_count, group_count, -1).astype(jnp.bfloat16),
        "group",
        scatter_dimension=1,
        tiled=True,
    )
    grad_shard = (
        lax.psum_scatter(sectioned_grad, "dp", scatter_dimension=0, tiled=True)
        .astype(jnp.float32)
        .reshape(-1)
    )
    square_sum = lax.psum(jnp.sum(grad_shard * grad_shard), ("dp", "group"))
    grad_scale = 1.0 / (jnp.sqrt(square_sum) + 1e-06)
    scaled = grad_shard * grad_scale
    new_one = BETA_ONE * moment_one + (1.0 - BETA_ONE) * scaled
    new_two = BETA_TWO * moment_two + (1.0 - BETA_TWO) * scaled * scaled
    correct_one = 1.0 - BETA_ONE**STEP
    correct_two = 1.0 - BETA_TWO**STEP
    new_master = master - LEARN_RATE * (
        new_one / correct_one / (jnp.sqrt(new_two / correct_two) + ADAM_EPS) + DECAY_RATE * master
    )
    return (block_out, grad_in, grad_shard, new_master, new_one, new_two)


def padded(count, step):
    return -(-count // step) * step


@functools.lru_cache(None)
def row_plan(width, hidden, dp_count, group_count, shard_len):
    half = width // 2
    row = width * group_count
    devices = dp_count * group_count
    if hidden != row or (width // HEAD) % group_count or shard_len % half or width % 128:
        return None
    base = [i * shard_len // row for i in range(devices)]
    shift = [i * shard_len % row // half for i in range(devices)]
    span = max(-(-(s * half + shard_len) // row) for s in shift)
    stride = shard_len // row
    starts, at = {}, 0
    for entry_name, entry_shape in param_layout(width, hidden):
        starts[entry_name] = at // width
        at += int(np.prod(entry_shape))
    piece_base = [d * group_count * shard_len // row for d in range(dp_count)]
    spans = all(
        base[i] == piece_base[i // group_count] + stride * (i % group_count) for i in range(devices)
    )
    aligned = (
        starts["weight_up"] % group_count == 0
        and starts["weight_down"] % group_count == 0
        and starts["bias_qkv"] % group_count == 0
        and (starts["weight_out"] + 1) % group_count == 0
        and span == stride + 1
        and spans
        and base == [stride * i + i // (2 * group_count) for i in range(devices)]
        and shift == [i % (2 * group_count) for i in range(devices)]
    )
    if not aligned:
        return None
    row_out = starts["bias_qkv"] // group_count
    return dict(
        base=base,
        shift=shift,
        span=span,
        stride=stride,
        starts=starts,
        piece_base=piece_base,
        row_out=row_out,
        row_up=starts["weight_up"] // group_count,
        row_down=starts["weight_down"] // group_count,
        out_chunk=max(i for i in range(devices) if base[i] <= row_out),
        send_rows=padded(span + 7, TILE_ROWS),
        over=[i for i in range(devices - 1) if base[i + 1] == base[i] + stride],
        period=2 * group_count,
    )


def chunk_place(plan, me):
    period = plan["period"]
    return plan["stride"] * me + me // period, lax.rem(me, period)


def flip(value, bit):
    return value + bit - 2 * bit * ((value // bit) % 2)


def remote(src, dst, send_sem, recv_sem, device):
    return pltpu.make_async_remote_copy(
        src_ref=src,
        dst_ref=dst,
        send_sem=send_sem,
        recv_sem=recv_sem,
        device_id=device,
        device_id_type=MESH,
    )


def greet(devices):
    barrier = pltpu.get_barrier_semaphore()
    for device in devices:
        pl.semaphore_signal(barrier, inc=1, device_id=device, device_id_type=MESH)
    pl.semaphore_wait(barrier, len(devices))


def places(group_count):
    d, z = lax.axis_index("dp"), lax.axis_index("group")
    to = [lax.rem(z + k, group_count) for k in range(group_count)]
    frm = [lax.rem(z - k + group_count, group_count) for k in range(group_count)]
    return d, z, to, frm


def gather_kernel(
    plan, group_count, flat, turn_in, tok, grd, ids, whole, toks, grds, idss, outs,
    pad, send, stage, near, obuf, loc, p1s, p1r, cs, cr, xs, xr, ys, yr, ts, tr, os, orr,
):
    d, z, to, frm = places(group_count)
    n = group_count
    dc, dx, dy = flip(d, 1), flip(d, 2), flip(d, 4)
    dxy = flip(dx, 4)
    greet([(d, to[k]) for k in range(1, n)] + [(dc, z), (dx, z), (dy, z)])
    span, stride = plan["span"], plan["stride"]
    send_rows, width = send.shape[1:]
    unit = width // n
    tiles = width // 128
    group = tiles * n
    length = flat.shape[0]
    me = d * n + z
    base, shift = chunk_place(plan, me)
    pad[0:group] = jnp.zeros((group, 128), jnp.float32)
    pad[group : group + length] = flat[...]
    rest = pad.shape[0] - group - length
    pad[group + length :] = jnp.zeros((rest, 128), jnp.float32)
    row = base + lax.broadcasted_iota(jnp.int32, (send_rows, 1), 0)
    whole_lines = ((row >= plan["row_out"]) & (row < plan["row_up"])) | (row >= plan["row_down"])
    up_rows = (row >= plan["row_up"]) & (row < plan["row_down"])
    first_row = group - tiles // 2 * shift
    for b in range(n):
        stage[b] = jnp.concatenate(
            [
                pad[pl.ds(first_row + tiles * b + t, send_rows, stride=group), :]
                for t in range(tiles)
            ],
            1,
        )
    for b in range(n):
        line = stage[b]
        turned = jnp.dot(
            line.astype(jnp.bfloat16), turn_in[...], preferred_element_type=jnp.float32
        )
        near[b] = jnp.where(up_rows, turned, line)
    extra = jnp.concatenate(
        [stage[j % n, stride - 1 + j // n : stride + j // n, :] for j in range(send_rows - span)], 0
    )
    for g in range(n):
        by_column = jnp.concatenate([near[b][:, g * unit : (g + 1) * unit] for b in range(n)], 1)
        value = jnp.where(whole_lines, stage[g], by_column)
        value = jnp.concatenate([value[:stride], jnp.concatenate([value[stride:span], extra], 0)], 0)
        send[g] = value.astype(jnp.bfloat16)
    first, later = [], []
    for k in range(1, n):
        copy = remote(send.at[to[k]], whole.at[d, z], p1s.at[k], p1r.at[k], (d, to[k]))
        copy.start()
        first.append(copy)
    own = pltpu.make_async_copy(send.at[z], whole.at[d, z], loc.at[0])
    own.start()
    stays = []
    for m, (src, dst) in enumerate(((ids, idss), (tok, toks), (grd, grds))):
        stay = pltpu.make_async_copy(src, dst.at[z], loc.at[1 + m])
        stay.start()
        stays.append(stay)
        for k in range(1, n):
            copy = remote(src, dst.at[z], ts.at[m, k], tr.at[m, k], (d, to[k]))
            copy.start()
            later.append((copy, remote(src, dst.at[frm[k]], ts.at[m, k], tr.at[m, k], (d, to[k]))))
    sent = []

    def push(ref, s, r, device):
        copy = remote(ref, ref, s, r, device)
        copy.start()
        sent.append(copy)

    def arrived(ref, s, r, device):
        remote(ref, ref, s, r, device).wait_recv()

    for k in range(n):
        ref = whole.at[d, frm[k]]
        if k == 0:
            own.wait()
        else:
            arrived(ref, p1s.at[k], p1r.at[k], (d, to[k]))
        push(ref, xs.at[k], xr.at[k], (dx, z))
        push(ref, ys.at[k], yr.at[k], (dy, z))
        push(ref, cs.at[k], cr.at[k], (dc, z))
    for k in range(n):
        by_x, by_y = whole.at[dx, frm[k]], whole.at[dy, frm[k]]
        arrived(by_x, xs.at[k], xr.at[k], (dx, z))
        if k < n // 2:
            push(by_x, ys.at[n + k], yr.at[n + k], (dy, z))
        push(by_x, cs.at[n + k], cr.at[n + k], (dc, z))
        arrived(by_y, ys.at[k], yr.at[k], (dy, z))
        if k >= n // 2:
            push(by_y, xs.at[n + k], xr.at[n + k], (dx, z))
        push(by_y, cs.at[2 * n + k], cr.at[2 * n + k], (dc, z))
    for k in range(n):
        across = whole.at[dxy, frm[k]]
        if k < n // 2:
            arrived(across, ys.at[n + k], yr.at[n + k], (dy, z))
        else:
            arrived(across, xs.at[n + k], xr.at[n + k], (dx, z))
        push(across, cs.at[3 * n + k], cr.at[3 * n + k], (dc, z))
    for j, owner in enumerate((d, dx, dy, dxy)):
        for k in range(n):
            ref = whole.at[flip(owner, 1), frm[k]]
            arrived(ref, cs.at[j * n + k], cr.at[j * n + k], (dc, z))
    for copy in first + sent:
        copy.wait_send()
    pulls = []
    for j in range(4):
        i = plan["out_chunk"] + j
        pull = pltpu.make_async_copy(whole.at[i // n, i % n], send.at[j], loc.at[4 + j])
        pull.start()
        pulls.append(pull)
    for pull in pulls:
        pull.wait()
    block = unit // n
    lines = []
    for j in range(1, 4):
        count = min(stride, unit - stride * (j - 1))
        part = send[j].astype(jnp.float32)[:count]
        if j > 1:
            head = send[j - 1].astype(jnp.float32)[stride : stride + 8]
            row8 = lax.broadcasted_iota(jnp.int32, (8, 1), 0)
            part = jnp.concatenate([part[:8] + jnp.where(row8 == 0, head, 0.0), part[8:]], 0)
        lines.append(part)
    lines = jnp.concatenate(lines, 0)
    before = send[0].astype(jnp.float32)[stride : stride + 1]
    moved = pltpu.roll(lines, 1, 0)
    at = lax.broadcasted_iota(jnp.int32, (unit, 1), 0)
    moved = jnp.where(at == 0, before, moved)
    lines = jnp.where(z == n - 1, moved, lines).astype(jnp.bfloat16)
    for g in range(n):
        obuf[g] = lines[g * block : (g + 1) * block]
    mine = pltpu.make_async_copy(obuf.at[z], outs.at[z], loc.at[0])
    mine.start()
    trades = []
    for k in range(1, n):
        copy = remote(obuf.at[to[k]], outs.at[z], os.at[k], orr.at[k], (d, to[k]))
        copy.start()
        trades.append(
            (copy, remote(obuf.at[to[k]], outs.at[frm[k]], os.at[k], orr.at[k], (d, to[k])))
        )
    mine.wait()
    for stay in stays:
        stay.wait()
    for copy, other in later + trades:
        other.wait_recv()
        copy.wait_send()


def gather_call(plan, dp_count, group_count, flat, turn_in, tok, grd, ids):
    n = group_count
    width = tok.shape[1]
    bf16, f32 = jnp.bfloat16, jnp.float32
    send_rows = plan["send_rows"]
    group = width // 128 * n
    pad_rows = padded(2 * group + group * send_rows, 8)
    block = width // n // n

    def gathered(value):
        return jax.ShapeDtypeStruct((n,) + value.shape, value.dtype)

    return pl.pallas_call(
        functools.partial(gather_kernel, plan, n),
        out_shape=[
            jax.ShapeDtypeStruct((dp_count, n, send_rows, width), bf16),
            gathered(tok),
            gathered(grd),
            gathered(ids),
            jax.ShapeDtypeStruct((n, block, width), bf16),
        ],
        in_specs=[INVMEM, INVMEM, ANY, ANY, ANY],
        out_specs=[ANY] * 5,
        scratch_shapes=[
            pltpu.VMEM((pad_rows, 128), f32),
            pltpu.VMEM((n, send_rows, width), bf16),
            pltpu.VMEM((n, send_rows, width), f32),
            pltpu.VMEM((n, send_rows, width), f32),
            pltpu.VMEM((n, block, width), bf16),
            DMA((8,)), DMA((n,)), DMA((n,)), DMA((4 * n,)), DMA((4 * n,)),
            DMA((2 * n,)), DMA((2 * n,)), DMA((2 * n,)), DMA((2 * n,)), DMA((3, n)), DMA((3, n)),
            DMA((n,)), DMA((n,)),
        ],
        compiler_params=pltpu.CompilerParams(
            collective_id=1, has_side_effects=True, vmem_limit_bytes=32 * 2**20
        ),
        name="gather_parts",
    )(flat, turn_in, tok, grd, ids)


def compute_kernel(
    plan, n, whole, toks, grds, idss, outs, unperm, pieces, parts, gout,
    w32, gm32, w_up, w_down, w_qkv, w_out, normed, attn_in, mlp_in, slope, act, g_pre, acc, g_mlp,
    tabs, qm, km, vm, gm, k_all, v_all, ctx, gq, gk, gv, g_qkv, rel_a, rel_b,
):
    f32, bf16 = jnp.float32, jnp.bfloat16
    z = lax.axis_index("group")
    rows, width = normed.shape
    unit = width // n
    local = rows // n
    block = unit // n
    wide = 256
    heads = unit // HEAD
    base, span, stride = plan["base"], plan["span"], plan["stride"]
    row_out, row_up, row_down, over = plan["row_out"], plan["row_up"], plan["row_down"], plan["over"]

    def mm(lhs, rhs):
        return jnp.dot(lhs, rhs, preferred_element_type=f32)

    def mm_t(lhs, rhs):
        return lax.dot_general(lhs, rhs, (((1,), (1,)), ((), ())), preferred_element_type=f32)

    def t_mm(lhs, rhs):
        return lax.dot_general(lhs, rhs, (((0,), (0,)), ((), ())), preferred_element_type=f32)

    def chunk(i):
        return whole[i].astype(f32)

    def fill(low, high):
        for i, first in enumerate(base):
            last = first + (stride if i in over else span)
            lo, hi = max(low, first), min(high, last)
            if lo >= hi:
                continue
            w32[lo - low : hi - low] = chunk(i)[lo - first : hi - first]
            if lo == first and i - 1 in over:
                tail = whole[i - 1, stride : stride + 8].astype(f32)[:1]
                w32[lo - low : lo - low + 1] = w32[lo - low : lo - low + 1] + tail

    def line(row):
        i = max(i for i in range(len(base)) if base[i] <= row)
        return chunk(i)[row - base[i] : row - base[i] + 1]

    fill(row_up, row_up + width)
    w_up[...] = w32[:width].astype(bf16)
    fill(row_down, row_down + width)
    w_down[...] = w32[:width].astype(bf16)
    fill(0, row_out)
    third = width // n
    gap = jnp.zeros((third, wide - unit), f32)
    tiles = width // 128
    for t in range(tiles):
        rel_a[t, :row_out] = w32[:row_out, t * 128 : (t + 1) * 128]

    def strided_rows(ref, start, step):
        return jnp.concatenate(
            [ref[t, pl.ds(start, third, stride=step), :] for t in range(tiles)], 1
        )

    def put_rows(ref, start, step, value):
        for t in range(tiles):
            ref[t, pl.ds(start, third, stride=step), :] = value[:, t * 128 : (t + 1) * 128]

    planes = [strided_rows(rel_a, p, 3) for p in range(3)]
    for t in range(n):
        blocks = []
        for j in range(3):
            p, b = (3 * t + j) // n, (3 * t + j) % n
            blocks += [planes[p][:, b * unit : (b + 1) * unit], gap]
        put_rows(rel_b, t, n, jnp.concatenate(blocks, 1))
    for t in range(tiles):
        w_qkv[:, t * 128 : (t + 1) * 128] = rel_b[t].astype(bf16)
    order = [(t - 1) % n for t in range(n)]
    out_rows = jnp.concatenate([outs[j] for j in order], 0)
    w_out[...] = mm(unperm[...], out_rows).astype(bf16)
    bias_up = line(row_up + width)
    vectors = chunk(len(base) - 1)[span : span + n + 1]
    bias_down, gain_attn, shift_attn, gain_mlp, shift_mlp = (vectors[j : j + 1] for j in range(5))
    is_last = z == n - 1
    bias_rest = jnp.where(is_last, bias_down + line(row_up - 1), 0.0)
    bias_lines = chunk(plan["out_chunk"])[span + n : span + n + 3]
    bias_qkv = []
    for j in range(3):
        mine = jnp.zeros((1, unit), f32)
        for g in range(n):
            mine = jnp.where(z == g, bias_lines[j : j + 1, g * unit : (g + 1) * unit], mine)
        bias_qkv += [mine, jnp.zeros((1, wide - unit), f32)]
    bias_qkv = jnp.concatenate(bias_qkv, 1)

    step = 64

    @pl.loop(0, rows // step)
    def _(i):
        at = pl.ds(i * step, step)
        x = toks[at, :].astype(f32)
        centred = x - jnp.mean(x, -1, keepdims=True)
        inv = lax.rsqrt(jnp.mean(centred * centred, -1, keepdims=True) + NORM_EPS)
        value = centred * inv
        normed[at, :] = value
        attn_in[at, :] = (value * gain_attn + shift_attn).astype(bf16)
        mlp_in[at, :] = (value * gain_mlp + shift_mlp).astype(bf16)

    w32[0:8] = jnp.broadcast_to(bias_up, (8, width))
    w32[8:16] = jnp.broadcast_to(bias_qkv, (8, width))

    @pl.loop(0, width // wide)
    def _(i):
        at = pl.ds(pl.multiple_of(i * wide, wide), wide)
        up = mm(mlp_in[...], w_up[:, at]) + w32[0:1, at]
        half = 0.5 * (1.0 + lax.erf(up * 0.7071067811865476))
        act[:, at] = (up * half).astype(bf16)
        slope[:, at] = half + up * jnp.exp(-0.5 * up * up) * 0.3989422804014327

    @pl.loop(0, width // wide)
    def _(i):
        at = pl.ds(pl.multiple_of(i * wide, wide), wide)
        acc[:, at] = mm(act[...], w_down[:, at])
        g_pre[:, at] = (mm_t(grds[...], w_down[at, :]) * slope[:, at]).astype(bf16)

    @pl.loop(0, width // wide)
    def _(i):
        at = pl.ds(pl.multiple_of(i * wide, wide), wide)
        g_mlp[:, at] = mm_t(g_pre[...], w_up[at, :])

    for i in range(width // wide):
        at = slice(i * wide, (i + 1) * wide)
        gm32[row_up + i * wide : row_up + (i + 1) * wide] = t_mm(mlp_in[:, at], g_pre[...])
        gm32[row_down + i * wide : row_down + (i + 1) * wide] = t_mm(act[:, at], grds[...])
    gm32[row_up + width : row_up + width + 1] = jnp.sum(g_pre[...].astype(f32), 0, keepdims=True)
    bias_grad = jnp.where(is_last, jnp.sum(grds[...].astype(f32), 0, keepdims=True), 0.0)

    position = jnp.concatenate([idss[g, 1:2, :] for g in range(n)], 1).astype(f32)
    half_rot = ROT // 2
    at_freq = lax.broadcasted_iota(jnp.int32, (half_rot, 1), 0)
    freq = jnp.zeros((half_rot, 1), f32)
    for i in range(half_rot):
        freq = jnp.where(at_freq == i, float(10000.0 ** (-2.0 * i / ROT)), freq)
    angles = freq * position
    lane = lax.broadcasted_iota(jnp.int32, (half_rot, wide), 1) % HEAD
    same = lane % half_rot == lax.broadcasted_iota(jnp.int32, (half_rot, wide), 0)
    hot = [same & (lane < ROT), same & (lane < half_rot), same & (lane >= half_rot) & (lane < ROT)]

    def expand(table, where):
        return lax.dot_general(
            table,
            where.astype(f32),
            (((0,), (0,)), ((), ())),
            precision=lax.Precision.HIGHEST,
            preferred_element_type=f32,
        )

    cosine, sine = jnp.cos(angles), jnp.sin(angles)
    lane_wide = lax.broadcasted_iota(jnp.int32, (1, wide), 1)
    head_lane = lane_wide % HEAD
    tabs[0] = expand(cosine, hot[0]) + jnp.where(head_lane >= ROT, 1.0, 0.0)
    tabs[1] = expand(sine, hot[1])
    tabs[2] = expand(sine, hot[2])

    def turn(value, at, sign):
        ahead = pltpu.roll(value, wide - half_rot, 1)
        behind = pltpu.roll(value, half_rot, 1)
        return value * tabs[0, at] + sign * (behind * tabs[2, at] - ahead * tabs[1, at])

    def masked(ref, value):
        for h in range(heads):
            ref[h] = jnp.where(lane_wide // HEAD == h, value, 0.0).astype(bf16)

    every = slice(0, rows)
    q32 = turn(mm(attn_in[...], w_qkv[:, :wide]) + w32[8:9, :wide], every, 1.0)
    masked(qm, q32)
    k32 = turn(mm(attn_in[...], w_qkv[:, wide : 2 * wide]) + w32[8:9, wide : 2 * wide], every, 1.0)
    masked(km, k32)
    k_all[...] = k32.astype(bf16)
    v32 = mm(attn_in[...], w_qkv[:, 2 * wide :]) + w32[8:9, 2 * wide :]
    masked(vm, v32)
    v_all[...] = v32.astype(bf16)
    masked(gm, mm_t(grds[...], w_out[...]).astype(bf16).astype(f32))

    seg_row = jnp.concatenate([idss[g, 0:1, :] for g in range(n)], 1).astype(f32)
    seg_col = jnp.transpose(jnp.broadcast_to(seg_row, (128, rows)))[:, 0:1]
    ctx[...] = jnp.zeros_like(ctx)
    gq[...] = jnp.zeros_like(gq)
    gk[...] = jnp.zeros_like(gk)
    gv[...] = jnp.zeros_like(gv)
    for b in range(n):
        at = slice(b * local, (b + 1) * local)
        upto = (b + 1) * local
        seen = slice(0, upto)
        earlier = lax.broadcasted_iota(jnp.int32, (local, upto), 1) <= b * local + (
            lax.broadcasted_iota(jnp.int32, (local, upto), 0)
        )
        allowed = (seg_col[at] == seg_row[:, seen]) & earlier

        @pl.loop(0, heads)
        def _(h):
            scores = jnp.where(allowed, mm_t(qm[h, at], k_all[seen]) * SCORE_SCALE, MASKED)
            top = jnp.max(scores, -1, keepdims=True)
            weights = jnp.exp(scores - top)
            probs = weights / jnp.sum(weights, -1, keepdims=True)
            low = probs.astype(bf16)
            context = mm(low, vm[h, seen])
            ctx[at] += context
            kept = context.astype(bf16).astype(f32)
            delta = jnp.sum(gm[h, at].astype(f32) * kept, -1, keepdims=True)
            slanted = (probs * (mm_t(gm[h, at], v_all[seen]) - delta) * SCORE_SCALE).astype(bf16)
            gq[at] += mm(slanted, km[h, seen])
            gk[seen] += t_mm(slanted, qm[h, at])
            gv[seen] += t_mm(low, gm[h, at])

    g_qkv[:, :wide] = turn(gq[...], every, -1.0).astype(bf16)
    g_qkv[:, wide : 2 * wide] = turn(gk[...], every, -1.0).astype(bf16)
    g_qkv[:, 2 * wide :] = gv[...].astype(bf16)
    ctx_low = ctx[...].astype(bf16)
    out_grad = t_mm(ctx_low, grds[...]).astype(bf16)
    out_grad = t_mm(unperm[...], out_grad).astype(bf16)
    for g in range(n):
        t = (g + 1) % n
        gout[g] = out_grad[t * block : (t + 1) * block]
    for i in range(width // wide):
        at = slice(i * wide, (i + 1) * wide)
        value = acc[:, at] + mm(ctx_low, w_out[:, at]) + bias_rest[:, at]
        for g in range(n):
            parts[g, :, at] = value[g * local : (g + 1) * local].astype(bf16)
    vecs = [[], [], [], []]
    for i in range(width // wide):
        at = slice(i * wide, (i + 1) * wide)
        g_attn = mm_t(g_qkv[...], w_qkv[at, :])
        g_up = g_mlp[:, at]
        value = (g_attn * gain_attn[:, at] + g_up * gain_mlp[:, at]).astype(bf16)
        for g in range(n):
            parts[g, :, width + i * wide : width + (i + 1) * wide] = value[g * local : (g + 1) * local]
        here = normed[:, at]
        for j, term in enumerate((g_attn * here, g_attn, g_up * here, g_up)):
            vecs[j].append(jnp.sum(term, 0, keepdims=True))
        value = t_mm(attn_in[:, at], g_qkv[...])
        for t in range(tiles):
            rel_b[t, at] = value[:, t * 128 : (t + 1) * 128]
    columns = [strided_rows(rel_b, t, n) for t in range(n)]
    for p in range(3):
        blocks = []
        for b in range(n):
            t, j = (n * p + b) // 3, (n * p + b) % 3
            blocks.append(columns[t][:, j * wide : j * wide + unit])
        put_rows(rel_a, p, 3, jnp.concatenate(blocks, 1))
    for t in range(tiles):
        gm32[:row_out, t * 128 : (t + 1) * 128] = rel_a[t, :row_out]
    gm32[row_out:row_up] = jnp.zeros((row_up - row_out, width), f32)
    gm32[row_up - 1 : row_up] = bias_grad
    row_end = row_down + width
    gm32[row_end:] = jnp.zeros((gm32.shape[0] - row_end, width), f32)
    sums = jnp.sum(g_qkv[...].astype(f32), 0, keepdims=True)
    sums = jnp.concatenate(
        [sums[:, j * wide : j * wide + unit] for j in range(3)] + [jnp.zeros((1, unit), f32)], 1
    )
    extra = [bias_grad] + [jnp.concatenate(v, 1) for v in vecs] + [sums, jnp.zeros((2, width), f32)]
    body = n * stride
    for d, first in enumerate(plan["piece_base"]):
        pieces[d, :body] = gm32[first : first + body].astype(bf16)
        last = [gm32[first + body : first + body + 1], jnp.zeros((7, width), f32)] + extra
        pieces[d, body:] = jnp.concatenate(last, 0).astype(bf16)


def compute_call(plan, dp_count, n, whole, toks, grds, idss, outs, unperm):
    rows, width = toks.shape
    f32, bf16 = jnp.float32, jnp.bfloat16
    wide, heads = 256, width // n // HEAD
    row_end = plan["row_down"] + width

    def fl(*shape):
        return pltpu.VMEM(shape, f32)

    def bf(*shape):
        return pltpu.VMEM(shape, bf16)

    return pl.pallas_call(
        functools.partial(compute_kernel, plan, n),
        out_shape=[
            jax.ShapeDtypeStruct((dp_count, n * plan["stride"] + TILE_ROWS, width), bf16),
            jax.ShapeDtypeStruct((n, rows // n, 2 * width), bf16),
            jax.ShapeDtypeStruct(outs.shape, bf16),
        ],
        in_specs=[INVMEM] * 6,
        out_specs=[INVMEM] * 3,
        scratch_shapes=[
            fl(width + 8, width), fl(padded(row_end + 8, 8), width),
            bf(width, width), bf(width, width), bf(width, 3 * wide), bf(wide, width),
            fl(rows, width), bf(rows, width), bf(rows, width), fl(rows, width), bf(rows, width),
            bf(rows, width), fl(rows, width), fl(rows, width),
            fl(3, rows, wide), bf(heads, rows, wide), bf(heads, rows, wide), bf(heads, rows, wide),
            bf(heads, rows, wide), bf(rows, wide), bf(rows, wide), fl(rows, wide),
            fl(rows, wide), fl(rows, wide), fl(rows, wide), bf(rows, 3 * wide),
            fl(width // 128, width, 128), fl(width // 128, width, 128),
        ],
        compiler_params=pltpu.CompilerParams(vmem_limit_bytes=56 * 2**20),
        name="compute_parts",
    )(whole, toks, grds, idss, outs, unperm)


def finish_kernel(
    plan, dp_count, group_count, cut, pieces, parts, gout, turn_in, grad, swapped, square_sum,
    held, from_core, from_first, from_last, total, gbuf, slabs, back, stage, pad, sq, sqz, sqd,
    loc, cs, cr, xs, xr, ys, yr, zs, zr, gs, gr, bs, br, qs, qr, ds, dr,
):
    f32, bf16 = jnp.float32, jnp.bfloat16
    d, z, to, frm = places(group_count)
    n, m = group_count, dp_count
    y, x, c = d // 4, lax.rem(d // 2, 2), lax.rem(d, 2)
    dc, dx, dy = flip(d, 1), flip(d, 2), flip(d, 4)
    turn_to = [lax.rem(d + k, m) for k in range(m)]
    turn_from = [lax.rem(d - k + m, m) for k in range(m)]
    greet([(d, to[k]) for k in range(1, n)] + [(turn_to[k], z) for k in range(1, m)])
    rows, width = total.shape
    unit = width // n
    block = unit // n
    span, stride = plan["span"], plan["stride"]
    body = n * stride
    loads = []
    for i in range(m):
        load = pltpu.make_async_copy(pieces.at[i], held.at[i], loc.at[i])
        load.start()
        loads.append(load)
    keep = pltpu.make_async_copy(gout.at[z], gbuf.at[z], loc.at[m])
    keep.start()
    trades = []
    for k in range(1, n):
        copy = remote(gout.at[to[k]], gbuf.at[z], gs.at[k], gr.at[k], (d, to[k]))
        copy.start()
        trades.append((copy, remote(gout.at[to[k]], gbuf.at[frm[k]], gs.at[k], gr.at[k], (d, to[k]))))
    stay = pltpu.make_async_copy(parts.at[z], swapped.at[z], loc.at[m + 1])
    stay.start()
    swaps = []
    for k in range(1, n):
        copy = remote(parts.at[to[k]], swapped.at[z], zs.at[k], zr.at[k], (d, to[k]))
        copy.start()
        swaps.append(
            (copy, remote(parts.at[to[k]], swapped.at[frm[k]], zs.at[k], zr.at[k], (d, to[k])))
        )
    for load in loads:
        load.wait()
    keep.wait()
    for copy, other in trades:
        other.wait_recv()
    out_rows = jnp.concatenate([gbuf[g].astype(f32) for g in range(n)], 0)
    at = lax.broadcasted_iota(jnp.int32, (unit, 1), 0)
    moved = jnp.where(at == unit - 1, 0.0, pltpu.roll(out_rows, unit - 1, 0))
    is_last = z == n - 1
    after = plan["out_chunk"] // n + 1
    held[after, :unit] = (
        held[after, :unit].astype(f32) + jnp.where(is_last, moved, out_rows)
    ).astype(bf16)
    at = lax.broadcasted_iota(jnp.int32, (TILE_ROWS, 1), 0)
    first_line = jnp.where((at == 0) & is_last, out_rows[:1], 0.0)
    held[after - 1, body:] = (held[after - 1, body:].astype(f32) + first_line).astype(bf16)

    low, high = pl.ds(0, cut), pl.ds(cut, rows - cut)
    here = 2 * y + x
    quads = [flip(flip(here, 1), 2), flip(here, 1), flip(here, 2), here]
    mine = [held.at[2 * q + c] for q in quads]
    cross = []
    for k in range(4):
        copy = remote(
            held.at[2 * quads[k] + 1 - c], from_core.at[k], cs.at[k], cr.at[k], (dc, z)
        )
        copy.start()
        cross.append(copy)

    def add(dst, src):
        dst[...] = (dst[...].astype(f32) + src[...].astype(f32)).astype(dst.dtype)

    sent = []

    def push(src, dst, s, r, device):
        copy = remote(src, dst, s, r, device)
        copy.start()
        sent.append(copy)
        return copy

    by_x, by_y = (dx, z), (dy, z)
    for k in range(4):
        cross[k].wait_recv()
        add(mine[k], from_core.at[k])
        if k == 0:
            x0 = push(mine[0].at[low], from_first.at[0, low], xs.at[0], xr.at[0], by_x)
            y0 = push(mine[0].at[high], from_first.at[0, high], ys.at[0], yr.at[0], by_y)
        elif k == 1:
            x1 = push(mine[1].at[low], from_first.at[1, low], xs.at[1], xr.at[1], by_x)
        elif k == 2:
            y1 = push(mine[2].at[high], from_first.at[1, high], ys.at[1], yr.at[1], by_y)
    x0.wait_recv()
    add(mine[2].at[low], from_first.at[0, low])
    y2 = push(mine[2].at[low], from_last.at[low], ys.at[2], yr.at[2], by_y)
    y0.wait_recv()
    add(mine[1].at[high], from_first.at[0, high])
    x2 = push(mine[1].at[high], from_last.at[high], xs.at[2], xr.at[2], by_x)
    x1.wait_recv()
    add(mine[3].at[low], from_first.at[1, low])
    y1.wait_recv()
    add(mine[3].at[high], from_first.at[1, high])
    y2.wait_recv()
    x2.wait_recv()
    total[...] = (mine[3][...].astype(f32) + from_last[...].astype(f32)).astype(bf16).astype(f32)

    odd = lax.rem(d, 2)
    at = lax.broadcasted_iota(jnp.int32, (rows, 1), 0)
    counted = jnp.where((at >= odd) & (at < body + 1), total[...], 0.0)
    sq[z] = jnp.full(sq.shape[1:], jnp.sum(counted * counted), f32)
    for k in range(1, n):
        copy = remote(sq.at[z], sq.at[z], qs.at[k], qr.at[k], (d, to[k]))
        copy.start()
        sent.append(copy)
    extra = total[body + 8 : body + 14]
    for j in range(n):
        slab = jnp.concatenate(
            [
                total[stride * j : stride * j + stride],
                jnp.concatenate(
                    [total[stride * j + stride : stride * j + span], extra, jnp.zeros((1, width), f32)], 0
                ),
            ],
            0,
        )
        slabs[j] = slab.astype(bf16)
    far = []
    for k in range(1, n):
        copy = remote(slabs.at[to[k]], back.at[z], bs.at[k], br.at[k], (d, to[k]))
        copy.start()
        far.append((copy, remote(slabs.at[to[k]], back.at[frm[k]], bs.at[k], br.at[k], (d, to[k]))))
    back[z] = slabs[z]
    for k in range(1, n):
        remote(sq.at[z], sq.at[frm[k]], qs.at[k], qr.at[k], (d, to[k])).wait_recv()
    sqz[...] = sq[0] + sq[1] + sq[2] + sq[3]
    sqd[d] = sqz[...]
    for k in range(1, m):
        copy = remote(sqz, sqd.at[d], ds.at[k], dr.at[k], (turn_to[k], z))
        copy.start()
        sent.append(copy)
    for copy, other in far:
        other.wait_recv()

    me = d * n + z
    base, shift = chunk_place(plan, me)
    send_rows = back.shape[1]
    row = base + lax.broadcasted_iota(jnp.int32, (send_rows, 1), 0)
    whole_lines = ((row >= plan["row_out"]) & (row < plan["row_up"])) | (row >= plan["row_down"])
    up_rows = (row >= plan["row_up"]) & (row < plan["row_down"])
    for g in range(n):
        stage[g] = back[g].astype(f32)
    vec = stage[0, stride : stride + 8]
    for g in range(1, n):
        vec = vec + stage[g, stride : stride + 8]
    vec = vec[1:6]
    bias_rows = [stage[g, span + 5 : span + 6] for g in range(n)]
    squares = jnp.sum(vec * vec)
    for g in range(n):
        squares = squares + jnp.sum(bias_rows[g] * bias_rows[g])
    tiles = width // 128
    group = tiles * n
    first_row = group - tiles // 2 * shift
    row_end = plan["row_down"] + width
    for b in range(n):
        part = slice(b * unit, (b + 1) * unit)
        by_column = jnp.concatenate([stage[g, :, part] for g in range(n)], 1)
        unturned = lax.dot_general(
            by_column.astype(bf16), turn_in[...], (((1,), (1,)), ((), ())), preferred_element_type=f32
        )
        value = jnp.where(up_rows, unturned, by_column)
        value = jnp.where(whole_lines, stage[b], value)
        if b < 3:
            bias_line = jnp.concatenate([bias_rows[g][:, part] for g in range(n)], 1)
            value = jnp.where(row == plan["row_out"], bias_line, value)
        value = jnp.where(row == row_end, vec[b : b + 1], value)
        if b == 0:
            value = jnp.where(row == row_end + 1, vec[n : n + 1], value)
        for t in range(tiles):
            pad[pl.ds(first_row + tiles * b + t, send_rows, stride=group), :] = value[
                :, t * 128 : (t + 1) * 128
            ]
    grad[...] = pad[group : group + grad.shape[0]]
    for k in range(1, m):
        remote(sqz, sqd.at[turn_from[k]], ds.at[k], dr.at[k], (turn_to[k], z)).wait_recv()
    result = sqd[0]
    for k in range(1, m):
        result = result + sqd[k]
    square_sum[...] = result + squares
    for copy in cross + sent:
        copy.wait_send()
    stay.wait()
    for copy, other in swaps:
        other.wait_recv()
        copy.wait_send()
    for copy, other in trades + far:
        copy.wait_send()


def finish_call(plan, dp_count, group_count, pieces, parts, gout, turn_in, length):
    rows, width = pieces.shape[1:]
    n, m = group_count, dp_count
    f32, bf16 = jnp.float32, jnp.bfloat16
    send_rows = plan["send_rows"]
    group = width // 128 * n
    pad_rows = padded(2 * group + group * send_rows, 8)
    return pl.pallas_call(
        functools.partial(finish_kernel, plan, m, n, padded(rows // 2, TILE_ROWS)),
        out_shape=[
            jax.ShapeDtypeStruct((length // 128, 128), f32),
            jax.ShapeDtypeStruct(parts.shape, bf16),
            jax.ShapeDtypeStruct((8, 128), f32),
        ],
        in_specs=[ANY, ANY, ANY, INVMEM],
        out_specs=[INVMEM, ANY, INVMEM],
        scratch_shapes=[
            pltpu.VMEM((m, rows, width), bf16),
            pltpu.VMEM((4, rows, width), bf16),
            pltpu.VMEM((2, rows, width), bf16),
            pltpu.VMEM((rows, width), bf16),
            pltpu.VMEM((rows, width), f32),
            pltpu.VMEM(gout.shape, bf16),
            pltpu.VMEM((n, send_rows, width), bf16),
            pltpu.VMEM((n, send_rows, width), bf16),
            pltpu.VMEM((n, send_rows, width), f32),
            pltpu.VMEM((pad_rows, 128), f32),
            pltpu.VMEM((n, 8, 128), f32),
            pltpu.VMEM((8, 128), f32),
            pltpu.VMEM((m, 8, 128), f32),
            DMA((m + 2,)), DMA((4,)), DMA((4,)), DMA((3,)), DMA((3,)), DMA((3,)), DMA((3,)),
            DMA((n,)), DMA((n,)), DMA((n,)), DMA((n,)), DMA((n,)), DMA((n,)),
            DMA((n,)), DMA((n,)), DMA((m,)), DMA((m,)),
        ],
        compiler_params=pltpu.CompilerParams(
            collective_id=2, has_side_effects=True, vmem_limit_bytes=40 * 2**20
        ),
        name="finish_parts",
    )(pieces, parts, gout, turn_in)


def one_hot(size, natural):
    return (np.arange(size)[:, None] == np.asarray(natural)[None, :]).astype(np.float32)


def strided(size, step):
    each = size // step
    column = np.arange(size)
    return one_hot(size, (column % each) * step + column // each)


def on_device_split(tokens, grad_out, segment_ids, positions, counts, master, moment_one, moment_two):
    f32, bf16 = jnp.float32, jnp.bfloat16
    dp_count, group_count = lax.axis_size("dp"), lax.axis_size("group")
    local_rows, width = tokens.shape
    n = group_count
    rows = local_rows * n
    plan = row_plan(width, FF, dp_count, n, master.shape[0])
    turn_in = jnp.asarray(strided(width, n), bf16)
    unit = width // n
    unperm = jnp.asarray(np.pad(strided(unit, n), ((0, 256 - unit), (0, 0))), bf16)

    flat = master.reshape(-1, 128)
    valid_rows = jnp.arange(local_rows) < counts[0]
    grad_own = jnp.where(valid_rows[:, None], grad_out, jnp.zeros_like(grad_out))
    ids = jnp.pad(jnp.stack([segment_ids, positions]), ((0, 6), (0, 0)))
    whole, toks, grds, idss, outs = gather_call(plan, dp_count, n, flat, turn_in, tokens, grad_own, ids)
    whole = whole.reshape((dp_count * n,) + whole.shape[2:])
    toks, grds = toks.reshape(rows, width), grds.reshape(rows, width)
    pieces, parts, gout = compute_call(plan, dp_count, n, whole, toks, grds, idss, outs, unperm)
    grad_rows, swapped, squares = finish_call(
        plan, dp_count, n, pieces, parts, gout, turn_in, master.shape[0]
    )
    grad_shard = grad_rows.reshape(-1)

    own = jnp.sum(swapped.astype(f32), 0)
    tokens_own = tokens.astype(f32)
    block_out = (tokens_own + own[:, :width]).astype(bf16)
    own_normed, own_inv = layer_stats(tokens_own)
    grad_in = (grad_own.astype(f32) + norm_backward(own[:, width:], own_normed, own_inv)).astype(bf16)
    return (block_out, grad_in) + update(grad_shard, squares[0, 0], master, moment_one, moment_two)


def update(grad_shard, square_sum, master, moment_one, moment_two):
    grad_scale = 1.0 / (jnp.sqrt(square_sum) + 1e-06)
    scaled = grad_shard * grad_scale
    new_one = BETA_ONE * moment_one + (1.0 - BETA_ONE) * scaled
    new_two = BETA_TWO * moment_two + (1.0 - BETA_TWO) * scaled * scaled
    correct_one = 1.0 - BETA_ONE**STEP
    correct_two = 1.0 - BETA_TWO**STEP
    new_master = master - LEARN_RATE * (
        new_one / correct_one / (jnp.sqrt(new_two / correct_two) + ADAM_EPS) + DECAY_RATE * master
    )
    return (grad_shard, new_master, new_one, new_two)


def on_device(tokens, grad_out, segment_ids, positions, counts, master, moment_one, moment_two):
    dp_count, group_count = lax.axis_size("dp"), lax.axis_size("group")
    width = tokens.shape[1]
    splits = (
        (dp_count, group_count) == (8, 4)
        and tokens.shape[0] == 128
        and width // group_count <= 256
        and row_plan(width, FF, dp_count, group_count, master.shape[0]) is not None
    )
    body = on_device_split if splits else on_device_gathered
    return body(tokens, grad_out, segment_ids, positions, counts, master, moment_one, moment_two)


def solution(mesh):
    placed = (
        P(("dp", "group"), None),
        P(("dp", "group"), None),
        P(("dp", "group")),
        P(("dp", "group")),
        P(("dp", "group")),
        P(("dp", "group")),
        P(("dp", "group")),
        P(("dp", "group")),
    )
    return jax.shard_map(
        on_device,
        mesh=mesh,
        in_specs=placed,
        out_specs=(
            P(("dp", "group"), None),
            P(("dp", "group"), None),
            P(("dp", "group")),
            P(("dp", "group")),
            P(("dp", "group")),
            P(("dp", "group")),
        ),
        check_vma=False,
    )
```

```python
import functools

import jax
import jax.numpy as jnp
import numpy as np
from jax import lax
from jax.experimental import pallas as pl
from jax.experimental.pallas import tpu as pltpu
from jax.sharding import PartitionSpec as P

FF = 3072
HEAD = 64
ROT = 16
STEP = 3


BETA_ONE = 0.9
BETA_TWO = 0.95
LEARN_RATE = 0.01
DECAY_RATE = 0.1
ADAM_EPS = 1e-08
NORM_EPS = 1e-05
SCORE_SCALE = 0.125
MASKED = -1e30
TILE_ROWS = 16
MESH = pl.DeviceIdType.MESH
DMA = pltpu.SemaphoreType.DMA
ANY = pl.BlockSpec(memory_space=pl.ANY)
INVMEM = pl.BlockSpec(memory_space=pltpu.VMEM)


def param_layout(model_width, hidden):
    return [
        ("weight_qkv", (model_width, 3 * model_width)),
        ("bias_qkv", (3 * model_width,)),
        ("weight_out", (model_width, model_width)),
        ("bias_out", (model_width,)),
        ("weight_up", (model_width, hidden)),
        ("bias_up", (hidden,)),
        ("weight_down", (hidden, model_width)),
        ("bias_down", (model_width,)),
        ("gain_attn", (model_width,)),
        ("shift_attn", (model_width,)),
        ("gain_mlp", (model_width,)),
        ("shift_mlp", (model_width,)),
    ]


def unpack_params(flat_params, model_width, hidden):
    result = {}
    offset = 0
    for entry_name, entry_shape in param_layout(model_width, hidden):
        length = 1
        for extent in entry_shape:
            length = length * extent
        result[entry_name] = flat_params[offset : offset + length].reshape(entry_shape)
        offset = offset + length
    return result


def pack_grads(grad_dict, model_width, hidden, total_len):
    pieces = []
    used_count = 0
    for entry_name, entry_shape in param_layout(model_width, hidden):
        flat_grad = grad_dict[entry_name].reshape(-1)
        pieces.append(flat_grad)
        used_count = used_count + flat_grad.shape[0]
    pieces.append(jnp.zeros((total_len - used_count,), jnp.float32))
    return jnp.concatenate(pieces)


def rotary_tables(pos_ids):
    half_rot = ROT // 2
    inverse_freq = 10000.0 ** (-jnp.arange(half_rot, dtype=jnp.float32) * 2.0 / ROT)
    angles = pos_ids.astype(jnp.float32)[:, None] * inverse_freq[None, :]
    return (jnp.cos(angles), jnp.sin(angles))


def rotate(values, cosine, sine_rows):
    half_rot = ROT // 2
    lower_part = values[..., :half_rot]
    upper_part = values[..., half_rot:ROT]
    cos_rows = cosine[:, None, :]
    sin_rows = sine_rows[:, None, :]
    return jnp.concatenate(
        [
            lower_part * cos_rows - upper_part * sin_rows,
            upper_part * cos_rows + lower_part * sin_rows,
            values[..., ROT:],
        ],
        -1,
    )


def rotate_back(values, cosine, sine_rows):
    half_rot = ROT // 2
    lower_part = values[..., :half_rot]
    upper_part = values[..., half_rot:ROT]
    cos_rows = cosine[:, None, :]
    sin_rows = sine_rows[:, None, :]
    return jnp.concatenate(
        [
            lower_part * cos_rows + upper_part * sin_rows,
            upper_part * cos_rows - lower_part * sin_rows,
            values[..., ROT:],
        ],
        -1,
    )


def layer_stats(block_in):
    centred = block_in - jnp.mean(block_in, -1, keepdims=True)
    inv_std = lax.rsqrt(jnp.mean(centred * centred, -1, keepdims=True) + NORM_EPS)
    return (centred * inv_std, inv_std)


def norm_backward(grad_normed, normed, inv_std):
    return inv_std * (
        grad_normed
        - jnp.mean(grad_normed, -1, keepdims=True)
        - normed * jnp.mean(grad_normed * normed, -1, keepdims=True)
    )


def gelu_slope(up_pre):
    return (
        0.5 * (1.0 + lax.erf(up_pre * 0.7071067811865476))
        + up_pre * jnp.exp(-0.5 * up_pre * up_pre) * 0.3989422804014327
    )


def masked_scores(query_part, key_part, query_seg, key_seg, query_slot, key_slot):
    scores = (
        jnp.einsum("qhd,khd->hqk", query_part, key_part, preferred_element_type=jnp.float32)
        * SCORE_SCALE
    )
    allowed = (query_seg[:, None] == key_seg[None, :]) & (key_slot[None, :] <= query_slot[:, None])
    return (jnp.where(allowed[None], scores, MASKED), allowed)


def score_grads(scores, allowed, log_total, row_delta, grad_context, value_part):
    attn_probs = jnp.where(allowed[None], jnp.exp(scores - log_total[..., None]), 0.0)
    grad_probs = jnp.einsum(
        "qhd,khd->hqk", grad_context, value_part, preferred_element_type=jnp.float32
    )
    grad_scores = (attn_probs * (grad_probs - row_delta[..., None]) * SCORE_SCALE).astype(
        jnp.bfloat16
    )
    return (attn_probs.astype(jnp.bfloat16), grad_scores)


def on_device_gathered(tokens, grad_out, segment_ids, positions, counts, master, moment_one, moment_two):
    local_rows = tokens.shape[0]
    model_width = tokens.shape[1]
    head_count = model_width // HEAD
    local_master = master.astype(jnp.bfloat16)
    sectioned = lax.all_gather(local_master.reshape(1, 1, -1), "group", axis=1, tiled=True)
    sectioned = lax.all_gather(sectioned, "dp", axis=0, tiled=True)
    flat_params = sectioned.reshape(-1)
    params = unpack_params(flat_params, model_width, FF)
    block_in = tokens.astype(jnp.float32)
    normed, inv_std = layer_stats(block_in)
    gain_attn = params["gain_attn"].astype(jnp.float32)
    gain_mlp = params["gain_mlp"].astype(jnp.float32)
    attn_in = (normed * gain_attn + params["shift_attn"].astype(jnp.float32)).astype(jnp.bfloat16)
    mlp_in = (normed * gain_mlp + params["shift_mlp"].astype(jnp.float32)).astype(jnp.bfloat16)
    qkv_pre = (
        jnp.dot(attn_in, params["weight_qkv"], preferred_element_type=jnp.float32)
        + params["bias_qkv"].astype(jnp.float32)
    ).reshape(local_rows, 3, head_count, HEAD)
    cosine, sine_rows = rotary_tables(positions)
    queries = rotate(qkv_pre[:, 0], cosine, sine_rows).astype(jnp.bfloat16)
    keys_own = rotate(qkv_pre[:, 1], cosine, sine_rows).astype(jnp.bfloat16)
    values_own = qkv_pre[:, 2].astype(jnp.bfloat16)
    key_vals = jnp.stack(
        [keys_own.reshape(local_rows, model_width), values_own.reshape(local_rows, model_width)], 1
    )
    query_slot = lax.axis_index("group") * local_rows + jnp.arange(local_rows, dtype=jnp.int32)

    def split_keys(piece_kv):
        count_keys = piece_kv.shape[0]
        return (
            piece_kv[:, 0].reshape(count_keys, head_count, HEAD),
            piece_kv[:, 1].reshape(count_keys, head_count, HEAD),
        )

    run_max = jnp.full((head_count, local_rows), MASKED, jnp.float32)
    piece_kv = lax.all_gather(key_vals, "group", axis=0, tiled=True)
    piece_seg = lax.all_gather(segment_ids, "group", axis=0, tiled=True)
    piece_keys, piece_values = split_keys(piece_kv)
    key_slot = jnp.arange(piece_seg.shape[0], dtype=jnp.int32)
    scores, allowed = masked_scores(
        queries, piece_keys, segment_ids, piece_seg, query_slot, key_slot
    )
    new_max = jnp.maximum(run_max, jnp.max(scores, -1))
    weights = jnp.where(allowed[None], jnp.exp(scores - new_max[..., None]), 0.0)
    run_sum = jnp.sum(weights, -1)
    run_acc = jnp.einsum(
        "hqk,khd->hqd",
        weights.astype(jnp.bfloat16),
        piece_values,
        preferred_element_type=jnp.float32,
    )
    run_max, run_sum, run_acc = (new_max, run_sum, run_acc)
    log_total = run_max + jnp.log(run_sum)
    context = jnp.transpose(run_acc / run_sum[..., None], (1, 0, 2)).astype(jnp.bfloat16)
    context_flat = context.reshape(local_rows, model_width)
    attn_out = jnp.dot(
        context_flat, params["weight_out"], preferred_element_type=jnp.float32
    ) + params["bias_out"].astype(jnp.float32)
    up_pre = jnp.dot(mlp_in, params["weight_up"], preferred_element_type=jnp.float32) + params[
        "bias_up"
    ].astype(jnp.float32)
    up_act = jax.nn.gelu(up_pre, approximate=False).astype(jnp.bfloat16)
    mlp_out = jnp.dot(up_act, params["weight_down"], preferred_element_type=jnp.float32) + params[
        "bias_down"
    ].astype(jnp.float32)
    block_out = (block_in + attn_out + mlp_out).astype(jnp.bfloat16)
    valid_rows = (jnp.arange(local_rows) < counts[0]).astype(jnp.float32)
    grad_rows = grad_out.astype(jnp.float32) * valid_rows[:, None]
    grad_low = grad_rows.astype(jnp.bfloat16)
    bias_grad = jnp.sum(grad_rows, 0)
    grad_dict = {}
    grad_dict["weight_down"] = jnp.dot(up_act.T, grad_low, preferred_element_type=jnp.float32)
    grad_dict["bias_down"] = bias_grad
    grad_dict["weight_out"] = jnp.dot(context_flat.T, grad_low, preferred_element_type=jnp.float32)
    grad_dict["bias_out"] = bias_grad
    grad_act = jnp.dot(grad_low, params["weight_down"].T, preferred_element_type=jnp.float32)
    grad_pre = (grad_act * gelu_slope(up_pre)).astype(jnp.bfloat16)
    grad_dict["weight_up"] = jnp.dot(mlp_in.T, grad_pre, preferred_element_type=jnp.float32)
    grad_dict["bias_up"] = jnp.sum(grad_pre.astype(jnp.float32), 0)
    grad_mlp_in = jnp.dot(grad_pre, params["weight_up"].T, preferred_element_type=jnp.float32)
    grad_context = jnp.dot(
        grad_low, params["weight_out"].T, preferred_element_type=jnp.float32
    ).astype(jnp.bfloat16)
    grad_context = grad_context.reshape(local_rows, head_count, HEAD)
    row_delta = jnp.einsum(
        "qhd,qhd->hq", grad_context.astype(jnp.float32), context.astype(jnp.float32)
    )
    piece_kv = lax.all_gather(key_vals, "group", axis=0, tiled=True)
    piece_seg = lax.all_gather(segment_ids, "group", axis=0, tiled=True)
    piece_keys, piece_values = split_keys(piece_kv)
    count_keys = piece_seg.shape[0]
    key_slot = jnp.arange(count_keys, dtype=jnp.int32)
    scores, allowed = masked_scores(
        queries, piece_keys, segment_ids, piece_seg, query_slot, key_slot
    )
    probs_low, grad_scores = score_grads(
        scores, allowed, log_total, row_delta, grad_context, piece_values
    )
    grad_queries = jnp.einsum(
        "hqk,khd->qhd", grad_scores, piece_keys, preferred_element_type=jnp.float32
    )
    part_keys = jnp.einsum("hqk,qhd->khd", grad_scores, queries, preferred_element_type=jnp.float32)
    part_values = jnp.einsum(
        "hqk,qhd->khd", probs_low, grad_context, preferred_element_type=jnp.float32
    )
    addition = jnp.stack(
        [part_keys.reshape(count_keys, model_width), part_values.reshape(count_keys, model_width)],
        1,
    )
    grad_kv = addition
    grad_queries, batch_kv = (grad_queries, grad_kv)
    grad_kv = lax.psum_scatter(
        batch_kv.astype(jnp.bfloat16), "group", scatter_dimension=0, tiled=True
    ).astype(jnp.float32)
    grad_keys = grad_kv[:, 0].reshape(local_rows, head_count, HEAD)
    grad_values = grad_kv[:, 1].reshape(local_rows, head_count, HEAD)
    grad_qkv = (
        jnp.stack(
            [
                rotate_back(grad_queries, cosine, sine_rows),
                rotate_back(grad_keys, cosine, sine_rows),
                grad_values,
            ],
            1,
        )
        .reshape(local_rows, 3 * model_width)
        .astype(jnp.bfloat16)
    )
    grad_dict["weight_qkv"] = jnp.dot(attn_in.T, grad_qkv, preferred_element_type=jnp.float32)
    grad_dict["bias_qkv"] = jnp.sum(grad_qkv.astype(jnp.float32), 0)
    grad_attn_in = jnp.dot(grad_qkv, params["weight_qkv"].T, preferred_element_type=jnp.float32)
    grad_dict["gain_attn"] = jnp.sum(grad_attn_in * normed, 0)
    grad_dict["shift_attn"] = jnp.sum(grad_attn_in, 0)
    grad_dict["gain_mlp"] = jnp.sum(grad_mlp_in * normed, 0)
    grad_dict["shift_mlp"] = jnp.sum(grad_mlp_in, 0)
    grad_normed = grad_attn_in * gain_attn + grad_mlp_in * gain_mlp
    grad_in = (grad_rows + norm_backward(grad_normed, normed, inv_std)).astype(jnp.bfloat16)
    dp_count = lax.axis_size("dp")
    group_count = lax.axis_size("group")
    partial_value = pack_grads(grad_dict, model_width, FF, master.shape[0] * dp_count * group_count)
    sectioned_grad = lax.psum_scatter(
        partial_value.reshape(dp_count, group_count, -1).astype(jnp.bfloat16),
        "group",
        scatter_dimension=1,
        tiled=True,
    )
    grad_shard = (
        lax.psum_scatter(sectioned_grad, "dp", scatter_dimension=0, tiled=True)
        .astype(jnp.float32)
        .reshape(-1)
    )
    square_sum = lax.psum(jnp.sum(grad_shard * grad_shard), ("dp", "group"))
    grad_scale = 1.0 / (jnp.sqrt(square_sum) + 1e-06)
    scaled = grad_shard * grad_scale
    new_one = BETA_ONE * moment_one + (1.0 - BETA_ONE) * scaled
    new_two = BETA_TWO * moment_two + (1.0 - BETA_TWO) * scaled * scaled
    correct_one = 1.0 - BETA_ONE**STEP
    correct_two = 1.0 - BETA_TWO**STEP
    new_master = master - LEARN_RATE * (
        new_one / correct_one / (jnp.sqrt(new_two / correct_two) + ADAM_EPS) + DECAY_RATE * master
    )
    return (block_out, grad_in, grad_shard, new_master, new_one, new_two)


def padded(count, step):
    return -(-count // step) * step


@functools.lru_cache(None)
def row_plan(width, hidden, dp_count, group_count, shard_len):
    half = width // 2
    row = width * group_count
    devices = dp_count * group_count
    if hidden != row or (width // HEAD) % group_count or shard_len % half or width % 128:
        return None
    base = [i * shard_len // row for i in range(devices)]
    shift = [i * shard_len % row // half for i in range(devices)]
    span = max(-(-(s * half + shard_len) // row) for s in shift)
    stride = shard_len // row
    starts, at = {}, 0
    for entry_name, entry_shape in param_layout(width, hidden):
        starts[entry_name] = at // width
        at += int(np.prod(entry_shape))
    piece_base = [d * group_count * shard_len // row for d in range(dp_count)]
    spans = all(
        base[i] == piece_base[i // group_count] + stride * (i % group_count) for i in range(devices)
    )
    aligned = (
        starts["weight_up"] % group_count == 0
        and starts["weight_down"] % group_count == 0
        and starts["bias_qkv"] % group_count == 0
        and (starts["weight_out"] + 1) % group_count == 0
        and span == stride + 1
        and spans
        and base == [stride * i + i // (2 * group_count) for i in range(devices)]
        and shift == [i % (2 * group_count) for i in range(devices)]
    )
    if not aligned:
        return None
    row_out = starts["bias_qkv"] // group_count
    return dict(
        base=base,
        shift=shift,
        span=span,
        stride=stride,
        starts=starts,
        piece_base=piece_base,
        row_out=row_out,
        row_up=starts["weight_up"] // group_count,
        row_down=starts["weight_down"] // group_count,
        out_chunk=max(i for i in range(devices) if base[i] <= row_out),
        send_rows=padded(span + 7, TILE_ROWS),
        over=[i for i in range(devices - 1) if base[i + 1] == base[i] + stride],
        period=2 * group_count,
    )


def chunk_place(plan, me):
    period = plan["period"]
    return plan["stride"] * me + me // period, lax.rem(me, period)


def flip(value, bit):
    return value + bit - 2 * bit * ((value // bit) % 2)


def remote(src, dst, send_sem, recv_sem, device):
    return pltpu.make_async_remote_copy(
        src_ref=src,
        dst_ref=dst,
        send_sem=send_sem,
        recv_sem=recv_sem,
        device_id=device,
        device_id_type=MESH,
    )


def greet(devices):
    barrier = pltpu.get_barrier_semaphore()
    for device in devices:
        pl.semaphore_signal(barrier, inc=1, device_id=device, device_id_type=MESH)
    pl.semaphore_wait(barrier, len(devices))


def places(group_count):
    d, z = lax.axis_index("dp"), lax.axis_index("group")
    to = [lax.rem(z + k, group_count) for k in range(group_count)]
    frm = [lax.rem(z - k + group_count, group_count) for k in range(group_count)]
    return d, z, to, frm


def layer_kernel(
    plan, dp_count, group_count, flat, turn_in, unperm, tok, grd, ids, grad, swap_a, swap_b, square_sum,
    pad, send, stage, near, obuf, whole, toks, grds, idss, outs, w32, gm32, w_up, w_down,
    w_qkv, w_out, normed, attn_in, mlp_in, slope, act, g_pre, g_low, acc, g_mlp, tabs, qm, km,
    vm, gm, k_all, v_all, ctx, gq, gk, gv, g_qkv, rel_a, rel_b, parts_a, parts_b, gout, held,
    from_core, from_first, from_last, total, gbuf, slabs, back, sq, sqz, sqd, loc, p1s, p1r,
    cs, cr, xs, xr, ys, yr, ts, tr, os, orr, fcs, fcr, fxs, fxr, fys, fyr, zs, zr, gs, gr, bs,
    br, qs, qr, ds, dr,
):
    d, z, to, frm = places(group_count)
    n = group_count
    dc, dx, dy = flip(d, 1), flip(d, 2), flip(d, 4)
    dxy = flip(dx, 4)
    m = dp_count
    turn_to = [lax.rem(d + k, m) for k in range(m)]
    turn_from = [lax.rem(d - k + m, m) for k in range(m)]
    greet([(d, to[k]) for k in range(1, n)] + [(turn_to[k], z) for k in range(1, m)])
    stays, later = [], []

    def share(j, src, dst):
        stay = pltpu.make_async_copy(src, dst.at[z], loc.at[1 + j])
        stay.start()
        stays.append(stay)
        for k in range(1, n):
            copy = remote(src, dst.at[z], ts.at[j, k], tr.at[j, k], (d, to[k]))
            copy.start()
            later.append((copy, remote(src, dst.at[frm[k]], ts.at[j, k], tr.at[j, k], (d, to[k]))))

    def settle():
        for stay in stays:
            stay.wait()
        for copy, other in later:
            other.wait_recv()
            copy.wait_send()
        stays.clear()
        later.clear()

    share(0, ids, idss)
    share(1, tok, toks)
    span, stride = plan["span"], plan["stride"]
    send_rows, width = send.shape[1:]
    unit = width // n
    tiles = width // 128
    group = tiles * n
    length = flat.shape[0]
    me = d * n + z
    base, shift = chunk_place(plan, me)
    pad[0:group] = jnp.zeros((group, 128), jnp.float32)
    pad[group : group + length] = flat[...]
    rest = pad.shape[0] - group - length
    pad[group + length :] = jnp.zeros((rest, 128), jnp.float32)
    row = base + lax.broadcasted_iota(jnp.int32, (send_rows, 1), 0)
    whole_lines = ((row >= plan["row_out"]) & (row < plan["row_up"])) | (row >= plan["row_down"])
    up_rows = (row >= plan["row_up"]) & (row < plan["row_down"])
    first_row = group - tiles // 2 * shift
    for b in range(n):
        stage[b] = jnp.concatenate(
            [
                pad[pl.ds(first_row + tiles * b + t, send_rows, stride=group), :]
                for t in range(tiles)
            ],
            1,
        )
    for b in range(n):
        line = stage[b]
        turned = jnp.dot(
            line.astype(jnp.bfloat16), turn_in[...], preferred_element_type=jnp.float32
        )
        near[b] = jnp.where(up_rows, turned, line)
    extra = jnp.concatenate(
        [stage[j % n, stride - 1 + j // n : stride + j // n, :] for j in range(send_rows - span)], 0
    )
    for g in range(n):
        by_column = jnp.concatenate([near[b][:, g * unit : (g + 1) * unit] for b in range(n)], 1)
        value = jnp.where(whole_lines, stage[g], by_column)
        value = jnp.concatenate([value[:stride], jnp.concatenate([value[stride:span], extra], 0)], 0)
        send[g] = value.astype(jnp.bfloat16)
    first = []
    for k in range(1, n):
        copy = remote(send.at[to[k]], whole.at[d, z], p1s.at[k], p1r.at[k], (d, to[k]))
        copy.start()
        first.append(copy)
    whole[d, z] = send[z]
    sent = []

    def push(ref, s, r, device):
        copy = remote(ref, ref, s, r, device)
        copy.start()
        sent.append(copy)

    def arrived(ref, s, r, device):
        remote(ref, ref, s, r, device).wait_recv()

    for k in range(n):
        ref = whole.at[d, frm[k]]
        if k > 0:
            arrived(ref, p1s.at[k], p1r.at[k], (d, to[k]))
        push(ref, xs.at[k], xr.at[k], (dx, z))
        push(ref, ys.at[k], yr.at[k], (dy, z))
        push(ref, cs.at[k], cr.at[k], (dc, z))
    settle()
    share(2, grd, grds)
    for k in range(n):
        by_x, by_y = whole.at[dx, frm[k]], whole.at[dy, frm[k]]
        arrived(by_x, xs.at[k], xr.at[k], (dx, z))
        if k < n // 2:
            push(by_x, ys.at[n + k], yr.at[n + k], (dy, z))
        push(by_x, cs.at[n + k], cr.at[n + k], (dc, z))
        arrived(by_y, ys.at[k], yr.at[k], (dy, z))
        if k >= n // 2:
            push(by_y, xs.at[n + k], xr.at[n + k], (dx, z))
        push(by_y, cs.at[2 * n + k], cr.at[2 * n + k], (dc, z))
    for k in range(n):
        across = whole.at[dxy, frm[k]]
        if k < n // 2:
            arrived(across, ys.at[n + k], yr.at[n + k], (dy, z))
        else:
            arrived(across, xs.at[n + k], xr.at[n + k], (dx, z))
        push(across, cs.at[3 * n + k], cr.at[3 * n + k], (dc, z))
    for j, owner in enumerate((d, dx, dy, dxy)):
        for k in range(n):
            ref = whole.at[flip(owner, 1), frm[k]]
            arrived(ref, cs.at[j * n + k], cr.at[j * n + k], (dc, z))
    for copy in first + sent:
        copy.wait_send()
    chunks = [plan["out_chunk"] + j for j in range(4)]
    chunks = [whole[i // n, i % n].astype(jnp.float32) for i in chunks]
    block = unit // n
    lines = []
    for j in range(1, 4):
        count = min(stride, unit - stride * (j - 1))
        part = chunks[j][:count]
        if j > 1:
            head = chunks[j - 1][stride : stride + 8]
            row8 = lax.broadcasted_iota(jnp.int32, (8, 1), 0)
            part = jnp.concatenate([part[:8] + jnp.where(row8 == 0, head, 0.0), part[8:]], 0)
        lines.append(part)
    lines = jnp.concatenate(lines, 0)
    before = chunks[0][stride : stride + 1]
    moved = pltpu.roll(lines, 1, 0)
    at = lax.broadcasted_iota(jnp.int32, (unit, 1), 0)
    moved = jnp.where(at == 0, before, moved)
    lines = jnp.where(z == n - 1, moved, lines).astype(jnp.bfloat16)
    for g in range(n):
        obuf[g] = lines[g * block : (g + 1) * block]
    outs[z] = obuf[z]
    outs_moving = []
    for k in range(1, n):
        copy = remote(obuf.at[to[k]], outs.at[z], os.at[k], orr.at[k], (d, to[k]))
        copy.start()
        outs_moving.append(
            (copy, remote(obuf.at[to[k]], outs.at[frm[k]], os.at[k], orr.at[k], (d, to[k])))
        )
    f32, bf16 = jnp.float32, jnp.bfloat16
    rows = normed.shape[0]
    local = rows // n
    wide = 256
    heads = unit // HEAD
    bases = plan["base"]
    row_out, row_up, row_down, over = plan["row_out"], plan["row_up"], plan["row_down"], plan["over"]

    def mm(lhs, rhs):
        return jnp.dot(lhs, rhs, preferred_element_type=f32)

    def mm_t(lhs, rhs):
        return lax.dot_general(lhs, rhs, (((1,), (1,)), ((), ())), preferred_element_type=f32)

    def t_mm(lhs, rhs):
        return lax.dot_general(lhs, rhs, (((0,), (0,)), ((), ())), preferred_element_type=f32)

    def chunk(i):
        return whole[i // n, i % n].astype(f32)

    def fill(low, high):
        for i, first in enumerate(bases):
            last = first + (stride if i in over else span)
            lo, hi = max(low, first), min(high, last)
            if lo >= hi:
                continue
            w32[lo - low : hi - low] = chunk(i)[lo - first : hi - first]
            if lo == first and i - 1 in over:
                tail = whole[(i - 1) // n, (i - 1) % n, stride : stride + 8].astype(f32)[:1]
                w32[lo - low : lo - low + 1] = w32[lo - low : lo - low + 1] + tail

    def line(row):
        i = max(i for i in range(len(bases)) if bases[i] <= row)
        return chunk(i)[row - bases[i] : row - bases[i] + 1]

    fill(row_up, row_up + width)
    w_up[...] = w32[:width].astype(bf16)
    fill(row_down, row_down + width)
    w_down[...] = w32[:width].astype(bf16)
    fill(0, row_out)
    third = width // n
    gap = jnp.zeros((third, wide - unit), f32)
    for t in range(tiles):
        rel_a[t, :row_out] = w32[:row_out, t * 128 : (t + 1) * 128]

    def strided_rows(ref, start, step):
        return jnp.concatenate(
            [ref[t, pl.ds(start, third, stride=step), :] for t in range(tiles)], 1
        )

    def put_rows(ref, start, step, value):
        for t in range(tiles):
            ref[t, pl.ds(start, third, stride=step), :] = value[:, t * 128 : (t + 1) * 128]

    planes = [strided_rows(rel_a, p, 3) for p in range(3)]
    for t in range(n):
        blocks = []
        for j in range(3):
            p, b = (3 * t + j) // n, (3 * t + j) % n
            blocks += [planes[p][:, b * unit : (b + 1) * unit], gap]
        put_rows(rel_b, t, n, jnp.concatenate(blocks, 1))
    for t in range(tiles):
        w_qkv[:, t * 128 : (t + 1) * 128] = rel_b[t].astype(bf16)
    bias_up = line(row_up + width)
    vectors = chunk(len(bases) - 1)[span : span + n + 1]
    bias_down, gain_attn, shift_attn, gain_mlp, shift_mlp = (vectors[j : j + 1] for j in range(5))
    is_last = z == n - 1
    bias_rest = jnp.where(is_last, bias_down + line(row_up - 1), 0.0)
    bias_lines = chunk(plan["out_chunk"])[span + n : span + n + 3]
    bias_qkv = []
    for j in range(3):
        mine = jnp.zeros((1, unit), f32)
        for g in range(n):
            mine = jnp.where(z == g, bias_lines[j : j + 1, g * unit : (g + 1) * unit], mine)
        bias_qkv += [mine, jnp.zeros((1, wide - unit), f32)]
    bias_qkv = jnp.concatenate(bias_qkv, 1)

    step = 64

    @pl.loop(0, rows // step)
    def _(i):
        at = pl.ds(i * step, step)
        x = toks[i // (local // step), pl.ds(i % (local // step) * step, step), :].astype(f32)
        centred = x - jnp.mean(x, -1, keepdims=True)
        inv = lax.rsqrt(jnp.mean(centred * centred, -1, keepdims=True) + NORM_EPS)
        value = centred * inv
        normed[at, :] = value
        attn_in[at, :] = (value * gain_attn + shift_attn).astype(bf16)
        mlp_in[at, :] = (value * gain_mlp + shift_mlp).astype(bf16)

    w32[0:8] = jnp.broadcast_to(bias_up, (8, width))
    w32[8:16] = jnp.broadcast_to(bias_qkv, (8, width))

    @pl.loop(0, width // wide)
    def _(i):
        at = pl.ds(pl.multiple_of(i * wide, wide), wide)
        up = mm(mlp_in[...], w_up[:, at]) + w32[0:1, at]
        half = 0.5 * (1.0 + lax.erf(up * 0.7071067811865476))
        act[:, at] = (up * half).astype(bf16)
        slope[:, at] = half + up * jnp.exp(-0.5 * up * up) * 0.3989422804014327

    @pl.loop(0, width // wide)
    def _(i):
        at = pl.ds(pl.multiple_of(i * wide, wide), wide)
        acc[:, at] = mm(act[...], w_down[:, at])

    position = jnp.concatenate([idss[g, 1:2, :] for g in range(n)], 1).astype(f32)
    half_rot = ROT // 2
    at_freq = lax.broadcasted_iota(jnp.int32, (half_rot, 1), 0)
    freq = jnp.zeros((half_rot, 1), f32)
    for i in range(half_rot):
        freq = jnp.where(at_freq == i, float(10000.0 ** (-2.0 * i / ROT)), freq)
    angles = freq * position
    lane = lax.broadcasted_iota(jnp.int32, (half_rot, wide), 1) % HEAD
    same = lane % half_rot == lax.broadcasted_iota(jnp.int32, (half_rot, wide), 0)
    hot = [same & (lane < ROT), same & (lane < half_rot), same & (lane >= half_rot) & (lane < ROT)]

    def expand(table, where):
        return lax.dot_general(
            table,
            where.astype(f32),
            (((0,), (0,)), ((), ())),
            precision=lax.Precision.HIGHEST,
            preferred_element_type=f32,
        )

    cosine, sine = jnp.cos(angles), jnp.sin(angles)
    lane_wide = lax.broadcasted_iota(jnp.int32, (1, wide), 1)
    head_lane = lane_wide % HEAD
    tabs[0] = expand(cosine, hot[0]) + jnp.where(head_lane >= ROT, 1.0, 0.0)
    tabs[1] = expand(sine, hot[1])
    tabs[2] = expand(sine, hot[2])

    def turn(value, at, sign):
        ahead = pltpu.roll(value, wide - half_rot, 1)
        behind = pltpu.roll(value, half_rot, 1)
        return value * tabs[0, at] + sign * (behind * tabs[2, at] - ahead * tabs[1, at])

    def masked(ref, value):
        for h in range(heads):
            ref[h] = jnp.where(lane_wide // HEAD == h, value, 0.0).astype(bf16)

    every = slice(0, rows)
    q32 = turn(mm(attn_in[...], w_qkv[:, :wide]) + w32[8:9, :wide], every, 1.0)
    masked(qm, q32)
    k32 = turn(mm(attn_in[...], w_qkv[:, wide : 2 * wide]) + w32[8:9, wide : 2 * wide], every, 1.0)
    masked(km, k32)
    k_all[...] = k32.astype(bf16)
    v32 = mm(attn_in[...], w_qkv[:, 2 * wide :]) + w32[8:9, 2 * wide :]
    masked(vm, v32)
    v_all[...] = v32.astype(bf16)
    for copy, other in outs_moving:
        other.wait_recv()
        copy.wait_send()
    order = [(t - 1) % n for t in range(n)]
    out_rows = jnp.concatenate([outs[j] for j in order], 0)
    w_out[...] = mm(unperm[...], out_rows).astype(bf16)
    settle()
    for g in range(n):
        g_low[g * local : (g + 1) * local] = grds[g]
    masked(gm, mm_t(g_low[...], w_out[...]).astype(bf16).astype(f32))

    seg_row = jnp.concatenate([idss[g, 0:1, :] for g in range(n)], 1).astype(f32)
    seg_col = jnp.transpose(jnp.broadcast_to(seg_row, (128, rows)))[:, 0:1]
    ctx[...] = jnp.zeros_like(ctx)
    gq[...] = jnp.zeros_like(gq)
    gk[...] = jnp.zeros_like(gk)
    gv[...] = jnp.zeros_like(gv)
    for b in range(n):
        at = slice(b * local, (b + 1) * local)
        upto = (b + 1) * local
        seen = slice(0, upto)
        earlier = lax.broadcasted_iota(jnp.int32, (local, upto), 1) <= b * local + (
            lax.broadcasted_iota(jnp.int32, (local, upto), 0)
        )
        allowed = (seg_col[at] == seg_row[:, seen]) & earlier

        @pl.loop(0, heads)
        def _(h):
            scores = jnp.where(allowed, mm_t(qm[h, at], k_all[seen]) * SCORE_SCALE, MASKED)
            top = jnp.max(scores, -1, keepdims=True)
            weights = jnp.exp(scores - top)
            probs = weights / jnp.sum(weights, -1, keepdims=True)
            low = probs.astype(bf16)
            context = mm(low, vm[h, seen])
            ctx[at] += context
            kept = context.astype(bf16).astype(f32)
            delta = jnp.sum(gm[h, at].astype(f32) * kept, -1, keepdims=True)
            slanted = (probs * (mm_t(gm[h, at], v_all[seen]) - delta) * SCORE_SCALE).astype(bf16)
            gq[at] += mm(slanted, km[h, seen])
            gk[seen] += t_mm(slanted, qm[h, at])
            gv[seen] += t_mm(low, gm[h, at])

    g_qkv[:, :wide] = turn(gq[...], every, -1.0).astype(bf16)
    g_qkv[:, wide : 2 * wide] = turn(gk[...], every, -1.0).astype(bf16)
    g_qkv[:, 2 * wide :] = gv[...].astype(bf16)
    swaps = []

    def swap(j, src, dst):
        stay = pltpu.make_async_copy(src.at[z], dst.at[z], loc.at[4 + j])
        stay.start()
        swaps.append((stay, None))
        for k in range(1, n):
            copy = remote(src.at[to[k]], dst.at[z], zs.at[j, k], zr.at[j, k], (d, to[k]))
            copy.start()
            swaps.append(
                (copy, remote(src.at[to[k]], dst.at[frm[k]], zs.at[j, k], zr.at[j, k], (d, to[k])))
            )

    ctx_low = ctx[...].astype(bf16)
    out_grad = t_mm(ctx_low, g_low[...]).astype(bf16)
    out_grad = t_mm(unperm[...], out_grad).astype(bf16)
    for g in range(n):
        t = (g + 1) % n
        gout[g] = out_grad[t * block : (t + 1) * block]
    gbuf[z] = gout[z]
    trades = []
    for k in range(1, n):
        copy = remote(gout.at[to[k]], gbuf.at[z], gs.at[k], gr.at[k], (d, to[k]))
        copy.start()
        trades.append((copy, remote(gout.at[to[k]], gbuf.at[frm[k]], gs.at[k], gr.at[k], (d, to[k]))))
    for i in range(width // wide):
        at = slice(i * wide, (i + 1) * wide)
        value = acc[:, at] + mm(ctx_low, w_out[:, at]) + bias_rest[:, at]
        for g in range(n):
            parts_a[g, :, at] = value[g * local : (g + 1) * local].astype(bf16)
    swap(0, parts_a, swap_a)
    @pl.loop(0, width // wide)
    def _(i):
        at = pl.ds(pl.multiple_of(i * wide, wide), wide)
        g_pre[:, at] = (mm_t(g_low[...], w_down[at, :]) * slope[:, at]).astype(bf16)

    @pl.loop(0, width // wide)
    def _(i):
        at = pl.ds(pl.multiple_of(i * wide, wide), wide)
        g_mlp[:, at] = mm_t(g_pre[...], w_up[at, :])

    bias_grad = jnp.where(is_last, jnp.sum(g_low[...].astype(f32), 0, keepdims=True), 0.0)

    vecs = [[], [], [], []]
    for i in range(width // wide):
        at = slice(i * wide, (i + 1) * wide)
        g_attn = mm_t(g_qkv[...], w_qkv[at, :])
        g_up = g_mlp[:, at]
        value = (g_attn * gain_attn[:, at] + g_up * gain_mlp[:, at]).astype(bf16)
        for g in range(n):
            parts_b[g, :, at] = value[g * local : (g + 1) * local]
        here = normed[:, at]
        for j, term in enumerate((g_attn * here, g_attn, g_up * here, g_up)):
            vecs[j].append(jnp.sum(term, 0, keepdims=True))
    swap(1, parts_b, swap_b)
    for i in range(width // wide):
        at = slice(i * wide, (i + 1) * wide)
        gm32[row_up + i * wide : row_up + (i + 1) * wide] = t_mm(mlp_in[:, at], g_pre[...])
        gm32[row_down + i * wide : row_down + (i + 1) * wide] = t_mm(act[:, at], g_low[...])
    gm32[row_up + width : row_up + width + 1] = jnp.sum(g_pre[...].astype(f32), 0, keepdims=True)
    for i in range(width // wide):
        at = slice(i * wide, (i + 1) * wide)
        value = t_mm(attn_in[:, at], g_qkv[...])
        for t in range(tiles):
            rel_b[t, at] = value[:, t * 128 : (t + 1) * 128]
    columns = [strided_rows(rel_b, t, n) for t in range(n)]
    for p in range(3):
        blocks = []
        for b in range(n):
            t, j = (n * p + b) // 3, (n * p + b) % 3
            blocks.append(columns[t][:, j * wide : j * wide + unit])
        put_rows(rel_a, p, 3, jnp.concatenate(blocks, 1))
    for t in range(tiles):
        gm32[:row_out, t * 128 : (t + 1) * 128] = rel_a[t, :row_out]
    gm32[row_out:row_up] = jnp.zeros((row_up - row_out, width), f32)
    gm32[row_up - 1 : row_up] = bias_grad
    row_end = row_down + width
    gm32[row_end:] = jnp.zeros((gm32.shape[0] - row_end, width), f32)
    sums = jnp.sum(g_qkv[...].astype(f32), 0, keepdims=True)
    sums = jnp.concatenate(
        [sums[:, j * wide : j * wide + unit] for j in range(3)] + [jnp.zeros((1, unit), f32)], 1
    )
    extra = [bias_grad] + [jnp.concatenate(v, 1) for v in vecs] + [sums, jnp.zeros((2, width), f32)]
    body = n * stride
    for e, first in enumerate(plan["piece_base"]):
        held[e, :body] = gm32[first : first + body].astype(bf16)
        last = [gm32[first + body : first + body + 1], jnp.zeros((7, width), f32)] + extra
        held[e, body:] = jnp.concatenate(last, 0).astype(bf16)
    y, x, c = d // 4, lax.rem(d // 2, 2), lax.rem(d, 2)
    rows = total.shape[0]
    cut = padded(rows // 2, TILE_ROWS)
    for copy, other in trades:
        other.wait_recv()
    out_rows = jnp.concatenate([gbuf[g].astype(f32) for g in range(n)], 0)
    at = lax.broadcasted_iota(jnp.int32, (unit, 1), 0)
    moved = jnp.where(at == unit - 1, 0.0, pltpu.roll(out_rows, unit - 1, 0))
    is_last = z == n - 1
    after = plan["out_chunk"] // n + 1
    held[after, :unit] = (
        held[after, :unit].astype(f32) + jnp.where(is_last, moved, out_rows)
    ).astype(bf16)
    at = lax.broadcasted_iota(jnp.int32, (TILE_ROWS, 1), 0)
    first_line = jnp.where((at == 0) & is_last, out_rows[:1], 0.0)
    held[after - 1, body:] = (held[after - 1, body:].astype(f32) + first_line).astype(bf16)

    low, high = pl.ds(0, cut), pl.ds(cut, rows - cut)
    here = 2 * y + x
    quads = [flip(flip(here, 1), 2), flip(here, 1), flip(here, 2), here]
    mine = [held.at[2 * q + c] for q in quads]
    cross = []
    for k in range(4):
        copy = remote(
            held.at[2 * quads[k] + 1 - c], from_core.at[k], fcs.at[k], fcr.at[k], (dc, z)
        )
        copy.start()
        cross.append(copy)

    def add(dst, src):
        dst[...] = (dst[...].astype(f32) + src[...].astype(f32)).astype(dst.dtype)

    sent = []

    def pass_on(src, dst, s, r, device):
        copy = remote(src, dst, s, r, device)
        copy.start()
        sent.append(copy)
        return copy

    by_x, by_y = (dx, z), (dy, z)
    for k in range(4):
        cross[k].wait_recv()
        add(mine[k], from_core.at[k])
        if k == 0:
            x0 = pass_on(mine[0].at[low], from_first.at[0, low], fxs.at[0], fxr.at[0], by_x)
            y0 = pass_on(mine[0].at[high], from_first.at[0, high], fys.at[0], fyr.at[0], by_y)
        elif k == 1:
            x1 = pass_on(mine[1].at[low], from_first.at[1, low], fxs.at[1], fxr.at[1], by_x)
        elif k == 2:
            y1 = pass_on(mine[2].at[high], from_first.at[1, high], fys.at[1], fyr.at[1], by_y)
    x0.wait_recv()
    add(mine[2].at[low], from_first.at[0, low])
    y2 = pass_on(mine[2].at[low], from_last.at[low], fys.at[2], fyr.at[2], by_y)
    y0.wait_recv()
    add(mine[1].at[high], from_first.at[0, high])
    x2 = pass_on(mine[1].at[high], from_last.at[high], fxs.at[2], fxr.at[2], by_x)
    x1.wait_recv()
    add(mine[3].at[low], from_first.at[1, low])
    y1.wait_recv()
    add(mine[3].at[high], from_first.at[1, high])
    y2.wait_recv()
    x2.wait_recv()
    total[...] = (mine[3][...].astype(f32) + from_last[...].astype(f32)).astype(bf16).astype(f32)

    odd = lax.rem(d, 2)
    at = lax.broadcasted_iota(jnp.int32, (rows, 1), 0)
    counted = jnp.where((at >= odd) & (at < body + 1), total[...], 0.0)
    sq[z] = jnp.full(sq.shape[1:], jnp.sum(counted * counted), f32)
    for k in range(1, n):
        copy = remote(sq.at[z], sq.at[z], qs.at[k], qr.at[k], (d, to[k]))
        copy.start()
        sent.append(copy)
    extra = total[body + 8 : body + 14]
    for j in range(n):
        slab = jnp.concatenate(
            [
                total[stride * j : stride * j + stride],
                jnp.concatenate(
                    [total[stride * j + stride : stride * j + span], extra, jnp.zeros((1, width), f32)], 0
                ),
            ],
            0,
        )
        slabs[j] = slab.astype(bf16)
    far = []
    for k in range(1, n):
        copy = remote(slabs.at[to[k]], back.at[z], bs.at[k], br.at[k], (d, to[k]))
        copy.start()
        far.append((copy, remote(slabs.at[to[k]], back.at[frm[k]], bs.at[k], br.at[k], (d, to[k]))))
    back[z] = slabs[z]
    for k in range(1, n):
        remote(sq.at[z], sq.at[frm[k]], qs.at[k], qr.at[k], (d, to[k])).wait_recv()
    sqz[...] = sq[0] + sq[1] + sq[2] + sq[3]
    sqd[d] = sqz[...]
    for k in range(1, m):
        copy = remote(sqz, sqd.at[d], ds.at[k], dr.at[k], (turn_to[k], z))
        copy.start()
        sent.append(copy)
    for copy, other in far:
        other.wait_recv()

    for g in range(n):
        stage[g] = back[g].astype(f32)
    vec = stage[0, stride : stride + 8]
    for g in range(1, n):
        vec = vec + stage[g, stride : stride + 8]
    vec = vec[1:6]
    bias_rows = [stage[g, span + 5 : span + 6] for g in range(n)]
    squares = jnp.sum(vec * vec)
    for g in range(n):
        squares = squares + jnp.sum(bias_rows[g] * bias_rows[g])
    row_end = plan["row_down"] + width
    for b in range(n):
        part = slice(b * unit, (b + 1) * unit)
        by_column = jnp.concatenate([stage[g, :, part] for g in range(n)], 1)
        unturned = lax.dot_general(
            by_column.astype(bf16), turn_in[...], (((1,), (1,)), ((), ())), preferred_element_type=f32
        )
        value = jnp.where(up_rows, unturned, by_column)
        value = jnp.where(whole_lines, stage[b], value)
        if b < 3:
            bias_line = jnp.concatenate([bias_rows[g][:, part] for g in range(n)], 1)
            value = jnp.where(row == plan["row_out"], bias_line, value)
        value = jnp.where(row == row_end, vec[b : b + 1], value)
        if b == 0:
            value = jnp.where(row == row_end + 1, vec[n : n + 1], value)
        for t in range(tiles):
            pad[pl.ds(first_row + tiles * b + t, send_rows, stride=group), :] = value[
                :, t * 128 : (t + 1) * 128
            ]
    grad[...] = pad[group : group + grad.shape[0]]
    for k in range(1, m):
        remote(sqz, sqd.at[turn_from[k]], ds.at[k], dr.at[k], (turn_to[k], z)).wait_recv()
    result = sqd[0]
    for k in range(1, m):
        result = result + sqd[k]
    square_sum[...] = result + squares
    for copy in cross + sent:
        copy.wait_send()
    for copy, other in swaps:
        if other is None:
            copy.wait()
        else:
            other.wait_recv()
            copy.wait_send()
    for copy, other in trades + far:
        copy.wait_send()


def layer_call(plan, dp_count, group_count, flat, turn_in, unperm, tok, grd, ids):
    n, m = group_count, dp_count
    local, width = tok.shape
    rows = local * n
    f32, bf16 = jnp.float32, jnp.bfloat16
    wide, heads = 256, width // n // HEAD
    block = width // n // n
    send_rows = plan["send_rows"]
    group = width // 128 * n
    pad_rows = padded(2 * group + group * send_rows, 8)
    row_end = plan["row_down"] + width
    piece = n * plan["stride"] + TILE_ROWS

    def fl(*shape):
        return pltpu.VMEM(shape, f32)

    def bf(*shape):
        return pltpu.VMEM(shape, bf16)

    return pl.pallas_call(
        functools.partial(layer_kernel, plan, m, n),
        out_shape=[
            jax.ShapeDtypeStruct(flat.shape, f32),
            jax.ShapeDtypeStruct((n, local, width), bf16),
            jax.ShapeDtypeStruct((n, local, width), bf16),
            jax.ShapeDtypeStruct((8, 128), f32),
        ],
        in_specs=[INVMEM, INVMEM, INVMEM, ANY, ANY, ANY],
        out_specs=[INVMEM, ANY, ANY, INVMEM],
        scratch_shapes=[
            fl(pad_rows, 128),
            bf(n, send_rows, width),
            fl(n, send_rows, width),
            fl(n, send_rows, width),
            bf(n, block, width),
            bf(m, n, send_rows, width),
            bf(n, local, width),
            bf(n, local, width),
            pltpu.VMEM((n,) + ids.shape, jnp.int32),
            bf(n, block, width),
            fl(width + 8, width),
            fl(padded(row_end + 8, 8), width),
            bf(width, width),
            bf(width, width),
            bf(width, 3 * wide),
            bf(wide, width),
            fl(rows, width),
            bf(rows, width),
            bf(rows, width),
            fl(rows, width),
            bf(rows, width),
            bf(rows, width),
            bf(rows, width),
            fl(rows, width),
            fl(rows, width),
            fl(3, rows, wide),
            bf(heads, rows, wide),
            bf(heads, rows, wide),
            bf(heads, rows, wide),
            bf(heads, rows, wide),
            bf(rows, wide),
            bf(rows, wide),
            fl(rows, wide),
            fl(rows, wide),
            fl(rows, wide),
            fl(rows, wide),
            bf(rows, 3 * wide),
            fl(width // 128, width, 128),
            fl(width // 128, width, 128),
            bf(n, local, width),
            bf(n, local, width),
            bf(n, block, width),
            bf(m, piece, width),
            bf(4, piece, width),
            bf(2, piece, width),
            bf(piece, width),
            fl(piece, width),
            bf(n, block, width),
            bf(n, send_rows, width),
            bf(n, send_rows, width),
            fl(n, 8, 128),
            fl(8, 128),
            fl(m, 8, 128),
            DMA((8,)),
            DMA((n,)),
            DMA((n,)),
            DMA((4 * n,)),
            DMA((4 * n,)),
            DMA((2 * n,)),
            DMA((2 * n,)),
            DMA((2 * n,)),
            DMA((2 * n,)),
            DMA((3, n)),
            DMA((3, n)),
            DMA((n,)),
            DMA((n,)),
            DMA((4,)),
            DMA((4,)),
            DMA((3,)),
            DMA((3,)),
            DMA((3,)),
            DMA((3,)),
            DMA((2, n)),
            DMA((2, n)),
            DMA((n,)),
            DMA((n,)),
            DMA((n,)),
            DMA((n,)),
            DMA((n,)),
            DMA((n,)),
            DMA((m,)),
            DMA((m,)),
        ],
        compiler_params=pltpu.CompilerParams(
            collective_id=1, has_side_effects=True, vmem_limit_bytes=62 * 2**20
        ),
        name="layer_parts",
    )(flat, turn_in, unperm, tok, grd, ids)


def one_hot(size, natural):
    return (np.arange(size)[:, None] == np.asarray(natural)[None, :]).astype(np.float32)


def strided(size, step):
    each = size // step
    column = np.arange(size)
    return one_hot(size, (column % each) * step + column // each)


def on_device_split(tokens, grad_out, segment_ids, positions, counts, master, moment_one, moment_two):
    f32, bf16 = jnp.float32, jnp.bfloat16
    dp_count, group_count = lax.axis_size("dp"), lax.axis_size("group")
    local_rows, width = tokens.shape
    n = group_count
    plan = row_plan(width, FF, dp_count, n, master.shape[0])
    turn_in = jnp.asarray(strided(width, n), bf16)
    unit = width // n
    unperm = jnp.asarray(np.pad(strided(unit, n), ((0, 256 - unit), (0, 0))), bf16)

    flat = master.reshape(-1, 128)
    valid_rows = jnp.arange(local_rows) < counts[0]
    grad_own = jnp.where(valid_rows[:, None], grad_out, jnp.zeros_like(grad_out))
    ids = jnp.pad(jnp.stack([segment_ids, positions]), ((0, 6), (0, 0)))
    grad_rows, swap_a, swap_b, squares = layer_call(
        plan, dp_count, n, flat, turn_in, unperm, tokens, grad_own, ids
    )
    grad_shard = grad_rows.reshape(-1)

    own_out = jnp.sum(swap_a.astype(f32), 0)
    own_grad = jnp.sum(swap_b.astype(f32), 0)
    tokens_own = tokens.astype(f32)
    block_out = (tokens_own + own_out).astype(bf16)
    own_normed, own_inv = layer_stats(tokens_own)
    grad_in = (grad_own.astype(f32) + norm_backward(own_grad, own_normed, own_inv)).astype(bf16)
    return (block_out, grad_in) + update(grad_shard, squares[0, 0], master, moment_one, moment_two)


def update(grad_shard, square_sum, master, moment_one, moment_two):
    grad_scale = 1.0 / (jnp.sqrt(square_sum) + 1e-06)
    scaled = grad_shard * grad_scale
    new_one = BETA_ONE * moment_one + (1.0 - BETA_ONE) * scaled
    new_two = BETA_TWO * moment_two + (1.0 - BETA_TWO) * scaled * scaled
    correct_one = 1.0 - BETA_ONE**STEP
    correct_two = 1.0 - BETA_TWO**STEP
    new_master = master - LEARN_RATE * (
        new_one / correct_one / (jnp.sqrt(new_two / correct_two) + ADAM_EPS) + DECAY_RATE * master
    )
    return (grad_shard, new_master, new_one, new_two)


def on_device(tokens, grad_out, segment_ids, positions, counts, master, moment_one, moment_two):
    dp_count, group_count = lax.axis_size("dp"), lax.axis_size("group")
    width = tokens.shape[1]
    splits = (
        (dp_count, group_count) == (8, 4)
        and tokens.shape[0] == 128
        and width // group_count <= 256
        and row_plan(width, FF, dp_count, group_count, master.shape[0]) is not None
    )
    body = on_device_split if splits else on_device_gathered
    return body(tokens, grad_out, segment_ids, positions, counts, master, moment_one, moment_two)


def solution(mesh):
    placed = (
        P(("dp", "group"), None),
        P(("dp", "group"), None),
        P(("dp", "group")),
        P(("dp", "group")),
        P(("dp", "group")),
        P(("dp", "group")),
        P(("dp", "group")),
        P(("dp", "group")),
    )
    return jax.shard_map(
        on_device,
        mesh=mesh,
        in_specs=placed,
        out_specs=(
            P(("dp", "group"), None),
            P(("dp", "group"), None),
            P(("dp", "group")),
            P(("dp", "group")),
            P(("dp", "group")),
            P(("dp", "group")),
        ),
        check_vma=False,
    )
```

```python
import functools

import jax
import jax.numpy as jnp
import numpy as np
from jax import lax
from jax.experimental import pallas as pl
from jax.experimental.pallas import tpu as pltpu
from jax.sharding import PartitionSpec as P

FF = 3072
HEAD = 64
ROT = 16
STEP = 3


BETA_ONE = 0.9
BETA_TWO = 0.95
LEARN_RATE = 0.01
DECAY_RATE = 0.1
ADAM_EPS = 1e-08
NORM_EPS = 1e-05
SCORE_SCALE = 0.125
MASKED = -1e30
TILE_ROWS = 16
MESH = pl.DeviceIdType.MESH
DMA = pltpu.SemaphoreType.DMA
ANY = pl.BlockSpec(memory_space=pl.ANY)
INVMEM = pl.BlockSpec(memory_space=pltpu.VMEM)


def param_layout(model_width, hidden):
    return [
        ("weight_qkv", (model_width, 3 * model_width)),
        ("bias_qkv", (3 * model_width,)),
        ("weight_out", (model_width, model_width)),
        ("bias_out", (model_width,)),
        ("weight_up", (model_width, hidden)),
        ("bias_up", (hidden,)),
        ("weight_down", (hidden, model_width)),
        ("bias_down", (model_width,)),
        ("gain_attn", (model_width,)),
        ("shift_attn", (model_width,)),
        ("gain_mlp", (model_width,)),
        ("shift_mlp", (model_width,)),
    ]


def unpack_params(flat_params, model_width, hidden):
    result = {}
    offset = 0
    for entry_name, entry_shape in param_layout(model_width, hidden):
        length = 1
        for extent in entry_shape:
            length = length * extent
        result[entry_name] = flat_params[offset : offset + length].reshape(entry_shape)
        offset = offset + length
    return result


def pack_grads(grad_dict, model_width, hidden, total_len):
    pieces = []
    used_count = 0
    for entry_name, entry_shape in param_layout(model_width, hidden):
        flat_grad = grad_dict[entry_name].reshape(-1)
        pieces.append(flat_grad)
        used_count = used_count + flat_grad.shape[0]
    pieces.append(jnp.zeros((total_len - used_count,), jnp.float32))
    return jnp.concatenate(pieces)


def rotary_tables(pos_ids):
    half_rot = ROT // 2
    inverse_freq = 10000.0 ** (-jnp.arange(half_rot, dtype=jnp.float32) * 2.0 / ROT)
    angles = pos_ids.astype(jnp.float32)[:, None] * inverse_freq[None, :]
    return (jnp.cos(angles), jnp.sin(angles))


def rotate(values, cosine, sine_rows):
    half_rot = ROT // 2
    lower_part = values[..., :half_rot]
    upper_part = values[..., half_rot:ROT]
    cos_rows = cosine[:, None, :]
    sin_rows = sine_rows[:, None, :]
    return jnp.concatenate(
        [
            lower_part * cos_rows - upper_part * sin_rows,
            upper_part * cos_rows + lower_part * sin_rows,
            values[..., ROT:],
        ],
        -1,
    )


def rotate_back(values, cosine, sine_rows):
    half_rot = ROT // 2
    lower_part = values[..., :half_rot]
    upper_part = values[..., half_rot:ROT]
    cos_rows = cosine[:, None, :]
    sin_rows = sine_rows[:, None, :]
    return jnp.concatenate(
        [
            lower_part * cos_rows + upper_part * sin_rows,
            upper_part * cos_rows - lower_part * sin_rows,
            values[..., ROT:],
        ],
        -1,
    )


def layer_stats(block_in):
    centred = block_in - jnp.mean(block_in, -1, keepdims=True)
    inv_std = lax.rsqrt(jnp.mean(centred * centred, -1, keepdims=True) + NORM_EPS)
    return (centred * inv_std, inv_std)


def norm_backward(grad_normed, normed, inv_std):
    return inv_std * (
        grad_normed
        - jnp.mean(grad_normed, -1, keepdims=True)
        - normed * jnp.mean(grad_normed * normed, -1, keepdims=True)
    )


def gelu_slope(up_pre):
    return (
        0.5 * (1.0 + lax.erf(up_pre * 0.7071067811865476))
        + up_pre * jnp.exp(-0.5 * up_pre * up_pre) * 0.3989422804014327
    )


def masked_scores(query_part, key_part, query_seg, key_seg, query_slot, key_slot):
    scores = (
        jnp.einsum("qhd,khd->hqk", query_part, key_part, preferred_element_type=jnp.float32)
        * SCORE_SCALE
    )
    allowed = (query_seg[:, None] == key_seg[None, :]) & (key_slot[None, :] <= query_slot[:, None])
    return (jnp.where(allowed[None], scores, MASKED), allowed)


def score_grads(scores, allowed, log_total, row_delta, grad_context, value_part):
    attn_probs = jnp.where(allowed[None], jnp.exp(scores - log_total[..., None]), 0.0)
    grad_probs = jnp.einsum(
        "qhd,khd->hqk", grad_context, value_part, preferred_element_type=jnp.float32
    )
    grad_scores = (attn_probs * (grad_probs - row_delta[..., None]) * SCORE_SCALE).astype(
        jnp.bfloat16
    )
    return (attn_probs.astype(jnp.bfloat16), grad_scores)


def on_device_gathered(tokens, grad_out, segment_ids, positions, counts, master, moment_one, moment_two):
    local_rows = tokens.shape[0]
    model_width = tokens.shape[1]
    head_count = model_width // HEAD
    local_master = master.astype(jnp.bfloat16)
    sectioned = lax.all_gather(local_master.reshape(1, 1, -1), "group", axis=1, tiled=True)
    sectioned = lax.all_gather(sectioned, "dp", axis=0, tiled=True)
    flat_params = sectioned.reshape(-1)
    params = unpack_params(flat_params, model_width, FF)
    block_in = tokens.astype(jnp.float32)
    normed, inv_std = layer_stats(block_in)
    gain_attn = params["gain_attn"].astype(jnp.float32)
    gain_mlp = params["gain_mlp"].astype(jnp.float32)
    attn_in = (normed * gain_attn + params["shift_attn"].astype(jnp.float32)).astype(jnp.bfloat16)
    mlp_in = (normed * gain_mlp + params["shift_mlp"].astype(jnp.float32)).astype(jnp.bfloat16)
    qkv_pre = (
        jnp.dot(attn_in, params["weight_qkv"], preferred_element_type=jnp.float32)
        + params["bias_qkv"].astype(jnp.float32)
    ).reshape(local_rows, 3, head_count, HEAD)
    cosine, sine_rows = rotary_tables(positions)
    queries = rotate(qkv_pre[:, 0], cosine, sine_rows).astype(jnp.bfloat16)
    keys_own = rotate(qkv_pre[:, 1], cosine, sine_rows).astype(jnp.bfloat16)
    values_own = qkv_pre[:, 2].astype(jnp.bfloat16)
    key_vals = jnp.stack(
        [keys_own.reshape(local_rows, model_width), values_own.reshape(local_rows, model_width)], 1
    )
    query_slot = lax.axis_index("group") * local_rows + jnp.arange(local_rows, dtype=jnp.int32)

    def split_keys(piece_kv):
        count_keys = piece_kv.shape[0]
        return (
            piece_kv[:, 0].reshape(count_keys, head_count, HEAD),
            piece_kv[:, 1].reshape(count_keys, head_count, HEAD),
        )

    run_max = jnp.full((head_count, local_rows), MASKED, jnp.float32)
    piece_kv = lax.all_gather(key_vals, "group", axis=0, tiled=True)
    piece_seg = lax.all_gather(segment_ids, "group", axis=0, tiled=True)
    piece_keys, piece_values = split_keys(piece_kv)
    key_slot = jnp.arange(piece_seg.shape[0], dtype=jnp.int32)
    scores, allowed = masked_scores(
        queries, piece_keys, segment_ids, piece_seg, query_slot, key_slot
    )
    new_max = jnp.maximum(run_max, jnp.max(scores, -1))
    weights = jnp.where(allowed[None], jnp.exp(scores - new_max[..., None]), 0.0)
    run_sum = jnp.sum(weights, -1)
    run_acc = jnp.einsum(
        "hqk,khd->hqd",
        weights.astype(jnp.bfloat16),
        piece_values,
        preferred_element_type=jnp.float32,
    )
    run_max, run_sum, run_acc = (new_max, run_sum, run_acc)
    log_total = run_max + jnp.log(run_sum)
    context = jnp.transpose(run_acc / run_sum[..., None], (1, 0, 2)).astype(jnp.bfloat16)
    context_flat = context.reshape(local_rows, model_width)
    attn_out = jnp.dot(
        context_flat, params["weight_out"], preferred_element_type=jnp.float32
    ) + params["bias_out"].astype(jnp.float32)
    up_pre = jnp.dot(mlp_in, params["weight_up"], preferred_element_type=jnp.float32) + params[
        "bias_up"
    ].astype(jnp.float32)
    up_act = jax.nn.gelu(up_pre, approximate=False).astype(jnp.bfloat16)
    mlp_out = jnp.dot(up_act, params["weight_down"], preferred_element_type=jnp.float32) + params[
        "bias_down"
    ].astype(jnp.float32)
    block_out = (block_in + attn_out + mlp_out).astype(jnp.bfloat16)
    valid_rows = (jnp.arange(local_rows) < counts[0]).astype(jnp.float32)
    grad_rows = grad_out.astype(jnp.float32) * valid_rows[:, None]
    grad_low = grad_rows.astype(jnp.bfloat16)
    bias_grad = jnp.sum(grad_rows, 0)
    grad_dict = {}
    grad_dict["weight_down"] = jnp.dot(up_act.T, grad_low, preferred_element_type=jnp.float32)
    grad_dict["bias_down"] = bias_grad
    grad_dict["weight_out"] = jnp.dot(context_flat.T, grad_low, preferred_element_type=jnp.float32)
    grad_dict["bias_out"] = bias_grad
    grad_act = jnp.dot(grad_low, params["weight_down"].T, preferred_element_type=jnp.float32)
    grad_pre = (grad_act * gelu_slope(up_pre)).astype(jnp.bfloat16)
    grad_dict["weight_up"] = jnp.dot(mlp_in.T, grad_pre, preferred_element_type=jnp.float32)
    grad_dict["bias_up"] = jnp.sum(grad_pre.astype(jnp.float32), 0)
    grad_mlp_in = jnp.dot(grad_pre, params["weight_up"].T, preferred_element_type=jnp.float32)
    grad_context = jnp.dot(
        grad_low, params["weight_out"].T, preferred_element_type=jnp.float32
    ).astype(jnp.bfloat16)
    grad_context = grad_context.reshape(local_rows, head_count, HEAD)
    row_delta = jnp.einsum(
        "qhd,qhd->hq", grad_context.astype(jnp.float32), context.astype(jnp.float32)
    )
    piece_kv = lax.all_gather(key_vals, "group", axis=0, tiled=True)
    piece_seg = lax.all_gather(segment_ids, "group", axis=0, tiled=True)
    piece_keys, piece_values = split_keys(piece_kv)
    count_keys = piece_seg.shape[0]
    key_slot = jnp.arange(count_keys, dtype=jnp.int32)
    scores, allowed = masked_scores(
        queries, piece_keys, segment_ids, piece_seg, query_slot, key_slot
    )
    probs_low, grad_scores = score_grads(
        scores, allowed, log_total, row_delta, grad_context, piece_values
    )
    grad_queries = jnp.einsum(
        "hqk,khd->qhd", grad_scores, piece_keys, preferred_element_type=jnp.float32
    )
    part_keys = jnp.einsum("hqk,qhd->khd", grad_scores, queries, preferred_element_type=jnp.float32)
    part_values = jnp.einsum(
        "hqk,qhd->khd", probs_low, grad_context, preferred_element_type=jnp.float32
    )
    addition = jnp.stack(
        [part_keys.reshape(count_keys, model_width), part_values.reshape(count_keys, model_width)],
        1,
    )
    grad_kv = addition
    grad_queries, batch_kv = (grad_queries, grad_kv)
    grad_kv = lax.psum_scatter(
        batch_kv.astype(jnp.bfloat16), "group", scatter_dimension=0, tiled=True
    ).astype(jnp.float32)
    grad_keys = grad_kv[:, 0].reshape(local_rows, head_count, HEAD)
    grad_values = grad_kv[:, 1].reshape(local_rows, head_count, HEAD)
    grad_qkv = (
        jnp.stack(
            [
                rotate_back(grad_queries, cosine, sine_rows),
                rotate_back(grad_keys, cosine, sine_rows),
                grad_values,
            ],
            1,
        )
        .reshape(local_rows, 3 * model_width)
        .astype(jnp.bfloat16)
    )
    grad_dict["weight_qkv"] = jnp.dot(attn_in.T, grad_qkv, preferred_element_type=jnp.float32)
    grad_dict["bias_qkv"] = jnp.sum(grad_qkv.astype(jnp.float32), 0)
    grad_attn_in = jnp.dot(grad_qkv, params["weight_qkv"].T, preferred_element_type=jnp.float32)
    grad_dict["gain_attn"] = jnp.sum(grad_attn_in * normed, 0)
    grad_dict["shift_attn"] = jnp.sum(grad_attn_in, 0)
    grad_dict["gain_mlp"] = jnp.sum(grad_mlp_in * normed, 0)
    grad_dict["shift_mlp"] = jnp.sum(grad_mlp_in, 0)
    grad_normed = grad_attn_in * gain_attn + grad_mlp_in * gain_mlp
    grad_in = (grad_rows + norm_backward(grad_normed, normed, inv_std)).astype(jnp.bfloat16)
    dp_count = lax.axis_size("dp")
    group_count = lax.axis_size("group")
    partial_value = pack_grads(grad_dict, model_width, FF, master.shape[0] * dp_count * group_count)
    sectioned_grad = lax.psum_scatter(
        partial_value.reshape(dp_count, group_count, -1).astype(jnp.bfloat16),
        "group",
        scatter_dimension=1,
        tiled=True,
    )
    grad_shard = (
        lax.psum_scatter(sectioned_grad, "dp", scatter_dimension=0, tiled=True)
        .astype(jnp.float32)
        .reshape(-1)
    )
    square_sum = lax.psum(jnp.sum(grad_shard * grad_shard), ("dp", "group"))
    grad_scale = 1.0 / (jnp.sqrt(square_sum) + 1e-06)
    scaled = grad_shard * grad_scale
    new_one = BETA_ONE * moment_one + (1.0 - BETA_ONE) * scaled
    new_two = BETA_TWO * moment_two + (1.0 - BETA_TWO) * scaled * scaled
    correct_one = 1.0 - BETA_ONE**STEP
    correct_two = 1.0 - BETA_TWO**STEP
    new_master = master - LEARN_RATE * (
        new_one / correct_one / (jnp.sqrt(new_two / correct_two) + ADAM_EPS) + DECAY_RATE * master
    )
    return (block_out, grad_in, grad_shard, new_master, new_one, new_two)


def padded(count, step):
    return -(-count // step) * step


@functools.lru_cache(None)
def row_plan(width, hidden, dp_count, group_count, shard_len):
    half = width // 2
    row = width * group_count
    devices = dp_count * group_count
    if hidden != row or (width // HEAD) % group_count or shard_len % half or width % 128:
        return None
    base = [i * shard_len // row for i in range(devices)]
    shift = [i * shard_len % row // half for i in range(devices)]
    span = max(-(-(s * half + shard_len) // row) for s in shift)
    stride = shard_len // row
    starts, at = {}, 0
    for entry_name, entry_shape in param_layout(width, hidden):
        starts[entry_name] = at // width
        at += int(np.prod(entry_shape))
    piece_base = [d * group_count * shard_len // row for d in range(dp_count)]
    spans = all(
        base[i] == piece_base[i // group_count] + stride * (i % group_count) for i in range(devices)
    )
    aligned = (
        starts["weight_up"] % group_count == 0
        and starts["weight_down"] % group_count == 0
        and starts["bias_qkv"] % group_count == 0
        and (starts["weight_out"] + 1) % group_count == 0
        and span == stride + 1
        and spans
        and base == [stride * i + i // (2 * group_count) for i in range(devices)]
        and shift == [i % (2 * group_count) for i in range(devices)]
    )
    if not aligned:
        return None
    row_out = starts["bias_qkv"] // group_count
    return dict(
        base=base,
        shift=shift,
        span=span,
        stride=stride,
        starts=starts,
        piece_base=piece_base,
        row_out=row_out,
        row_up=starts["weight_up"] // group_count,
        row_down=starts["weight_down"] // group_count,
        out_chunk=max(i for i in range(devices) if base[i] <= row_out),
        send_rows=padded(span + 7, TILE_ROWS),
        over=[i for i in range(devices - 1) if base[i + 1] == base[i] + stride],
        period=2 * group_count,
    )


def chunk_place(plan, me):
    period = plan["period"]
    return plan["stride"] * me + me // period, lax.rem(me, period)


def flip(value, bit):
    return value + bit - 2 * bit * ((value // bit) % 2)


def remote(src, dst, send_sem, recv_sem, device):
    return pltpu.make_async_remote_copy(
        src_ref=src,
        dst_ref=dst,
        send_sem=send_sem,
        recv_sem=recv_sem,
        device_id=device,
        device_id_type=MESH,
    )


def greet(devices):
    barrier = pltpu.get_barrier_semaphore()
    for device in devices:
        pl.semaphore_signal(barrier, inc=1, device_id=device, device_id_type=MESH)
    pl.semaphore_wait(barrier, len(devices))


def places(group_count):
    d, z = lax.axis_index("dp"), lax.axis_index("group")
    to = [lax.rem(z + k, group_count) for k in range(group_count)]
    frm = [lax.rem(z - k + group_count, group_count) for k in range(group_count)]
    return d, z, to, frm


def layer_kernel(
    plan, dp_count, group_count, flat, turn_in, unperm, tok, grd, seg, pos, used, grad, block_out, grad_in,
    square_sum, swap_a, swap_b, rs, rr, ls, lr, pad, send, stage, near, obuf, whole, toks, grds, idss, outs, w32, gm32, w_up, w_down,
    w_qkv, w_out, normed, attn_in, mlp_in, slope, act, g_pre, g_low, acc, g_mlp, tabs, qm, km,
    vm, gm, k_all, v_all, ctx, gq, gk, gv, g_qkv, rel_a, rel_b, parts_a, parts_b, gout, held,
    from_core, from_first, from_last, total, gbuf, slabs, back, sq, sqz, sqd, loc, p1s, p1r,
    cs, cr, xs, xr, ys, yr, ts, tr, os, orr, fcs, fcr, fxs, fxr, fys, fyr, zs, zr, gs, gr, bs,
    br, qs, qr, ds, dr,
):
    d, z, to, frm = places(group_count)
    n = group_count
    dc, dx, dy = flip(d, 1), flip(d, 2), flip(d, 4)
    dxy = flip(dx, 4)
    m = dp_count
    turn_to = [lax.rem(d + k, m) for k in range(m)]
    turn_from = [lax.rem(d - k + m, m) for k in range(m)]
    greet([(d, to[k]) for k in range(1, n)] + [(turn_to[k], z) for k in range(1, m)])
    later = []

    def share(j, ref):
        for k in range(1, n):
            copy = remote(ref.at[z], ref.at[z], ts.at[j, k], tr.at[j, k], (d, to[k]))
            copy.start()
            other = remote(ref.at[z], ref.at[frm[k]], ts.at[j, k], tr.at[j, k], (d, to[k]))
            later.append((copy, other))

    def settle():
        for copy, other in later:
            other.wait_recv()
            copy.wait_send()
        later.clear()

    def hop_start(j, ref, s):
        @pl.when((z < n - 1) & (z - s + 1 >= 0))
        def _():
            block = ref.at[z - s + 1]
            remote(block, block, rs.at[j, s], rr.at[j, s], (d, z + 1)).start()

        @pl.when((z > 0) & (z + s - 1 <= n - 1))
        def _():
            block = ref.at[z + s - 1]
            remote(block, block, ls.at[j, s], lr.at[j, s], (d, z - 1)).start()

    def hop_arrived(j, ref, s):
        @pl.when(z - s >= 0)
        def _():
            block = ref.at[z - s]
            remote(block, block, rs.at[j, s], rr.at[j, s], (d, z - 1)).wait_recv()

        @pl.when(z + s <= n - 1)
        def _():
            block = ref.at[z + s]
            remote(block, block, ls.at[j, s], lr.at[j, s], (d, z + 1)).wait_recv()

    def hop_sent(j, ref, s):
        @pl.when((z < n - 1) & (z - s + 1 >= 0))
        def _():
            block = ref.at[z - s + 1]
            remote(block, block, rs.at[j, s], rr.at[j, s], (d, z + 1)).wait_send()

        @pl.when((z > 0) & (z + s - 1 <= n - 1))
        def _():
            block = ref.at[z + s - 1]
            remote(block, block, ls.at[j, s], lr.at[j, s], (d, z - 1)).wait_send()

    def hop_on(j, ref, s):
        hop_arrived(j, ref, s)
        if s < n - 1:
            hop_start(j, ref, s + 1)

    toks[z] = tok[...]
    idss[z] = jnp.concatenate(
        [seg[...], pos[...], jnp.zeros((6, seg.shape[1]), jnp.int32)], 0
    )
    hop_start(0, toks, 1)
    share(0, idss)
    slot = lax.broadcasted_iota(jnp.int32, (tok.shape[0], 1), 0)
    grds[z] = jnp.where(slot < used[0], grd[...].astype(jnp.float32), 0.0).astype(jnp.bfloat16)
    span, stride = plan["span"], plan["stride"]
    send_rows, width = send.shape[1:]
    unit = width // n
    tiles = width // 128
    group = tiles * n
    length = flat.shape[0]
    me = d * n + z
    base, shift = chunk_place(plan, me)
    pad[0:group] = jnp.zeros((group, 128), jnp.float32)
    pad[group : group + length] = flat[...]
    rest = pad.shape[0] - group - length
    pad[group + length :] = jnp.zeros((rest, 128), jnp.float32)
    row = base + lax.broadcasted_iota(jnp.int32, (send_rows, 1), 0)
    whole_lines = ((row >= plan["row_out"]) & (row < plan["row_up"])) | (row >= plan["row_down"])
    up_rows = (row >= plan["row_up"]) & (row < plan["row_down"])
    first_row = group - tiles // 2 * shift
    for b in range(n):
        stage[b] = jnp.concatenate(
            [
                pad[pl.ds(first_row + tiles * b + t, send_rows, stride=group), :]
                for t in range(tiles)
            ],
            1,
        )
    for b in range(n):
        line = stage[b]
        turned = jnp.dot(
            line.astype(jnp.bfloat16), turn_in[...], preferred_element_type=jnp.float32
        )
        near[b] = jnp.where(up_rows, turned, line)
    extra = jnp.concatenate(
        [stage[j % n, stride - 1 + j // n : stride + j // n, :] for j in range(send_rows - span)], 0
    )
    for g in range(n):
        by_column = jnp.concatenate([near[b][:, g * unit : (g + 1) * unit] for b in range(n)], 1)
        value = jnp.where(whole_lines, stage[g], by_column)
        value = jnp.concatenate([value[:stride], jnp.concatenate([value[stride:span], extra], 0)], 0)
        send[g] = value.astype(jnp.bfloat16)
    first = []
    for k in range(1, n):
        copy = remote(send.at[to[k]], whole.at[d, z], p1s.at[k], p1r.at[k], (d, to[k]))
        copy.start()
        first.append(copy)
    whole[d, z] = send[z]
    hop_on(0, toks, 1)
    sent = []

    def push(ref, s, r, device):
        copy = remote(ref, ref, s, r, device)
        copy.start()
        sent.append(copy)

    def arrived(ref, s, r, device):
        remote(ref, ref, s, r, device).wait_recv()

    for k in range(n):
        ref = whole.at[d, frm[k]]
        if k > 0:
            arrived(ref, p1s.at[k], p1r.at[k], (d, to[k]))
        push(ref, xs.at[k], xr.at[k], (dx, z))
        push(ref, ys.at[k], yr.at[k], (dy, z))
        push(ref, cs.at[k], cr.at[k], (dc, z))
    settle()
    hop_on(0, toks, 2)
    hop_start(1, grds, 1)
    for k in range(n):
        by_x, by_y = whole.at[dx, frm[k]], whole.at[dy, frm[k]]
        arrived(by_x, xs.at[k], xr.at[k], (dx, z))
        if k < n // 2:
            push(by_x, ys.at[n + k], yr.at[n + k], (dy, z))
        push(by_x, cs.at[n + k], cr.at[n + k], (dc, z))
        arrived(by_y, ys.at[k], yr.at[k], (dy, z))
        if k >= n // 2:
            push(by_y, xs.at[n + k], xr.at[n + k], (dx, z))
        push(by_y, cs.at[2 * n + k], cr.at[2 * n + k], (dc, z))
    hop_on(1, grds, 1)
    for k in range(n):
        across = whole.at[dxy, frm[k]]
        if k < n // 2:
            arrived(across, ys.at[n + k], yr.at[n + k], (dy, z))
        else:
            arrived(across, xs.at[n + k], xr.at[n + k], (dx, z))
        push(across, cs.at[3 * n + k], cr.at[3 * n + k], (dc, z))
    for j, owner in enumerate((d, dx, dy, dxy)):
        for k in range(n):
            ref = whole.at[flip(owner, 1), frm[k]]
            arrived(ref, cs.at[j * n + k], cr.at[j * n + k], (dc, z))
    hop_on(1, grds, 2)
    for copy in first + sent:
        copy.wait_send()
    chunks = [plan["out_chunk"] + j for j in range(4)]
    chunks = [whole[i // n, i % n].astype(jnp.float32) for i in chunks]
    block = unit // n
    lines = []
    for j in range(1, 4):
        count = min(stride, unit - stride * (j - 1))
        part = chunks[j][:count]
        if j > 1:
            head = chunks[j - 1][stride : stride + 8]
            row8 = lax.broadcasted_iota(jnp.int32, (8, 1), 0)
            part = jnp.concatenate([part[:8] + jnp.where(row8 == 0, head, 0.0), part[8:]], 0)
        lines.append(part)
    lines = jnp.concatenate(lines, 0)
    before = chunks[0][stride : stride + 1]
    moved = pltpu.roll(lines, 1, 0)
    at = lax.broadcasted_iota(jnp.int32, (unit, 1), 0)
    moved = jnp.where(at == 0, before, moved)
    lines = jnp.where(z == n - 1, moved, lines).astype(jnp.bfloat16)
    for g in range(n):
        obuf[g] = lines[g * block : (g + 1) * block]
    outs[z] = obuf[z]
    outs_moving = []
    for k in range(1, n):
        copy = remote(obuf.at[to[k]], outs.at[z], os.at[k], orr.at[k], (d, to[k]))
        copy.start()
        outs_moving.append(
            (copy, remote(obuf.at[to[k]], outs.at[frm[k]], os.at[k], orr.at[k], (d, to[k])))
        )
    f32, bf16 = jnp.float32, jnp.bfloat16
    rows = normed.shape[0]
    local = rows // n
    wide = 256
    heads = unit // HEAD
    bases = plan["base"]
    row_out, row_up, row_down, over = plan["row_out"], plan["row_up"], plan["row_down"], plan["over"]

    def mm(lhs, rhs):
        return jnp.dot(lhs, rhs, preferred_element_type=f32)

    def mm_t(lhs, rhs):
        return lax.dot_general(lhs, rhs, (((1,), (1,)), ((), ())), preferred_element_type=f32)

    def t_mm(lhs, rhs):
        return lax.dot_general(lhs, rhs, (((0,), (0,)), ((), ())), preferred_element_type=f32)

    def chunk(i):
        return whole[i // n, i % n].astype(f32)

    def fill(low, high):
        for i, first in enumerate(bases):
            last = first + (stride if i in over else span)
            lo, hi = max(low, first), min(high, last)
            if lo >= hi:
                continue
            w32[lo - low : hi - low] = chunk(i)[lo - first : hi - first]
            if lo == first and i - 1 in over:
                tail = whole[(i - 1) // n, (i - 1) % n, stride : stride + 8].astype(f32)[:1]
                w32[lo - low : lo - low + 1] = w32[lo - low : lo - low + 1] + tail

    def line(row):
        i = max(i for i in range(len(bases)) if bases[i] <= row)
        return chunk(i)[row - bases[i] : row - bases[i] + 1]

    fill(row_up, row_up + width)
    w_up[...] = w32[:width].astype(bf16)
    fill(row_down, row_down + width)
    w_down[...] = w32[:width].astype(bf16)
    fill(0, row_out)
    third = width // n
    gap = jnp.zeros((third, wide - unit), f32)
    for t in range(tiles):
        rel_a[t, :row_out] = w32[:row_out, t * 128 : (t + 1) * 128]

    def strided_rows(ref, start, step):
        return jnp.concatenate(
            [ref[t, pl.ds(start, third, stride=step), :] for t in range(tiles)], 1
        )

    def put_rows(ref, start, step, value):
        for t in range(tiles):
            ref[t, pl.ds(start, third, stride=step), :] = value[:, t * 128 : (t + 1) * 128]

    planes = [strided_rows(rel_a, p, 3) for p in range(3)]
    for t in range(n):
        blocks = []
        for j in range(3):
            p, b = (3 * t + j) // n, (3 * t + j) % n
            blocks += [planes[p][:, b * unit : (b + 1) * unit], gap]
        put_rows(rel_b, t, n, jnp.concatenate(blocks, 1))
    for t in range(tiles):
        w_qkv[:, t * 128 : (t + 1) * 128] = rel_b[t].astype(bf16)
    bias_up = line(row_up + width)
    vectors = chunk(len(bases) - 1)[span : span + n + 1]
    bias_down, gain_attn, shift_attn, gain_mlp, shift_mlp = (vectors[j : j + 1] for j in range(5))
    is_last = z == n - 1
    bias_rest = jnp.where(is_last, bias_down + line(row_up - 1), 0.0)
    bias_lines = chunk(plan["out_chunk"])[span + n : span + n + 3]
    bias_qkv = []
    for j in range(3):
        mine = jnp.zeros((1, unit), f32)
        for g in range(n):
            mine = jnp.where(z == g, bias_lines[j : j + 1, g * unit : (g + 1) * unit], mine)
        bias_qkv += [mine, jnp.zeros((1, wide - unit), f32)]
    bias_qkv = jnp.concatenate(bias_qkv, 1)

    step = 64
    hop_on(0, toks, 3)

    @pl.loop(0, rows // step)
    def _(i):
        at = pl.ds(i * step, step)
        x = toks[i // (local // step), pl.ds(i % (local // step) * step, step), :].astype(f32)
        centred = x - jnp.mean(x, -1, keepdims=True)
        inv = lax.rsqrt(jnp.mean(centred * centred, -1, keepdims=True) + NORM_EPS)
        value = centred * inv
        normed[at, :] = value
        attn_in[at, :] = (value * gain_attn + shift_attn).astype(bf16)
        mlp_in[at, :] = (value * gain_mlp + shift_mlp).astype(bf16)

    w32[0:8] = jnp.broadcast_to(bias_up, (8, width))
    w32[8:16] = jnp.broadcast_to(bias_qkv, (8, width))

    @pl.loop(0, width // wide)
    def _(i):
        at = pl.ds(pl.multiple_of(i * wide, wide), wide)
        up = mm(mlp_in[...], w_up[:, at]) + w32[0:1, at]
        half = 0.5 * (1.0 + lax.erf(up * 0.7071067811865476))
        act[:, at] = (up * half).astype(bf16)
        slope[:, at] = half + up * jnp.exp(-0.5 * up * up) * 0.3989422804014327

    @pl.loop(0, width // wide)
    def _(i):
        at = pl.ds(pl.multiple_of(i * wide, wide), wide)
        acc[:, at] = mm(act[...], w_down[:, at])

    position = jnp.concatenate([idss[g, 1:2, :] for g in range(n)], 1).astype(f32)
    half_rot = ROT // 2
    at_freq = lax.broadcasted_iota(jnp.int32, (half_rot, 1), 0)
    freq = jnp.zeros((half_rot, 1), f32)
    for i in range(half_rot):
        freq = jnp.where(at_freq == i, float(10000.0 ** (-2.0 * i / ROT)), freq)
    angles = freq * position
    lane = lax.broadcasted_iota(jnp.int32, (half_rot, wide), 1) % HEAD
    same = lane % half_rot == lax.broadcasted_iota(jnp.int32, (half_rot, wide), 0)
    hot = [same & (lane < ROT), same & (lane < half_rot), same & (lane >= half_rot) & (lane < ROT)]

    def expand(table, where):
        return lax.dot_general(
            table,
            where.astype(f32),
            (((0,), (0,)), ((), ())),
            precision=lax.Precision.HIGHEST,
            preferred_element_type=f32,
        )

    cosine, sine = jnp.cos(angles), jnp.sin(angles)
    lane_wide = lax.broadcasted_iota(jnp.int32, (1, wide), 1)
    head_lane = lane_wide % HEAD
    tabs[0] = expand(cosine, hot[0]) + jnp.where(head_lane >= ROT, 1.0, 0.0)
    tabs[1] = expand(sine, hot[1])
    tabs[2] = expand(sine, hot[2])

    def turn(value, at, sign):
        ahead = pltpu.roll(value, wide - half_rot, 1)
        behind = pltpu.roll(value, half_rot, 1)
        return value * tabs[0, at] + sign * (behind * tabs[2, at] - ahead * tabs[1, at])

    def masked(ref, value):
        for h in range(heads):
            ref[h] = jnp.where(lane_wide // HEAD == h, value, 0.0).astype(bf16)

    every = slice(0, rows)
    q32 = turn(mm(attn_in[...], w_qkv[:, :wide]) + w32[8:9, :wide], every, 1.0)
    masked(qm, q32)
    k32 = turn(mm(attn_in[...], w_qkv[:, wide : 2 * wide]) + w32[8:9, wide : 2 * wide], every, 1.0)
    masked(km, k32)
    k_all[...] = k32.astype(bf16)
    v32 = mm(attn_in[...], w_qkv[:, 2 * wide :]) + w32[8:9, 2 * wide :]
    masked(vm, v32)
    v_all[...] = v32.astype(bf16)
    for copy, other in outs_moving:
        other.wait_recv()
        copy.wait_send()
    order = [(t - 1) % n for t in range(n)]
    out_rows = jnp.concatenate([outs[j] for j in order], 0)
    w_out[...] = mm(unperm[...], out_rows).astype(bf16)
    hop_on(1, grds, 3)
    for g in range(n):
        g_low[g * local : (g + 1) * local] = grds[g]
    masked(gm, mm_t(g_low[...], w_out[...]).astype(bf16).astype(f32))

    @pl.loop(0, width // wide)
    def _(i):
        at = pl.ds(pl.multiple_of(i * wide, wide), wide)
        g_pre[:, at] = (mm_t(g_low[...], w_down[at, :]) * slope[:, at]).astype(bf16)

    @pl.loop(0, width // wide)
    def _(i):
        at = pl.ds(pl.multiple_of(i * wide, wide), wide)
        g_mlp[:, at] = mm_t(g_pre[...], w_up[at, :])

    bias_grad = jnp.where(is_last, jnp.sum(g_low[...].astype(f32), 0, keepdims=True), 0.0)

    def swap_start(j, src, dst, b):
        @pl.when(z != b)
        def _():
            remote(src.at[b], dst.at[z], zs.at[j, b], zr.at[j, z], (d, b)).start()

        @pl.when(z == b)
        def _():
            dst[b] = src[b]

    def swap_end(j, src, dst):
        for b in range(n):
            @pl.when(z != b)
            def _():
                remote(src.at[b], dst.at[b], zs.at[j, b], zr.at[j, b], (d, b)).wait_recv()
                remote(src.at[b], dst.at[b], zs.at[j, b], zr.at[j, b], (d, b)).wait_send()

    seg_row = jnp.concatenate([idss[g, 0:1, :] for g in range(n)], 1).astype(f32)
    seg_col = jnp.transpose(jnp.broadcast_to(seg_row, (128, rows)))[:, 0:1]
    ctx[...] = jnp.zeros_like(ctx)
    gq[...] = jnp.zeros_like(gq)
    gk[...] = jnp.zeros_like(gk)
    gv[...] = jnp.zeros_like(gv)
    vecs = [[], [], [], []]
    ends_first = [b for pair in zip(range(n // 2), reversed(range(n))) for b in pair]
    for b in ends_first:
        at = slice(b * local, (b + 1) * local)
        upto = (b + 1) * local
        seen = slice(0, upto)
        earlier = lax.broadcasted_iota(jnp.int32, (local, upto), 1) <= b * local + (
            lax.broadcasted_iota(jnp.int32, (local, upto), 0)
        )
        allowed = (seg_col[at] == seg_row[:, seen]) & earlier

        @pl.loop(0, heads)
        def _(h):
            scores = jnp.where(allowed, mm_t(qm[h, at], k_all[seen]) * SCORE_SCALE, MASKED)
            top = jnp.max(scores, -1, keepdims=True)
            weights = jnp.exp(scores - top)
            probs = weights / jnp.sum(weights, -1, keepdims=True)
            low = probs.astype(bf16)
            context = mm(low, vm[h, seen])
            ctx[at] += context
            kept = context.astype(bf16).astype(f32)
            delta = jnp.sum(gm[h, at].astype(f32) * kept, -1, keepdims=True)
            slanted = (probs * (mm_t(gm[h, at], v_all[seen]) - delta) * SCORE_SCALE).astype(bf16)
            gq[at] += mm(slanted, km[h, seen])
            gk[seen] += t_mm(slanted, qm[h, at])
            gv[seen] += t_mm(low, gm[h, at])

        parts_a[b] = (acc[at] + mm(ctx[at].astype(bf16), w_out[...]) + bias_rest).astype(bf16)
        swap_start(0, parts_a, swap_a, b)

    ctx_low = ctx[...].astype(bf16)
    g_qkv[:, :wide] = turn(gq[...], every, -1.0).astype(bf16)
    g_qkv[:, wide : 2 * wide] = turn(gk[...], every, -1.0).astype(bf16)
    g_qkv[:, 2 * wide :] = gv[...].astype(bf16)
    for i in range(width // wide):
        at = slice(i * wide, (i + 1) * wide)
        g_attn = mm_t(g_qkv[...], w_qkv[at, :])
        g_up = g_mlp[:, at]
        value = (g_attn * gain_attn[:, at] + g_up * gain_mlp[:, at]).astype(bf16)
        for g in range(n):
            parts_b[g, :, at] = value[g * local : (g + 1) * local]
        here = normed[:, at]
        for j, term in enumerate((g_attn * here, g_attn, g_up * here, g_up)):
            vecs[j].append(jnp.sum(term, 0, keepdims=True))
    out_grad = t_mm(ctx_low, g_low[...]).astype(bf16)
    out_grad = t_mm(unperm[...], out_grad).astype(bf16)
    for g in range(n):
        t = (g + 1) % n
        gout[g] = out_grad[t * block : (t + 1) * block]
    gbuf[z] = gout[z]
    trades = []
    for k in range(1, n):
        copy = remote(gout.at[to[k]], gbuf.at[z], gs.at[k], gr.at[k], (d, to[k]))
        copy.start()
        trades.append((copy, remote(gout.at[to[k]], gbuf.at[frm[k]], gs.at[k], gr.at[k], (d, to[k]))))
    for b in range(n):
        swap_start(1, parts_b, swap_b, b)
    for i in range(width // wide):
        at = slice(i * wide, (i + 1) * wide)
        gm32[row_up + i * wide : row_up + (i + 1) * wide] = t_mm(mlp_in[:, at], g_pre[...])
        gm32[row_down + i * wide : row_down + (i + 1) * wide] = t_mm(act[:, at], g_low[...])
    gm32[row_up + width : row_up + width + 1] = jnp.sum(g_pre[...].astype(f32), 0, keepdims=True)
    for i in range(width // wide):
        at = slice(i * wide, (i + 1) * wide)
        value = t_mm(attn_in[:, at], g_qkv[...])
        for t in range(tiles):
            rel_b[t, at] = value[:, t * 128 : (t + 1) * 128]
    columns = [strided_rows(rel_b, t, n) for t in range(n)]
    for p in range(3):
        blocks = []
        for b in range(n):
            t, j = (n * p + b) // 3, (n * p + b) % 3
            blocks.append(columns[t][:, j * wide : j * wide + unit])
        put_rows(rel_a, p, 3, jnp.concatenate(blocks, 1))
    for t in range(tiles):
        gm32[:row_out, t * 128 : (t + 1) * 128] = rel_a[t, :row_out]
    gm32[row_out:row_up] = jnp.zeros((row_up - row_out, width), f32)
    gm32[row_up - 1 : row_up] = bias_grad
    row_end = row_down + width
    gm32[row_end:] = jnp.zeros((gm32.shape[0] - row_end, width), f32)
    sums = jnp.sum(g_qkv[...].astype(f32), 0, keepdims=True)
    sums = jnp.concatenate(
        [sums[:, j * wide : j * wide + unit] for j in range(3)] + [jnp.zeros((1, unit), f32)], 1
    )
    extra = [bias_grad] + [jnp.concatenate(v, 1) for v in vecs] + [sums, jnp.zeros((2, width), f32)]
    body = n * stride
    for e, first in enumerate(plan["piece_base"]):
        held[e, :body] = gm32[first : first + body].astype(bf16)
        last = [gm32[first + body : first + body + 1], jnp.zeros((7, width), f32)] + extra
        held[e, body:] = jnp.concatenate(last, 0).astype(bf16)
    y, x, c = d // 4, lax.rem(d // 2, 2), lax.rem(d, 2)
    rows = total.shape[0]
    cut = padded(rows // 2, TILE_ROWS)
    for copy, other in trades:
        other.wait_recv()
    out_rows = jnp.concatenate([gbuf[g].astype(f32) for g in range(n)], 0)
    at = lax.broadcasted_iota(jnp.int32, (unit, 1), 0)
    moved = jnp.where(at == unit - 1, 0.0, pltpu.roll(out_rows, unit - 1, 0))
    is_last = z == n - 1
    after = plan["out_chunk"] // n + 1
    held[after, :unit] = (
        held[after, :unit].astype(f32) + jnp.where(is_last, moved, out_rows)
    ).astype(bf16)
    at = lax.broadcasted_iota(jnp.int32, (TILE_ROWS, 1), 0)
    first_line = jnp.where((at == 0) & is_last, out_rows[:1], 0.0)
    held[after - 1, body:] = (held[after - 1, body:].astype(f32) + first_line).astype(bf16)

    low, high = pl.ds(0, cut), pl.ds(cut, rows - cut)
    here = 2 * y + x
    quads = [flip(flip(here, 1), 2), flip(here, 1), flip(here, 2), here]
    mine = [held.at[2 * q + c] for q in quads]
    cross = []
    for k in range(4):
        copy = remote(
            held.at[2 * quads[k] + 1 - c], from_core.at[k], fcs.at[k], fcr.at[k], (dc, z)
        )
        copy.start()
        cross.append(copy)

    def add(dst, src):
        dst[...] = (dst[...].astype(f32) + src[...].astype(f32)).astype(dst.dtype)

    sent = []

    def pass_on(src, dst, s, r, device):
        copy = remote(src, dst, s, r, device)
        copy.start()
        sent.append(copy)
        return copy

    by_x, by_y = (dx, z), (dy, z)
    for k in range(4):
        cross[k].wait_recv()
        add(mine[k], from_core.at[k])
        if k == 0:
            x0 = pass_on(mine[0].at[low], from_first.at[0, low], fxs.at[0], fxr.at[0], by_x)
            y0 = pass_on(mine[0].at[high], from_first.at[0, high], fys.at[0], fyr.at[0], by_y)
        elif k == 1:
            x1 = pass_on(mine[1].at[low], from_first.at[1, low], fxs.at[1], fxr.at[1], by_x)
        elif k == 2:
            y1 = pass_on(mine[2].at[high], from_first.at[1, high], fys.at[1], fyr.at[1], by_y)
    x0.wait_recv()
    add(mine[2].at[low], from_first.at[0, low])
    y2 = pass_on(mine[2].at[low], from_last.at[low], fys.at[2], fyr.at[2], by_y)
    y0.wait_recv()
    add(mine[1].at[high], from_first.at[0, high])
    x2 = pass_on(mine[1].at[high], from_last.at[high], fxs.at[2], fxr.at[2], by_x)
    x1.wait_recv()
    add(mine[3].at[low], from_first.at[1, low])
    y1.wait_recv()
    add(mine[3].at[high], from_first.at[1, high])
    y2.wait_recv()
    x2.wait_recv()
    total[...] = (mine[3][...].astype(f32) + from_last[...].astype(f32)).astype(bf16).astype(f32)

    odd = lax.rem(d, 2)
    at = lax.broadcasted_iota(jnp.int32, (rows, 1), 0)
    counted = jnp.where((at >= odd) & (at < body + 1), total[...], 0.0)
    sq[z] = jnp.full(sq.shape[1:], jnp.sum(counted * counted), f32)
    for k in range(1, n):
        copy = remote(sq.at[z], sq.at[z], qs.at[k], qr.at[k], (d, to[k]))
        copy.start()
        sent.append(copy)
    extra = total[body + 8 : body + 14]
    for j in range(n):
        slab = jnp.concatenate(
            [
                total[stride * j : stride * j + stride],
                jnp.concatenate(
                    [total[stride * j + stride : stride * j + span], extra, jnp.zeros((1, width), f32)], 0
                ),
            ],
            0,
        )
        slabs[j] = slab.astype(bf16)
    far = []
    for k in range(1, n):
        copy = remote(slabs.at[to[k]], back.at[z], bs.at[k], br.at[k], (d, to[k]))
        copy.start()
        far.append((copy, remote(slabs.at[to[k]], back.at[frm[k]], bs.at[k], br.at[k], (d, to[k]))))
    back[z] = slabs[z]
    for k in range(1, n):
        remote(sq.at[z], sq.at[frm[k]], qs.at[k], qr.at[k], (d, to[k])).wait_recv()
    sqz[...] = sq[0] + sq[1] + sq[2] + sq[3]
    sqd[d] = sqz[...]
    for k in range(1, m):
        copy = remote(sqz, sqd.at[d], ds.at[k], dr.at[k], (turn_to[k], z))
        copy.start()
        sent.append(copy)
    swap_end(0, parts_a, swap_a)
    swap_end(1, parts_b, swap_b)
    x = toks[z].astype(f32)
    value = x
    for g in range(n):
        value = value + swap_a[g].astype(f32)
    block_out[...] = value.astype(bf16)
    centred = x - jnp.mean(x, -1, keepdims=True)
    inv = lax.rsqrt(jnp.mean(centred * centred, -1, keepdims=True) + NORM_EPS)
    own_normed = centred * inv
    value = swap_b[0].astype(f32)
    for g in range(1, n):
        value = value + swap_b[g].astype(f32)
    value = norm_backward(value, own_normed, inv)
    grad_in[...] = (grds[z].astype(f32) + value).astype(bf16)
    for copy, other in far:
        other.wait_recv()

    for g in range(n):
        stage[g] = back[g].astype(f32)
    vec = stage[0, stride : stride + 8]
    for g in range(1, n):
        vec = vec + stage[g, stride : stride + 8]
    vec = vec[1:6]
    bias_rows = [stage[g, span + 5 : span + 6] for g in range(n)]
    squares = jnp.sum(vec * vec)
    for g in range(n):
        squares = squares + jnp.sum(bias_rows[g] * bias_rows[g])
    row_end = plan["row_down"] + width
    for b in range(n):
        part = slice(b * unit, (b + 1) * unit)
        by_column = jnp.concatenate([stage[g, :, part] for g in range(n)], 1)
        unturned = lax.dot_general(
            by_column.astype(bf16), turn_in[...], (((1,), (1,)), ((), ())), preferred_element_type=f32
        )
        value = jnp.where(up_rows, unturned, by_column)
        value = jnp.where(whole_lines, stage[b], value)
        if b < 3:
            bias_line = jnp.concatenate([bias_rows[g][:, part] for g in range(n)], 1)
            value = jnp.where(row == plan["row_out"], bias_line, value)
        value = jnp.where(row == row_end, vec[b : b + 1], value)
        if b == 0:
            value = jnp.where(row == row_end + 1, vec[n : n + 1], value)
        for t in range(tiles):
            pad[pl.ds(first_row + tiles * b + t, send_rows, stride=group), :] = value[
                :, t * 128 : (t + 1) * 128
            ]
    grad[...] = pad[group : group + grad.shape[0]]
    for k in range(1, m):
        remote(sqz, sqd.at[turn_from[k]], ds.at[k], dr.at[k], (turn_to[k], z)).wait_recv()
    result = sqd[0]
    for k in range(1, m):
        result = result + sqd[k]
    square_sum[...] = result + squares
    for copy in cross + sent:
        copy.wait_send()
    hop_tensors = ((0, toks), (1, grds))
    for j, ref in hop_tensors:
        for k in range(1, n):
            hop_sent(j, ref, k)
    for copy, other in trades + far:
        copy.wait_send()


def layer_call(plan, dp_count, group_count, flat, turn_in, unperm, tok, grd, seg, pos, used):
    n, m = group_count, dp_count
    local, width = tok.shape
    rows = local * n
    f32, bf16 = jnp.float32, jnp.bfloat16
    wide, heads = 256, width // n // HEAD
    block = width // n // n
    send_rows = plan["send_rows"]
    group = width // 128 * n
    pad_rows = padded(2 * group + group * send_rows, 8)
    row_end = plan["row_down"] + width
    piece = n * plan["stride"] + TILE_ROWS

    def fl(*shape):
        return pltpu.VMEM(shape, f32)

    def bf(*shape):
        return pltpu.VMEM(shape, bf16)

    return pl.pallas_call(
        functools.partial(layer_kernel, plan, m, n),
        out_shape=[
            jax.ShapeDtypeStruct(flat.shape, f32),
            jax.ShapeDtypeStruct((local, width), bf16),
            jax.ShapeDtypeStruct((local, width), bf16),
            jax.ShapeDtypeStruct((8, 128), f32),
        ],
        in_specs=[INVMEM] * 7 + [pl.BlockSpec(memory_space=pltpu.SMEM)],
        out_specs=[INVMEM] * 4,
        scratch_shapes=[
            bf(n, local, width),
            bf(n, local, width),
            DMA((2, n)), DMA((2, n)), DMA((2, n)), DMA((2, n)),
            fl(pad_rows, 128),
            bf(n, send_rows, width),
            fl(n, send_rows, width),
            fl(n, send_rows, width),
            bf(n, block, width),
            bf(m, n, send_rows, width),
            bf(n, local, width),
            bf(n, local, width),
            pltpu.VMEM((n, 8) + seg.shape[1:], jnp.int32),
            bf(n, block, width),
            fl(width + 8, width),
            fl(padded(row_end + 8, 8), width),
            bf(width, width),
            bf(width, width),
            bf(width, 3 * wide),
            bf(wide, width),
            fl(rows, width),
            bf(rows, width),
            bf(rows, width),
            fl(rows, width),
            bf(rows, width),
            bf(rows, width),
            bf(rows, width),
            fl(rows, width),
            fl(rows, width),
            fl(3, rows, wide),
            bf(heads, rows, wide),
            bf(heads, rows, wide),
            bf(heads, rows, wide),
            bf(heads, rows, wide),
            bf(rows, wide),
            bf(rows, wide),
            fl(rows, wide),
            fl(rows, wide),
            fl(rows, wide),
            fl(rows, wide),
            bf(rows, 3 * wide),
            fl(width // 128, width, 128),
            fl(width // 128, width, 128),
            bf(n, local, width),
            bf(n, local, width),
            bf(n, block, width),
            bf(m, piece, width),
            bf(4, piece, width),
            bf(2, piece, width),
            bf(piece, width),
            fl(piece, width),
            bf(n, block, width),
            bf(n, send_rows, width),
            bf(n, send_rows, width),
            fl(n, 8, 128),
            fl(8, 128),
            fl(m, 8, 128),
            DMA((8,)),
            DMA((n,)),
            DMA((n,)),
            DMA((4 * n,)),
            DMA((4 * n,)),
            DMA((2 * n,)),
            DMA((2 * n,)),
            DMA((2 * n,)),
            DMA((2 * n,)),
            DMA((3, n)),
            DMA((3, n)),
            DMA((n,)),
            DMA((n,)),
            DMA((4,)),
            DMA((4,)),
            DMA((3,)),
            DMA((3,)),
            DMA((3,)),
            DMA((3,)),
            DMA((2, n)),
            DMA((2, n)),
            DMA((n,)),
            DMA((n,)),
            DMA((n,)),
            DMA((n,)),
            DMA((n,)),
            DMA((n,)),
            DMA((m,)),
            DMA((m,)),
        ],
        compiler_params=pltpu.CompilerParams(
            collective_id=1, has_side_effects=True, vmem_limit_bytes=62 * 2**20
        ),
        name="layer_parts",
    )(flat, turn_in, unperm, tok, grd, seg, pos, used)


def one_hot(size, natural):
    return (np.arange(size)[:, None] == np.asarray(natural)[None, :]).astype(np.float32)


def strided(size, step):
    each = size // step
    column = np.arange(size)
    return one_hot(size, (column % each) * step + column // each)


def on_device_split(tokens, grad_out, segment_ids, positions, counts, master, moment_one, moment_two):
    bf16 = jnp.bfloat16
    dp_count, group_count = lax.axis_size("dp"), lax.axis_size("group")
    width = tokens.shape[1]
    n = group_count
    plan = row_plan(width, FF, dp_count, n, master.shape[0])
    turn_in = jnp.asarray(strided(width, n), bf16)
    unit = width // n
    unperm = jnp.asarray(np.pad(strided(unit, n), ((0, 256 - unit), (0, 0))), bf16)

    flat = master.reshape(-1, 128)
    seg, pos = segment_ids.reshape(1, -1), positions.reshape(1, -1)
    grad_rows, block_out, grad_in, squares = layer_call(
        plan, dp_count, n, flat, turn_in, unperm, tokens, grad_out, seg, pos, counts
    )
    grad_shard = grad_rows.reshape(-1)
    return (block_out, grad_in) + update(grad_shard, squares[0, 0], master, moment_one, moment_two)


def update(grad_shard, square_sum, master, moment_one, moment_two):
    grad_scale = 1.0 / (jnp.sqrt(square_sum) + 1e-06)
    scaled = grad_shard * grad_scale
    new_one = BETA_ONE * moment_one + (1.0 - BETA_ONE) * scaled
    new_two = BETA_TWO * moment_two + (1.0 - BETA_TWO) * scaled * scaled
    correct_one = 1.0 - BETA_ONE**STEP
    correct_two = 1.0 - BETA_TWO**STEP
    new_master = master - LEARN_RATE * (
        new_one / correct_one / (jnp.sqrt(new_two / correct_two) + ADAM_EPS) + DECAY_RATE * master
    )
    return (grad_shard, new_master, new_one, new_two)


def on_device(tokens, grad_out, segment_ids, positions, counts, master, moment_one, moment_two):
    dp_count, group_count = lax.axis_size("dp"), lax.axis_size("group")
    width = tokens.shape[1]
    splits = (
        (dp_count, group_count) == (8, 4)
        and tokens.shape[0] == 128
        and width // group_count <= 256
        and row_plan(width, FF, dp_count, group_count, master.shape[0]) is not None
    )
    body = on_device_split if splits else on_device_gathered
    return body(tokens, grad_out, segment_ids, positions, counts, master, moment_one, moment_two)


def solution(mesh):
    placed = (
        P(("dp", "group"), None),
        P(("dp", "group"), None),
        P(("dp", "group")),
        P(("dp", "group")),
        P(("dp", "group")),
        P(("dp", "group")),
        P(("dp", "group")),
        P(("dp", "group")),
    )
    return jax.shard_map(
        on_device,
        mesh=mesh,
        in_specs=placed,
        out_specs=(
            P(("dp", "group"), None),
            P(("dp", "group"), None),
            P(("dp", "group")),
            P(("dp", "group")),
            P(("dp", "group")),
            P(("dp", "group")),
        ),
        check_vma=False,
    )
```

```python
import functools

import jax
import jax.numpy as jnp
import numpy as np
from jax import lax
from jax.experimental import pallas as pl
from jax.experimental.pallas import tpu as pltpu
from jax.sharding import PartitionSpec as P

FF = 3072
HEAD = 64
ROT = 16
STEP = 3


BETA_ONE = 0.9
BETA_TWO = 0.95
LEARN_RATE = 0.01
DECAY_RATE = 0.1
ADAM_EPS = 1e-08
NORM_EPS = 1e-05
SCORE_SCALE = 0.125
MASKED = -1e30
TILE_ROWS = 16
MESH = pl.DeviceIdType.MESH
DMA = pltpu.SemaphoreType.DMA
ANY = pl.BlockSpec(memory_space=pl.ANY)
INVMEM = pl.BlockSpec(memory_space=pltpu.VMEM)


def param_layout(model_width, hidden):
    return [
        ("weight_qkv", (model_width, 3 * model_width)),
        ("bias_qkv", (3 * model_width,)),
        ("weight_out", (model_width, model_width)),
        ("bias_out", (model_width,)),
        ("weight_up", (model_width, hidden)),
        ("bias_up", (hidden,)),
        ("weight_down", (hidden, model_width)),
        ("bias_down", (model_width,)),
        ("gain_attn", (model_width,)),
        ("shift_attn", (model_width,)),
        ("gain_mlp", (model_width,)),
        ("shift_mlp", (model_width,)),
    ]


def unpack_params(flat_params, model_width, hidden):
    result = {}
    offset = 0
    for entry_name, entry_shape in param_layout(model_width, hidden):
        length = 1
        for extent in entry_shape:
            length = length * extent
        result[entry_name] = flat_params[offset : offset + length].reshape(entry_shape)
        offset = offset + length
    return result


def pack_grads(grad_dict, model_width, hidden, total_len):
    pieces = []
    used_count = 0
    for entry_name, entry_shape in param_layout(model_width, hidden):
        flat_grad = grad_dict[entry_name].reshape(-1)
        pieces.append(flat_grad)
        used_count = used_count + flat_grad.shape[0]
    pieces.append(jnp.zeros((total_len - used_count,), jnp.float32))
    return jnp.concatenate(pieces)


def rotary_tables(pos_ids):
    half_rot = ROT // 2
    inverse_freq = 10000.0 ** (-jnp.arange(half_rot, dtype=jnp.float32) * 2.0 / ROT)
    angles = pos_ids.astype(jnp.float32)[:, None] * inverse_freq[None, :]
    return (jnp.cos(angles), jnp.sin(angles))


def rotate(values, cosine, sine_rows):
    half_rot = ROT // 2
    lower_part = values[..., :half_rot]
    upper_part = values[..., half_rot:ROT]
    cos_rows = cosine[:, None, :]
    sin_rows = sine_rows[:, None, :]
    return jnp.concatenate(
        [
            lower_part * cos_rows - upper_part * sin_rows,
            upper_part * cos_rows + lower_part * sin_rows,
            values[..., ROT:],
        ],
        -1,
    )


def rotate_back(values, cosine, sine_rows):
    half_rot = ROT // 2
    lower_part = values[..., :half_rot]
    upper_part = values[..., half_rot:ROT]
    cos_rows = cosine[:, None, :]
    sin_rows = sine_rows[:, None, :]
    return jnp.concatenate(
        [
            lower_part * cos_rows + upper_part * sin_rows,
            upper_part * cos_rows - lower_part * sin_rows,
            values[..., ROT:],
        ],
        -1,
    )


def layer_stats(block_in):
    centred = block_in - jnp.mean(block_in, -1, keepdims=True)
    inv_std = lax.rsqrt(jnp.mean(centred * centred, -1, keepdims=True) + NORM_EPS)
    return (centred * inv_std, inv_std)


def norm_backward(grad_normed, normed, inv_std):
    return inv_std * (
        grad_normed
        - jnp.mean(grad_normed, -1, keepdims=True)
        - normed * jnp.mean(grad_normed * normed, -1, keepdims=True)
    )


def gelu_slope(up_pre):
    return (
        0.5 * (1.0 + lax.erf(up_pre * 0.7071067811865476))
        + up_pre * jnp.exp(-0.5 * up_pre * up_pre) * 0.3989422804014327
    )


def masked_scores(query_part, key_part, query_seg, key_seg, query_slot, key_slot):
    scores = (
        jnp.einsum("qhd,khd->hqk", query_part, key_part, preferred_element_type=jnp.float32)
        * SCORE_SCALE
    )
    allowed = (query_seg[:, None] == key_seg[None, :]) & (key_slot[None, :] <= query_slot[:, None])
    return (jnp.where(allowed[None], scores, MASKED), allowed)


def score_grads(scores, allowed, log_total, row_delta, grad_context, value_part):
    attn_probs = jnp.where(allowed[None], jnp.exp(scores - log_total[..., None]), 0.0)
    grad_probs = jnp.einsum(
        "qhd,khd->hqk", grad_context, value_part, preferred_element_type=jnp.float32
    )
    grad_scores = (attn_probs * (grad_probs - row_delta[..., None]) * SCORE_SCALE).astype(
        jnp.bfloat16
    )
    return (attn_probs.astype(jnp.bfloat16), grad_scores)


def on_device_gathered(tokens, grad_out, segment_ids, positions, counts, master, moment_one, moment_two):
    local_rows = tokens.shape[0]
    model_width = tokens.shape[1]
    head_count = model_width // HEAD
    local_master = master.astype(jnp.bfloat16)
    sectioned = lax.all_gather(local_master.reshape(1, 1, -1), "group", axis=1, tiled=True)
    sectioned = lax.all_gather(sectioned, "dp", axis=0, tiled=True)
    flat_params = sectioned.reshape(-1)
    params = unpack_params(flat_params, model_width, FF)
    block_in = tokens.astype(jnp.float32)
    normed, inv_std = layer_stats(block_in)
    gain_attn = params["gain_attn"].astype(jnp.float32)
    gain_mlp = params["gain_mlp"].astype(jnp.float32)
    attn_in = (normed * gain_attn + params["shift_attn"].astype(jnp.float32)).astype(jnp.bfloat16)
    mlp_in = (normed * gain_mlp + params["shift_mlp"].astype(jnp.float32)).astype(jnp.bfloat16)
    qkv_pre = (
        jnp.dot(attn_in, params["weight_qkv"], preferred_element_type=jnp.float32)
        + params["bias_qkv"].astype(jnp.float32)
    ).reshape(local_rows, 3, head_count, HEAD)
    cosine, sine_rows = rotary_tables(positions)
    queries = rotate(qkv_pre[:, 0], cosine, sine_rows).astype(jnp.bfloat16)
    keys_own = rotate(qkv_pre[:, 1], cosine, sine_rows).astype(jnp.bfloat16)
    values_own = qkv_pre[:, 2].astype(jnp.bfloat16)
    key_vals = jnp.stack(
        [keys_own.reshape(local_rows, model_width), values_own.reshape(local_rows, model_width)], 1
    )
    query_slot = lax.axis_index("group") * local_rows + jnp.arange(local_rows, dtype=jnp.int32)

    def split_keys(piece_kv):
        count_keys = piece_kv.shape[0]
        return (
            piece_kv[:, 0].reshape(count_keys, head_count, HEAD),
            piece_kv[:, 1].reshape(count_keys, head_count, HEAD),
        )

    run_max = jnp.full((head_count, local_rows), MASKED, jnp.float32)
    piece_kv = lax.all_gather(key_vals, "group", axis=0, tiled=True)
    piece_seg = lax.all_gather(segment_ids, "group", axis=0, tiled=True)
    piece_keys, piece_values = split_keys(piece_kv)
    key_slot = jnp.arange(piece_seg.shape[0], dtype=jnp.int32)
    scores, allowed = masked_scores(
        queries, piece_keys, segment_ids, piece_seg, query_slot, key_slot
    )
    new_max = jnp.maximum(run_max, jnp.max(scores, -1))
    weights = jnp.where(allowed[None], jnp.exp(scores - new_max[..., None]), 0.0)
    run_sum = jnp.sum(weights, -1)
    run_acc = jnp.einsum(
        "hqk,khd->hqd",
        weights.astype(jnp.bfloat16),
        piece_values,
        preferred_element_type=jnp.float32,
    )
    run_max, run_sum, run_acc = (new_max, run_sum, run_acc)
    log_total = run_max + jnp.log(run_sum)
    context = jnp.transpose(run_acc / run_sum[..., None], (1, 0, 2)).astype(jnp.bfloat16)
    context_flat = context.reshape(local_rows, model_width)
    attn_out = jnp.dot(
        context_flat, params["weight_out"], preferred_element_type=jnp.float32
    ) + params["bias_out"].astype(jnp.float32)
    up_pre = jnp.dot(mlp_in, params["weight_up"], preferred_element_type=jnp.float32) + params[
        "bias_up"
    ].astype(jnp.float32)
    up_act = jax.nn.gelu(up_pre, approximate=False).astype(jnp.bfloat16)
    mlp_out = jnp.dot(up_act, params["weight_down"], preferred_element_type=jnp.float32) + params[
        "bias_down"
    ].astype(jnp.float32)
    block_out = (block_in + attn_out + mlp_out).astype(jnp.bfloat16)
    valid_rows = (jnp.arange(local_rows) < counts[0]).astype(jnp.float32)
    grad_rows = grad_out.astype(jnp.float32) * valid_rows[:, None]
    grad_low = grad_rows.astype(jnp.bfloat16)
    bias_grad = jnp.sum(grad_rows, 0)
    grad_dict = {}
    grad_dict["weight_down"] = jnp.dot(up_act.T, grad_low, preferred_element_type=jnp.float32)
    grad_dict["bias_down"] = bias_grad
    grad_dict["weight_out"] = jnp.dot(context_flat.T, grad_low, preferred_element_type=jnp.float32)
    grad_dict["bias_out"] = bias_grad
    grad_act = jnp.dot(grad_low, params["weight_down"].T, preferred_element_type=jnp.float32)
    grad_pre = (grad_act * gelu_slope(up_pre)).astype(jnp.bfloat16)
    grad_dict["weight_up"] = jnp.dot(mlp_in.T, grad_pre, preferred_element_type=jnp.float32)
    grad_dict["bias_up"] = jnp.sum(grad_pre.astype(jnp.float32), 0)
    grad_mlp_in = jnp.dot(grad_pre, params["weight_up"].T, preferred_element_type=jnp.float32)
    grad_context = jnp.dot(
        grad_low, params["weight_out"].T, preferred_element_type=jnp.float32
    ).astype(jnp.bfloat16)
    grad_context = grad_context.reshape(local_rows, head_count, HEAD)
    row_delta = jnp.einsum(
        "qhd,qhd->hq", grad_context.astype(jnp.float32), context.astype(jnp.float32)
    )
    piece_kv = lax.all_gather(key_vals, "group", axis=0, tiled=True)
    piece_seg = lax.all_gather(segment_ids, "group", axis=0, tiled=True)
    piece_keys, piece_values = split_keys(piece_kv)
    count_keys = piece_seg.shape[0]
    key_slot = jnp.arange(count_keys, dtype=jnp.int32)
    scores, allowed = masked_scores(
        queries, piece_keys, segment_ids, piece_seg, query_slot, key_slot
    )
    probs_low, grad_scores = score_grads(
        scores, allowed, log_total, row_delta, grad_context, piece_values
    )
    grad_queries = jnp.einsum(
        "hqk,khd->qhd", grad_scores, piece_keys, preferred_element_type=jnp.float32
    )
    part_keys = jnp.einsum("hqk,qhd->khd", grad_scores, queries, preferred_element_type=jnp.float32)
    part_values = jnp.einsum(
        "hqk,qhd->khd", probs_low, grad_context, preferred_element_type=jnp.float32
    )
    addition = jnp.stack(
        [part_keys.reshape(count_keys, model_width), part_values.reshape(count_keys, model_width)],
        1,
    )
    grad_kv = addition
    grad_queries, batch_kv = (grad_queries, grad_kv)
    grad_kv = lax.psum_scatter(
        batch_kv.astype(jnp.bfloat16), "group", scatter_dimension=0, tiled=True
    ).astype(jnp.float32)
    grad_keys = grad_kv[:, 0].reshape(local_rows, head_count, HEAD)
    grad_values = grad_kv[:, 1].reshape(local_rows, head_count, HEAD)
    grad_qkv = (
        jnp.stack(
            [
                rotate_back(grad_queries, cosine, sine_rows),
                rotate_back(grad_keys, cosine, sine_rows),
                grad_values,
            ],
            1,
        )
        .reshape(local_rows, 3 * model_width)
        .astype(jnp.bfloat16)
    )
    grad_dict["weight_qkv"] = jnp.dot(attn_in.T, grad_qkv, preferred_element_type=jnp.float32)
    grad_dict["bias_qkv"] = jnp.sum(grad_qkv.astype(jnp.float32), 0)
    grad_attn_in = jnp.dot(grad_qkv, params["weight_qkv"].T, preferred_element_type=jnp.float32)
    grad_dict["gain_attn"] = jnp.sum(grad_attn_in * normed, 0)
    grad_dict["shift_attn"] = jnp.sum(grad_attn_in, 0)
    grad_dict["gain_mlp"] = jnp.sum(grad_mlp_in * normed, 0)
    grad_dict["shift_mlp"] = jnp.sum(grad_mlp_in, 0)
    grad_normed = grad_attn_in * gain_attn + grad_mlp_in * gain_mlp
    grad_in = (grad_rows + norm_backward(grad_normed, normed, inv_std)).astype(jnp.bfloat16)
    dp_count = lax.axis_size("dp")
    group_count = lax.axis_size("group")
    partial_value = pack_grads(grad_dict, model_width, FF, master.shape[0] * dp_count * group_count)
    sectioned_grad = lax.psum_scatter(
        partial_value.reshape(dp_count, group_count, -1).astype(jnp.bfloat16),
        "group",
        scatter_dimension=1,
        tiled=True,
    )
    grad_shard = (
        lax.psum_scatter(sectioned_grad, "dp", scatter_dimension=0, tiled=True)
        .astype(jnp.float32)
        .reshape(-1)
    )
    square_sum = lax.psum(jnp.sum(grad_shard * grad_shard), ("dp", "group"))
    grad_scale = 1.0 / (jnp.sqrt(square_sum) + 1e-06)
    scaled = grad_shard * grad_scale
    new_one = BETA_ONE * moment_one + (1.0 - BETA_ONE) * scaled
    new_two = BETA_TWO * moment_two + (1.0 - BETA_TWO) * scaled * scaled
    correct_one = 1.0 - BETA_ONE**STEP
    correct_two = 1.0 - BETA_TWO**STEP
    new_master = master - LEARN_RATE * (
        new_one / correct_one / (jnp.sqrt(new_two / correct_two) + ADAM_EPS) + DECAY_RATE * master
    )
    return (block_out, grad_in, grad_shard, new_master, new_one, new_two)


def padded(count, step):
    return -(-count // step) * step


@functools.lru_cache(None)
def row_plan(width, hidden, dp_count, group_count, shard_len):
    half = width // 2
    row = width * group_count
    devices = dp_count * group_count
    if hidden != row or (width // HEAD) % group_count or shard_len % half or width % 128:
        return None
    base = [i * shard_len // row for i in range(devices)]
    shift = [i * shard_len % row // half for i in range(devices)]
    span = max(-(-(s * half + shard_len) // row) for s in shift)
    stride = shard_len // row
    starts, at = {}, 0
    for entry_name, entry_shape in param_layout(width, hidden):
        starts[entry_name] = at // width
        at += int(np.prod(entry_shape))
    piece_base = [d * group_count * shard_len // row for d in range(dp_count)]
    spans = all(
        base[i] == piece_base[i // group_count] + stride * (i % group_count) for i in range(devices)
    )
    aligned = (
        starts["weight_up"] % group_count == 0
        and starts["weight_down"] % group_count == 0
        and starts["bias_qkv"] % group_count == 0
        and (starts["weight_out"] + 1) % group_count == 0
        and span == stride + 1
        and spans
        and base == [stride * i + i // (2 * group_count) for i in range(devices)]
        and shift == [i % (2 * group_count) for i in range(devices)]
    )
    if not aligned:
        return None
    row_out = starts["bias_qkv"] // group_count
    return dict(
        base=base,
        shift=shift,
        span=span,
        stride=stride,
        starts=starts,
        piece_base=piece_base,
        row_out=row_out,
        row_up=starts["weight_up"] // group_count,
        row_down=starts["weight_down"] // group_count,
        out_chunk=max(i for i in range(devices) if base[i] <= row_out),
        send_rows=padded(span + 7, TILE_ROWS),
        over=[i for i in range(devices - 1) if base[i + 1] == base[i] + stride],
        period=2 * group_count,
    )


def chunk_place(plan, me):
    period = plan["period"]
    return plan["stride"] * me + me // period, lax.rem(me, period)


def flip(value, bit):
    return value + bit - 2 * bit * ((value // bit) % 2)


def remote(src, dst, send_sem, recv_sem, device):
    return pltpu.make_async_remote_copy(
        src_ref=src,
        dst_ref=dst,
        send_sem=send_sem,
        recv_sem=recv_sem,
        device_id=device,
        device_id_type=MESH,
    )


def greet(devices):
    barrier = pltpu.get_barrier_semaphore()
    for device in devices:
        pl.semaphore_signal(barrier, inc=1, device_id=device, device_id_type=MESH)
    pl.semaphore_wait(barrier, len(devices))


def places(group_count):
    d, z = lax.axis_index("dp"), lax.axis_index("group")
    to = [lax.rem(z + k, group_count) for k in range(group_count)]
    frm = [lax.rem(z - k + group_count, group_count) for k in range(group_count)]
    return d, z, to, frm


def layer_kernel(
    plan, dp_count, group_count, flat, turn_in, unperm, tok, grd, seg, pos, used, grad, block_out, grad_in,
    square_sum, swap_a, swap_b, rs, rr, ls, lr, pad, send, stage, near, obuf, whole, toks, grds, idss, outs, w32, gm32, w_up, w_down,
    w_qkv, w_out, normed, attn_in, mlp_in, slope, act, g_pre, g_low, acc, g_mlp, tabs, qm, km,
    vm, gm, k_all, v_all, ctx, gq, gk, gv, g_qkv, rel_a, rel_b, parts_a, parts_b, gout, held,
    from_core, from_first, from_last, total, gbuf, slabs, back, sq, sqz, sqd, loc, p1s, p1r,
    cs, cr, xs, xr, ys, yr, ts, tr, os, orr, fcs, fcr, fxs, fxr, fys, fyr, zs, zr, gs, gr, bs,
    br, qs, qr, ds, dr,
):
    d, z, to, frm = places(group_count)
    n = group_count
    dc, dx, dy = flip(d, 1), flip(d, 2), flip(d, 4)
    dxy = flip(dx, 4)
    m = dp_count
    turn_to = [lax.rem(d + k, m) for k in range(m)]
    turn_from = [lax.rem(d - k + m, m) for k in range(m)]
    greet([(d, to[k]) for k in range(1, n)] + [(turn_to[k], z) for k in range(1, m)])
    later = []

    def share(j, ref):
        for k in range(1, n):
            copy = remote(ref.at[z], ref.at[z], ts.at[j, k], tr.at[j, k], (d, to[k]))
            copy.start()
            other = remote(ref.at[z], ref.at[frm[k]], ts.at[j, k], tr.at[j, k], (d, to[k]))
            later.append((copy, other))

    def settle():
        for copy, other in later:
            other.wait_recv()
            copy.wait_send()
        later.clear()

    def hop_start(j, ref, s):
        @pl.when((z < n - 1) & (z - s + 1 >= 0))
        def _():
            block = ref.at[z - s + 1]
            remote(block, block, rs.at[j, s], rr.at[j, s], (d, z + 1)).start()

        @pl.when((z > 0) & (z + s - 1 <= n - 1))
        def _():
            block = ref.at[z + s - 1]
            remote(block, block, ls.at[j, s], lr.at[j, s], (d, z - 1)).start()

    def hop_arrived(j, ref, s):
        @pl.when(z - s >= 0)
        def _():
            block = ref.at[z - s]
            remote(block, block, rs.at[j, s], rr.at[j, s], (d, z - 1)).wait_recv()

        @pl.when(z + s <= n - 1)
        def _():
            block = ref.at[z + s]
            remote(block, block, ls.at[j, s], lr.at[j, s], (d, z + 1)).wait_recv()

    def hop_sent(j, ref, s):
        @pl.when((z < n - 1) & (z - s + 1 >= 0))
        def _():
            block = ref.at[z - s + 1]
            remote(block, block, rs.at[j, s], rr.at[j, s], (d, z + 1)).wait_send()

        @pl.when((z > 0) & (z + s - 1 <= n - 1))
        def _():
            block = ref.at[z + s - 1]
            remote(block, block, ls.at[j, s], lr.at[j, s], (d, z - 1)).wait_send()

    def hop_on(j, ref, s):
        hop_arrived(j, ref, s)
        if s < n - 1:
            hop_start(j, ref, s + 1)

    toks[z] = tok[...]
    idss[z] = jnp.concatenate(
        [seg[...], pos[...], jnp.zeros((6, seg.shape[1]), jnp.int32)], 0
    )
    hop_start(0, toks, 1)
    share(0, idss)
    slot = lax.broadcasted_iota(jnp.int32, (tok.shape[0], 1), 0)
    grds[z] = jnp.where(slot < used[0], grd[...].astype(jnp.float32), 0.0).astype(jnp.bfloat16)
    span, stride = plan["span"], plan["stride"]
    send_rows, width = send.shape[1:]
    unit = width // n
    tiles = width // 128
    group = tiles * n
    length = flat.shape[0]
    me = d * n + z
    base, shift = chunk_place(plan, me)
    pad[0:group] = jnp.zeros((group, 128), jnp.float32)
    pad[group : group + length] = flat[...]
    rest = pad.shape[0] - group - length
    pad[group + length :] = jnp.zeros((rest, 128), jnp.float32)
    row = base + lax.broadcasted_iota(jnp.int32, (send_rows, 1), 0)
    whole_lines = ((row >= plan["row_out"]) & (row < plan["row_up"])) | (row >= plan["row_down"])
    up_rows = (row >= plan["row_up"]) & (row < plan["row_down"])
    first_row = group - tiles // 2 * shift
    for b in range(n):
        stage[b] = jnp.concatenate(
            [
                pad[pl.ds(first_row + tiles * b + t, send_rows, stride=group), :]
                for t in range(tiles)
            ],
            1,
        )
    for b in range(n):
        line = stage[b]
        turned = jnp.dot(
            line.astype(jnp.bfloat16), turn_in[...], preferred_element_type=jnp.float32
        )
        near[b] = jnp.where(up_rows, turned, line)
    extra = jnp.concatenate(
        [stage[j % n, stride - 1 + j // n : stride + j // n, :] for j in range(send_rows - span)], 0
    )
    for g in range(n):
        by_column = jnp.concatenate([near[b][:, g * unit : (g + 1) * unit] for b in range(n)], 1)
        value = jnp.where(whole_lines, stage[g], by_column)
        value = jnp.concatenate([value[:stride], jnp.concatenate([value[stride:span], extra], 0)], 0)
        send[g] = value.astype(jnp.bfloat16)
    first = []
    for k in range(1, n):
        copy = remote(send.at[to[k]], whole.at[d, z], p1s.at[k], p1r.at[k], (d, to[k]))
        copy.start()
        first.append(copy)
    whole[d, z] = send[z]
    sent = []

    def push(ref, s, r, device):
        copy = remote(ref, ref, s, r, device)
        copy.start()
        sent.append(copy)

    def arrived(ref, s, r, device):
        remote(ref, ref, s, r, device).wait_recv()

    for k in range(n):
        ref = whole.at[d, frm[k]]
        if k > 0:
            arrived(ref, p1s.at[k], p1r.at[k], (d, to[k]))
        push(ref, xs.at[k], xr.at[k], (dx, z))
        push(ref, ys.at[k], yr.at[k], (dy, z))
        push(ref, cs.at[k], cr.at[k], (dc, z))
    settle()
    hop_on(0, toks, 1)
    hop_start(1, grds, 1)
    for k in range(n):
        by_x, by_y = whole.at[dx, frm[k]], whole.at[dy, frm[k]]
        arrived(by_x, xs.at[k], xr.at[k], (dx, z))
        if k < n // 2:
            push(by_x, ys.at[n + k], yr.at[n + k], (dy, z))
        push(by_x, cs.at[n + k], cr.at[n + k], (dc, z))
        arrived(by_y, ys.at[k], yr.at[k], (dy, z))
        if k >= n // 2:
            push(by_y, xs.at[n + k], xr.at[n + k], (dx, z))
        push(by_y, cs.at[2 * n + k], cr.at[2 * n + k], (dc, z))
    hop_on(0, toks, 2)
    hop_on(1, grds, 1)
    for k in range(n):
        across = whole.at[dxy, frm[k]]
        if k < n // 2:
            arrived(across, ys.at[n + k], yr.at[n + k], (dy, z))
        else:
            arrived(across, xs.at[n + k], xr.at[n + k], (dx, z))
        push(across, cs.at[3 * n + k], cr.at[3 * n + k], (dc, z))
    for j, owner in enumerate((d, dx, dy, dxy)):
        for k in range(n):
            ref = whole.at[flip(owner, 1), frm[k]]
            arrived(ref, cs.at[j * n + k], cr.at[j * n + k], (dc, z))
    hop_on(1, grds, 2)
    for copy in first + sent:
        copy.wait_send()
    chunks = [plan["out_chunk"] + j for j in range(4)]
    chunks = [whole[i // n, i % n].astype(jnp.float32) for i in chunks]
    block = unit // n
    lines = []
    for j in range(1, 4):
        count = min(stride, unit - stride * (j - 1))
        part = chunks[j][:count]
        if j > 1:
            head = chunks[j - 1][stride : stride + 8]
            row8 = lax.broadcasted_iota(jnp.int32, (8, 1), 0)
            part = jnp.concatenate([part[:8] + jnp.where(row8 == 0, head, 0.0), part[8:]], 0)
        lines.append(part)
    lines = jnp.concatenate(lines, 0)
    before = chunks[0][stride : stride + 1]
    moved = pltpu.roll(lines, 1, 0)
    at = lax.broadcasted_iota(jnp.int32, (unit, 1), 0)
    moved = jnp.where(at == 0, before, moved)
    lines = jnp.where(z == n - 1, moved, lines).astype(jnp.bfloat16)
    for g in range(n):
        obuf[g] = lines[g * block : (g + 1) * block]
    outs[z] = obuf[z]
    outs_moving = []
    for k in range(1, n):
        copy = remote(obuf.at[to[k]], outs.at[z], os.at[k], orr.at[k], (d, to[k]))
        copy.start()
        outs_moving.append(
            (copy, remote(obuf.at[to[k]], outs.at[frm[k]], os.at[k], orr.at[k], (d, to[k])))
        )
    f32, bf16 = jnp.float32, jnp.bfloat16
    rows = normed.shape[0]
    local = rows // n
    wide = 256
    heads = unit // HEAD
    bases = plan["base"]
    row_out, row_up, row_down, over = plan["row_out"], plan["row_up"], plan["row_down"], plan["over"]

    def mm(lhs, rhs):
        return jnp.dot(lhs, rhs, preferred_element_type=f32)

    def mm_t(lhs, rhs):
        return lax.dot_general(lhs, rhs, (((1,), (1,)), ((), ())), preferred_element_type=f32)

    def t_mm(lhs, rhs):
        return lax.dot_general(lhs, rhs, (((0,), (0,)), ((), ())), preferred_element_type=f32)

    def chunk(i):
        return whole[i // n, i % n].astype(f32)

    def fill(low, high):
        for i, first in enumerate(bases):
            last = first + (stride if i in over else span)
            lo, hi = max(low, first), min(high, last)
            if lo >= hi:
                continue
            w32[lo - low : hi - low] = chunk(i)[lo - first : hi - first]
            if lo == first and i - 1 in over:
                tail = whole[(i - 1) // n, (i - 1) % n, stride : stride + 8].astype(f32)[:1]
                w32[lo - low : lo - low + 1] = w32[lo - low : lo - low + 1] + tail

    def line(row):
        i = max(i for i in range(len(bases)) if bases[i] <= row)
        return chunk(i)[row - bases[i] : row - bases[i] + 1]

    fill(row_up, row_up + width)
    w_up[...] = w32[:width].astype(bf16)
    fill(row_down, row_down + width)
    w_down[...] = w32[:width].astype(bf16)
    fill(0, row_out)
    third = width // n
    gap = jnp.zeros((third, wide - unit), f32)
    for t in range(tiles):
        rel_a[t, :row_out] = w32[:row_out, t * 128 : (t + 1) * 128]

    def strided_rows(ref, start, step):
        return jnp.concatenate(
            [ref[t, pl.ds(start, third, stride=step), :] for t in range(tiles)], 1
        )

    def put_rows(ref, start, step, value):
        for t in range(tiles):
            ref[t, pl.ds(start, third, stride=step), :] = value[:, t * 128 : (t + 1) * 128]

    planes = [strided_rows(rel_a, p, 3) for p in range(3)]
    for t in range(n):
        blocks = []
        for j in range(3):
            p, b = (3 * t + j) // n, (3 * t + j) % n
            blocks += [planes[p][:, b * unit : (b + 1) * unit], gap]
        put_rows(rel_b, t, n, jnp.concatenate(blocks, 1))
    for t in range(tiles):
        w_qkv[:, t * 128 : (t + 1) * 128] = rel_b[t].astype(bf16)
    bias_up = line(row_up + width)
    vectors = chunk(len(bases) - 1)[span : span + n + 1]
    bias_down, gain_attn, shift_attn, gain_mlp, shift_mlp = (vectors[j : j + 1] for j in range(5))
    is_last = z == n - 1
    bias_rest = jnp.where(is_last, bias_down + line(row_up - 1), 0.0)
    bias_lines = chunk(plan["out_chunk"])[span + n : span + n + 3]
    bias_qkv = []
    for j in range(3):
        mine = jnp.zeros((1, unit), f32)
        for g in range(n):
            mine = jnp.where(z == g, bias_lines[j : j + 1, g * unit : (g + 1) * unit], mine)
        bias_qkv += [mine, jnp.zeros((1, wide - unit), f32)]
    bias_qkv = jnp.concatenate(bias_qkv, 1)

    step = 64
    hop_on(0, toks, 3)

    @pl.loop(0, rows // step)
    def _(i):
        at = pl.ds(i * step, step)
        x = toks[i // (local // step), pl.ds(i % (local // step) * step, step), :].astype(f32)
        centred = x - jnp.mean(x, -1, keepdims=True)
        inv = lax.rsqrt(jnp.mean(centred * centred, -1, keepdims=True) + NORM_EPS)
        value = centred * inv
        normed[at, :] = value
        attn_in[at, :] = (value * gain_attn + shift_attn).astype(bf16)
        mlp_in[at, :] = (value * gain_mlp + shift_mlp).astype(bf16)

    w32[0:8] = jnp.broadcast_to(bias_up, (8, width))
    w32[8:16] = jnp.broadcast_to(bias_qkv, (8, width))

    @pl.loop(0, width // wide)
    def _(i):
        at = pl.ds(pl.multiple_of(i * wide, wide), wide)
        up = mm(mlp_in[...], w_up[:, at]) + w32[0:1, at]
        half = 0.5 * (1.0 + lax.erf(up * 0.7071067811865476))
        act[:, at] = (up * half).astype(bf16)
        slope[:, at] = half + up * jnp.exp(-0.5 * up * up) * 0.3989422804014327

    @pl.loop(0, width // wide)
    def _(i):
        at = pl.ds(pl.multiple_of(i * wide, wide), wide)
        acc[:, at] = mm(act[...], w_down[:, at])

    position = jnp.concatenate([idss[g, 1:2, :] for g in range(n)], 1).astype(f32)
    half_rot = ROT // 2
    at_freq = lax.broadcasted_iota(jnp.int32, (half_rot, 1), 0)
    freq = jnp.zeros((half_rot, 1), f32)
    for i in range(half_rot):
        freq = jnp.where(at_freq == i, float(10000.0 ** (-2.0 * i / ROT)), freq)
    angles = freq * position
    lane = lax.broadcasted_iota(jnp.int32, (half_rot, wide), 1) % HEAD
    same = lane % half_rot == lax.broadcasted_iota(jnp.int32, (half_rot, wide), 0)
    hot = [same & (lane < ROT), same & (lane < half_rot), same & (lane >= half_rot) & (lane < ROT)]

    def expand(table, where):
        return lax.dot_general(
            table,
            where.astype(f32),
            (((0,), (0,)), ((), ())),
            precision=lax.Precision.HIGHEST,
            preferred_element_type=f32,
        )

    cosine, sine = jnp.cos(angles), jnp.sin(angles)
    lane_wide = lax.broadcasted_iota(jnp.int32, (1, wide), 1)
    head_lane = lane_wide % HEAD
    tabs[0] = expand(cosine, hot[0]) + jnp.where(head_lane >= ROT, 1.0, 0.0)
    tabs[1] = expand(sine, hot[1])
    tabs[2] = expand(sine, hot[2])

    def turn(value, at, sign):
        ahead = pltpu.roll(value, wide - half_rot, 1)
        behind = pltpu.roll(value, half_rot, 1)
        return value * tabs[0, at] + sign * (behind * tabs[2, at] - ahead * tabs[1, at])

    def masked(ref, value):
        for h in range(heads):
            ref[h] = jnp.where(lane_wide // HEAD == h, value, 0.0).astype(bf16)

    every = slice(0, rows)
    q32 = turn(mm(attn_in[...], w_qkv[:, :wide]) + w32[8:9, :wide], every, 1.0)
    masked(qm, q32)
    k32 = turn(mm(attn_in[...], w_qkv[:, wide : 2 * wide]) + w32[8:9, wide : 2 * wide], every, 1.0)
    masked(km, k32)
    k_all[...] = k32.astype(bf16)
    v32 = mm(attn_in[...], w_qkv[:, 2 * wide :]) + w32[8:9, 2 * wide :]
    masked(vm, v32)
    v_all[...] = v32.astype(bf16)
    for copy, other in outs_moving:
        other.wait_recv()
        copy.wait_send()
    order = [(t - 1) % n for t in range(n)]
    out_rows = jnp.concatenate([outs[j] for j in order], 0)
    w_out[...] = mm(unperm[...], out_rows).astype(bf16)
    hop_on(1, grds, 3)
    for g in range(n):
        g_low[g * local : (g + 1) * local] = grds[g]
    masked(gm, mm_t(g_low[...], w_out[...]).astype(bf16).astype(f32))

    @pl.loop(0, width // wide)
    def _(i):
        at = pl.ds(pl.multiple_of(i * wide, wide), wide)
        g_pre[:, at] = (mm_t(g_low[...], w_down[at, :]) * slope[:, at]).astype(bf16)

    @pl.loop(0, width // wide)
    def _(i):
        at = pl.ds(pl.multiple_of(i * wide, wide), wide)
        g_mlp[:, at] = mm_t(g_pre[...], w_up[at, :])

    bias_grad = jnp.where(is_last, jnp.sum(g_low[...].astype(f32), 0, keepdims=True), 0.0)

    def swap_start(j, src, dst, b):
        @pl.when(z != b)
        def _():
            remote(src.at[b], dst.at[z], zs.at[j, b], zr.at[j, z], (d, b)).start()

        @pl.when(z == b)
        def _():
            dst[b] = src[b]

    def swap_end(j, src, dst):
        for b in range(n):
            @pl.when(z != b)
            def _():
                remote(src.at[b], dst.at[b], zs.at[j, b], zr.at[j, b], (d, b)).wait_recv()
                remote(src.at[b], dst.at[b], zs.at[j, b], zr.at[j, b], (d, b)).wait_send()

    seg_row = jnp.concatenate([idss[g, 0:1, :] for g in range(n)], 1).astype(f32)
    seg_col = jnp.transpose(jnp.broadcast_to(seg_row, (128, rows)))[:, 0:1]
    ctx[...] = jnp.zeros_like(ctx)
    gq[...] = jnp.zeros_like(gq)
    gk[...] = jnp.zeros_like(gk)
    gv[...] = jnp.zeros_like(gv)
    vecs = [[], [], [], []]
    ends_first = [b for pair in zip(range(n // 2), reversed(range(n))) for b in pair]
    for b in ends_first:
        at = slice(b * local, (b + 1) * local)
        upto = (b + 1) * local
        seen = slice(0, upto)
        earlier = lax.broadcasted_iota(jnp.int32, (local, upto), 1) <= b * local + (
            lax.broadcasted_iota(jnp.int32, (local, upto), 0)
        )
        allowed = (seg_col[at] == seg_row[:, seen]) & earlier

        @pl.loop(0, heads)
        def _(h):
            scores = jnp.where(allowed, mm_t(qm[h, at], k_all[seen]) * SCORE_SCALE, MASKED)
            top = jnp.max(scores, -1, keepdims=True)
            weights = jnp.exp(scores - top)
            probs = weights / jnp.sum(weights, -1, keepdims=True)
            low = probs.astype(bf16)
            context = mm(low, vm[h, seen])
            ctx[at] += context
            kept = context.astype(bf16).astype(f32)
            delta = jnp.sum(gm[h, at].astype(f32) * kept, -1, keepdims=True)
            slanted = (probs * (mm_t(gm[h, at], v_all[seen]) - delta) * SCORE_SCALE).astype(bf16)
            gq[at] += mm(slanted, km[h, seen])
            gk[seen] += t_mm(slanted, qm[h, at])
            gv[seen] += t_mm(low, gm[h, at])

        parts_a[b] = (acc[at] + mm(ctx[at].astype(bf16), w_out[...]) + bias_rest).astype(bf16)
        swap_start(0, parts_a, swap_a, b)

    ctx_low = ctx[...].astype(bf16)
    g_qkv[:, :wide] = turn(gq[...], every, -1.0).astype(bf16)
    g_qkv[:, wide : 2 * wide] = turn(gk[...], every, -1.0).astype(bf16)
    g_qkv[:, 2 * wide :] = gv[...].astype(bf16)
    for i in range(width // wide):
        at = slice(i * wide, (i + 1) * wide)
        g_attn = mm_t(g_qkv[...], w_qkv[at, :])
        g_up = g_mlp[:, at]
        value = (g_attn * gain_attn[:, at] + g_up * gain_mlp[:, at]).astype(bf16)
        for g in range(n):
            parts_b[g, :, at] = value[g * local : (g + 1) * local]
        here = normed[:, at]
        for j, term in enumerate((g_attn * here, g_attn, g_up * here, g_up)):
            vecs[j].append(jnp.sum(term, 0, keepdims=True))
    out_grad = t_mm(ctx_low, g_low[...]).astype(bf16)
    out_grad = t_mm(unperm[...], out_grad).astype(bf16)
    for g in range(n):
        t = (g + 1) % n
        gout[g] = out_grad[t * block : (t + 1) * block]
    gbuf[z] = gout[z]
    trades = []
    for k in range(1, n):
        copy = remote(gout.at[to[k]], gbuf.at[z], gs.at[k], gr.at[k], (d, to[k]))
        copy.start()
        trades.append((copy, remote(gout.at[to[k]], gbuf.at[frm[k]], gs.at[k], gr.at[k], (d, to[k]))))
    for b in range(n):
        swap_start(1, parts_b, swap_b, b)
    for i in range(width // wide):
        at = slice(i * wide, (i + 1) * wide)
        gm32[row_up + i * wide : row_up + (i + 1) * wide] = t_mm(mlp_in[:, at], g_pre[...])
        gm32[row_down + i * wide : row_down + (i + 1) * wide] = t_mm(act[:, at], g_low[...])
    gm32[row_up + width : row_up + width + 1] = jnp.sum(g_pre[...].astype(f32), 0, keepdims=True)
    for i in range(width // wide):
        at = slice(i * wide, (i + 1) * wide)
        value = t_mm(attn_in[:, at], g_qkv[...])
        for t in range(tiles):
            rel_b[t, at] = value[:, t * 128 : (t + 1) * 128]
    columns = [strided_rows(rel_b, t, n) for t in range(n)]
    for p in range(3):
        blocks = []
        for b in range(n):
            t, j = (n * p + b) // 3, (n * p + b) % 3
            blocks.append(columns[t][:, j * wide : j * wide + unit])
        put_rows(rel_a, p, 3, jnp.concatenate(blocks, 1))
    for t in range(tiles):
        gm32[:row_out, t * 128 : (t + 1) * 128] = rel_a[t, :row_out]
    gm32[row_out:row_up] = jnp.zeros((row_up - row_out, width), f32)
    gm32[row_up - 1 : row_up] = bias_grad
    row_end = row_down + width
    gm32[row_end:] = jnp.zeros((gm32.shape[0] - row_end, width), f32)
    sums = jnp.sum(g_qkv[...].astype(f32), 0, keepdims=True)
    sums = jnp.concatenate(
        [sums[:, j * wide : j * wide + unit] for j in range(3)] + [jnp.zeros((1, unit), f32)], 1
    )
    extra = [bias_grad] + [jnp.concatenate(v, 1) for v in vecs] + [sums, jnp.zeros((2, width), f32)]
    body = n * stride
    for e, first in enumerate(plan["piece_base"]):
        held[e, :body] = gm32[first : first + body].astype(bf16)
        last = [gm32[first + body : first + body + 1], jnp.zeros((7, width), f32)] + extra
        held[e, body:] = jnp.concatenate(last, 0).astype(bf16)
    y, x, c = d // 4, lax.rem(d // 2, 2), lax.rem(d, 2)
    rows = total.shape[0]
    cut = padded(rows // 2, TILE_ROWS)
    for copy, other in trades:
        other.wait_recv()
    out_rows = jnp.concatenate([gbuf[g].astype(f32) for g in range(n)], 0)
    at = lax.broadcasted_iota(jnp.int32, (unit, 1), 0)
    moved = jnp.where(at == unit - 1, 0.0, pltpu.roll(out_rows, unit - 1, 0))
    is_last = z == n - 1
    after = plan["out_chunk"] // n + 1
    held[after, :unit] = (
        held[after, :unit].astype(f32) + jnp.where(is_last, moved, out_rows)
    ).astype(bf16)
    at = lax.broadcasted_iota(jnp.int32, (TILE_ROWS, 1), 0)
    first_line = jnp.where((at == 0) & is_last, out_rows[:1], 0.0)
    held[after - 1, body:] = (held[after - 1, body:].astype(f32) + first_line).astype(bf16)

    low, high = pl.ds(0, cut), pl.ds(cut, rows - cut)
    here = 2 * y + x
    quads = [flip(flip(here, 1), 2), flip(here, 1), flip(here, 2), here]
    mine = [held.at[2 * q + c] for q in quads]
    cross = []
    for k in range(4):
        copy = remote(
            held.at[2 * quads[k] + 1 - c], from_core.at[k], fcs.at[k], fcr.at[k], (dc, z)
        )
        copy.start()
        cross.append(copy)

    def add(dst, src):
        dst[...] = (dst[...].astype(f32) + src[...].astype(f32)).astype(dst.dtype)

    sent = []

    def pass_on(src, dst, s, r, device):
        copy = remote(src, dst, s, r, device)
        copy.start()
        sent.append(copy)
        return copy

    by_x, by_y = (dx, z), (dy, z)
    for k in range(4):
        cross[k].wait_recv()
        add(mine[k], from_core.at[k])
        if k == 0:
            x0 = pass_on(mine[0].at[low], from_first.at[0, low], fxs.at[0], fxr.at[0], by_x)
            y0 = pass_on(mine[0].at[high], from_first.at[0, high], fys.at[0], fyr.at[0], by_y)
        elif k == 1:
            x1 = pass_on(mine[1].at[low], from_first.at[1, low], fxs.at[1], fxr.at[1], by_x)
        elif k == 2:
            y1 = pass_on(mine[2].at[high], from_first.at[1, high], fys.at[1], fyr.at[1], by_y)
    x0.wait_recv()
    add(mine[2].at[low], from_first.at[0, low])
    y2 = pass_on(mine[2].at[low], from_last.at[low], fys.at[2], fyr.at[2], by_y)
    y0.wait_recv()
    add(mine[1].at[high], from_first.at[0, high])
    x2 = pass_on(mine[1].at[high], from_last.at[high], fxs.at[2], fxr.at[2], by_x)
    x1.wait_recv()
    add(mine[3].at[low], from_first.at[1, low])
    y1.wait_recv()
    add(mine[3].at[high], from_first.at[1, high])
    y2.wait_recv()
    x2.wait_recv()
    total[...] = (mine[3][...].astype(f32) + from_last[...].astype(f32)).astype(bf16).astype(f32)

    odd = lax.rem(d, 2)
    at = lax.broadcasted_iota(jnp.int32, (rows, 1), 0)
    counted = jnp.where((at >= odd) & (at < body + 1), total[...], 0.0)
    sq[z] = jnp.full(sq.shape[1:], jnp.sum(counted * counted), f32)
    for k in range(1, n):
        copy = remote(sq.at[z], sq.at[z], qs.at[k], qr.at[k], (d, to[k]))
        copy.start()
        sent.append(copy)
    extra = total[body + 8 : body + 14]
    for j in range(n):
        slab = jnp.concatenate(
            [
                total[stride * j : stride * j + stride],
                jnp.concatenate(
                    [total[stride * j + stride : stride * j + span], extra, jnp.zeros((1, width), f32)], 0
                ),
            ],
            0,
        )
        slabs[j] = slab.astype(bf16)
    far = []
    for k in range(1, n):
        copy = remote(slabs.at[to[k]], back.at[z], bs.at[k], br.at[k], (d, to[k]))
        copy.start()
        far.append((copy, remote(slabs.at[to[k]], back.at[frm[k]], bs.at[k], br.at[k], (d, to[k]))))
    back[z] = slabs[z]
    for k in range(1, n):
        remote(sq.at[z], sq.at[frm[k]], qs.at[k], qr.at[k], (d, to[k])).wait_recv()
    sqz[...] = sq[0] + sq[1] + sq[2] + sq[3]
    sqd[d] = sqz[...]
    for k in range(1, m):
        copy = remote(sqz, sqd.at[d], ds.at[k], dr.at[k], (turn_to[k], z))
        copy.start()
        sent.append(copy)
    swap_end(0, parts_a, swap_a)
    swap_end(1, parts_b, swap_b)
    x = toks[z].astype(f32)
    value = x
    for g in range(n):
        value = value + swap_a[g].astype(f32)
    block_out[...] = value.astype(bf16)
    centred = x - jnp.mean(x, -1, keepdims=True)
    inv = lax.rsqrt(jnp.mean(centred * centred, -1, keepdims=True) + NORM_EPS)
    own_normed = centred * inv
    value = swap_b[0].astype(f32)
    for g in range(1, n):
        value = value + swap_b[g].astype(f32)
    value = norm_backward(value, own_normed, inv)
    grad_in[...] = (grds[z].astype(f32) + value).astype(bf16)
    for copy, other in far:
        other.wait_recv()

    for g in range(n):
        stage[g] = back[g].astype(f32)
    vec = stage[0, stride : stride + 8]
    for g in range(1, n):
        vec = vec + stage[g, stride : stride + 8]
    vec = vec[1:6]
    bias_rows = [stage[g, span + 5 : span + 6] for g in range(n)]
    squares = jnp.sum(vec * vec)
    for g in range(n):
        squares = squares + jnp.sum(bias_rows[g] * bias_rows[g])
    row_end = plan["row_down"] + width
    for b in range(n):
        part = slice(b * unit, (b + 1) * unit)
        by_column = jnp.concatenate([stage[g, :, part] for g in range(n)], 1)
        unturned = lax.dot_general(
            by_column.astype(bf16), turn_in[...], (((1,), (1,)), ((), ())), preferred_element_type=f32
        )
        value = jnp.where(up_rows, unturned, by_column)
        value = jnp.where(whole_lines, stage[b], value)
        if b < 3:
            bias_line = jnp.concatenate([bias_rows[g][:, part] for g in range(n)], 1)
            value = jnp.where(row == plan["row_out"], bias_line, value)
        value = jnp.where(row == row_end, vec[b : b + 1], value)
        if b == 0:
            value = jnp.where(row == row_end + 1, vec[n : n + 1], value)
        for t in range(tiles):
            pad[pl.ds(first_row + tiles * b + t, send_rows, stride=group), :] = value[
                :, t * 128 : (t + 1) * 128
            ]
    grad[...] = pad[group : group + grad.shape[0]]
    for k in range(1, m):
        remote(sqz, sqd.at[turn_from[k]], ds.at[k], dr.at[k], (turn_to[k], z)).wait_recv()
    result = sqd[0]
    for k in range(1, m):
        result = result + sqd[k]
    square_sum[...] = result + squares
    for copy in cross + sent:
        copy.wait_send()
    hop_tensors = ((0, toks), (1, grds))
    for j, ref in hop_tensors:
        for k in range(1, n):
            hop_sent(j, ref, k)
    for copy, other in trades + far:
        copy.wait_send()


def layer_call(plan, dp_count, group_count, flat, turn_in, unperm, tok, grd, seg, pos, used):
    n, m = group_count, dp_count
    local, width = tok.shape
    rows = local * n
    f32, bf16 = jnp.float32, jnp.bfloat16
    wide, heads = 256, width // n // HEAD
    block = width // n // n
    send_rows = plan["send_rows"]
    group = width // 128 * n
    pad_rows = padded(2 * group + group * send_rows, 8)
    row_end = plan["row_down"] + width
    piece = n * plan["stride"] + TILE_ROWS

    def fl(*shape):
        return pltpu.VMEM(shape, f32)

    def bf(*shape):
        return pltpu.VMEM(shape, bf16)

    return pl.pallas_call(
        functools.partial(layer_kernel, plan, m, n),
        out_shape=[
            jax.ShapeDtypeStruct(flat.shape, f32),
            jax.ShapeDtypeStruct((local, width), bf16),
            jax.ShapeDtypeStruct((local, width), bf16),
            jax.ShapeDtypeStruct((8, 128), f32),
        ],
        in_specs=[INVMEM] * 7 + [pl.BlockSpec(memory_space=pltpu.SMEM)],
        out_specs=[INVMEM] * 4,
        scratch_shapes=[
            bf(n, local, width),
            bf(n, local, width),
            DMA((2, n)), DMA((2, n)), DMA((2, n)), DMA((2, n)),
            fl(pad_rows, 128),
            bf(n, send_rows, width),
            fl(n, send_rows, width),
            fl(n, send_rows, width),
            bf(n, block, width),
            bf(m, n, send_rows, width),
            bf(n, local, width),
            bf(n, local, width),
            pltpu.VMEM((n, 8) + seg.shape[1:], jnp.int32),
            bf(n, block, width),
            fl(width + 8, width),
            fl(padded(row_end + 8, 8), width),
            bf(width, width),
            bf(width, width),
            bf(width, 3 * wide),
            bf(wide, width),
            fl(rows, width),
            bf(rows, width),
            bf(rows, width),
            fl(rows, width),
            bf(rows, width),
            bf(rows, width),
            bf(rows, width),
            fl(rows, width),
            fl(rows, width),
            fl(3, rows, wide),
            bf(heads, rows, wide),
            bf(heads, rows, wide),
            bf(heads, rows, wide),
            bf(heads, rows, wide),
            bf(rows, wide),
            bf(rows, wide),
            fl(rows, wide),
            fl(rows, wide),
            fl(rows, wide),
            fl(rows, wide),
            bf(rows, 3 * wide),
            fl(width // 128, width, 128),
            fl(width // 128, width, 128),
            bf(n, local, width),
            bf(n, local, width),
            bf(n, block, width),
            bf(m, piece, width),
            bf(4, piece, width),
            bf(2, piece, width),
            bf(piece, width),
            fl(piece, width),
            bf(n, block, width),
            bf(n, send_rows, width),
            bf(n, send_rows, width),
            fl(n, 8, 128),
            fl(8, 128),
            fl(m, 8, 128),
            DMA((8,)),
            DMA((n,)),
            DMA((n,)),
            DMA((4 * n,)),
            DMA((4 * n,)),
            DMA((2 * n,)),
            DMA((2 * n,)),
            DMA((2 * n,)),
            DMA((2 * n,)),
            DMA((3, n)),
            DMA((3, n)),
            DMA((n,)),
            DMA((n,)),
            DMA((4,)),
            DMA((4,)),
            DMA((3,)),
            DMA((3,)),
            DMA((3,)),
            DMA((3,)),
            DMA((2, n)),
            DMA((2, n)),
            DMA((n,)),
            DMA((n,)),
            DMA((n,)),
            DMA((n,)),
            DMA((n,)),
            DMA((n,)),
            DMA((m,)),
            DMA((m,)),
        ],
        compiler_params=pltpu.CompilerParams(
            collective_id=1, has_side_effects=True, vmem_limit_bytes=62 * 2**20
        ),
        name="layer_parts",
    )(flat, turn_in, unperm, tok, grd, seg, pos, used)


def one_hot(size, natural):
    return (np.arange(size)[:, None] == np.asarray(natural)[None, :]).astype(np.float32)


def strided(size, step):
    each = size // step
    column = np.arange(size)
    return one_hot(size, (column % each) * step + column // each)


def on_device_split(tokens, grad_out, segment_ids, positions, counts, master, moment_one, moment_two):
    bf16 = jnp.bfloat16
    dp_count, group_count = lax.axis_size("dp"), lax.axis_size("group")
    width = tokens.shape[1]
    n = group_count
    plan = row_plan(width, FF, dp_count, n, master.shape[0])
    turn_in = jnp.asarray(strided(width, n), bf16)
    unit = width // n
    unperm = jnp.asarray(np.pad(strided(unit, n), ((0, 256 - unit), (0, 0))), bf16)

    flat = master.reshape(-1, 128)
    seg, pos = segment_ids.reshape(1, -1), positions.reshape(1, -1)
    grad_rows, block_out, grad_in, squares = layer_call(
        plan, dp_count, n, flat, turn_in, unperm, tokens, grad_out, seg, pos, counts
    )
    grad_shard = grad_rows.reshape(-1)
    return (block_out, grad_in) + update(grad_shard, squares[0, 0], master, moment_one, moment_two)


def update(grad_shard, square_sum, master, moment_one, moment_two):
    grad_scale = 1.0 / (jnp.sqrt(square_sum) + 1e-06)
    scaled = grad_shard * grad_scale
    new_one = BETA_ONE * moment_one + (1.0 - BETA_ONE) * scaled
    new_two = BETA_TWO * moment_two + (1.0 - BETA_TWO) * scaled * scaled
    correct_one = 1.0 - BETA_ONE**STEP
    correct_two = 1.0 - BETA_TWO**STEP
    new_master = master - LEARN_RATE * (
        new_one / correct_one / (jnp.sqrt(new_two / correct_two) + ADAM_EPS) + DECAY_RATE * master
    )
    return (grad_shard, new_master, new_one, new_two)


def on_device(tokens, grad_out, segment_ids, positions, counts, master, moment_one, moment_two):
    dp_count, group_count = lax.axis_size("dp"), lax.axis_size("group")
    width = tokens.shape[1]
    splits = (
        (dp_count, group_count) == (8, 4)
        and tokens.shape[0] == 128
        and width // group_count <= 256
        and row_plan(width, FF, dp_count, group_count, master.shape[0]) is not None
    )
    body = on_device_split if splits else on_device_gathered
    return body(tokens, grad_out, segment_ids, positions, counts, master, moment_one, moment_two)


def solution(mesh):
    placed = (
        P(("dp", "group"), None),
        P(("dp", "group"), None),
        P(("dp", "group")),
        P(("dp", "group")),
        P(("dp", "group")),
        P(("dp", "group")),
        P(("dp", "group")),
        P(("dp", "group")),
    )
    return jax.shard_map(
        on_device,
        mesh=mesh,
        in_specs=placed,
        out_specs=(
            P(("dp", "group"), None),
            P(("dp", "group"), None),
            P(("dp", "group")),
            P(("dp", "group")),
            P(("dp", "group")),
            P(("dp", "group")),
        ),
        check_vma=False,
    )
```

```python
import functools

import jax
import jax.numpy as jnp
import numpy as np
from jax import lax
from jax.experimental import pallas as pl
from jax.experimental.pallas import tpu as pltpu
from jax.sharding import PartitionSpec as P

FF = 3072
HEAD = 64
ROT = 16
STEP = 3


BETA_ONE = 0.9
BETA_TWO = 0.95
LEARN_RATE = 0.01
DECAY_RATE = 0.1
ADAM_EPS = 1e-08
NORM_EPS = 1e-05
SCORE_SCALE = 0.125
MASKED = -1e30
TILE_ROWS = 16
MESH = pl.DeviceIdType.MESH
DMA = pltpu.SemaphoreType.DMA
ANY = pl.BlockSpec(memory_space=pl.ANY)
INVMEM = pl.BlockSpec(memory_space=pltpu.VMEM)


def param_layout(model_width, hidden):
    return [
        ("weight_qkv", (model_width, 3 * model_width)),
        ("bias_qkv", (3 * model_width,)),
        ("weight_out", (model_width, model_width)),
        ("bias_out", (model_width,)),
        ("weight_up", (model_width, hidden)),
        ("bias_up", (hidden,)),
        ("weight_down", (hidden, model_width)),
        ("bias_down", (model_width,)),
        ("gain_attn", (model_width,)),
        ("shift_attn", (model_width,)),
        ("gain_mlp", (model_width,)),
        ("shift_mlp", (model_width,)),
    ]


def unpack_params(flat_params, model_width, hidden):
    result = {}
    offset = 0
    for entry_name, entry_shape in param_layout(model_width, hidden):
        length = 1
        for extent in entry_shape:
            length = length * extent
        result[entry_name] = flat_params[offset : offset + length].reshape(entry_shape)
        offset = offset + length
    return result


def pack_grads(grad_dict, model_width, hidden, total_len):
    pieces = []
    used_count = 0
    for entry_name, entry_shape in param_layout(model_width, hidden):
        flat_grad = grad_dict[entry_name].reshape(-1)
        pieces.append(flat_grad)
        used_count = used_count + flat_grad.shape[0]
    pieces.append(jnp.zeros((total_len - used_count,), jnp.float32))
    return jnp.concatenate(pieces)


def rotary_tables(pos_ids):
    half_rot = ROT // 2
    inverse_freq = 10000.0 ** (-jnp.arange(half_rot, dtype=jnp.float32) * 2.0 / ROT)
    angles = pos_ids.astype(jnp.float32)[:, None] * inverse_freq[None, :]
    return (jnp.cos(angles), jnp.sin(angles))


def rotate(values, cosine, sine_rows):
    half_rot = ROT // 2
    lower_part = values[..., :half_rot]
    upper_part = values[..., half_rot:ROT]
    cos_rows = cosine[:, None, :]
    sin_rows = sine_rows[:, None, :]
    return jnp.concatenate(
        [
            lower_part * cos_rows - upper_part * sin_rows,
            upper_part * cos_rows + lower_part * sin_rows,
            values[..., ROT:],
        ],
        -1,
    )


def rotate_back(values, cosine, sine_rows):
    half_rot = ROT // 2
    lower_part = values[..., :half_rot]
    upper_part = values[..., half_rot:ROT]
    cos_rows = cosine[:, None, :]
    sin_rows = sine_rows[:, None, :]
    return jnp.concatenate(
        [
            lower_part * cos_rows + upper_part * sin_rows,
            upper_part * cos_rows - lower_part * sin_rows,
            values[..., ROT:],
        ],
        -1,
    )


def layer_stats(block_in):
    centred = block_in - jnp.mean(block_in, -1, keepdims=True)
    inv_std = lax.rsqrt(jnp.mean(centred * centred, -1, keepdims=True) + NORM_EPS)
    return (centred * inv_std, inv_std)


def norm_backward(grad_normed, normed, inv_std):
    return inv_std * (
        grad_normed
        - jnp.mean(grad_normed, -1, keepdims=True)
        - normed * jnp.mean(grad_normed * normed, -1, keepdims=True)
    )


def gelu_slope(up_pre):
    return (
        0.5 * (1.0 + lax.erf(up_pre * 0.7071067811865476))
        + up_pre * jnp.exp(-0.5 * up_pre * up_pre) * 0.3989422804014327
    )


def masked_scores(query_part, key_part, query_seg, key_seg, query_slot, key_slot):
    scores = (
        jnp.einsum("qhd,khd->hqk", query_part, key_part, preferred_element_type=jnp.float32)
        * SCORE_SCALE
    )
    allowed = (query_seg[:, None] == key_seg[None, :]) & (key_slot[None, :] <= query_slot[:, None])
    return (jnp.where(allowed[None], scores, MASKED), allowed)


def score_grads(scores, allowed, log_total, row_delta, grad_context, value_part):
    attn_probs = jnp.where(allowed[None], jnp.exp(scores - log_total[..., None]), 0.0)
    grad_probs = jnp.einsum(
        "qhd,khd->hqk", grad_context, value_part, preferred_element_type=jnp.float32
    )
    grad_scores = (attn_probs * (grad_probs - row_delta[..., None]) * SCORE_SCALE).astype(
        jnp.bfloat16
    )
    return (attn_probs.astype(jnp.bfloat16), grad_scores)


def on_device_gathered(tokens, grad_out, segment_ids, positions, counts, master, moment_one, moment_two):
    local_rows = tokens.shape[0]
    model_width = tokens.shape[1]
    head_count = model_width // HEAD
    local_master = master.astype(jnp.bfloat16)
    sectioned = lax.all_gather(local_master.reshape(1, 1, -1), "group", axis=1, tiled=True)
    sectioned = lax.all_gather(sectioned, "dp", axis=0, tiled=True)
    flat_params = sectioned.reshape(-1)
    params = unpack_params(flat_params, model_width, FF)
    block_in = tokens.astype(jnp.float32)
    normed, inv_std = layer_stats(block_in)
    gain_attn = params["gain_attn"].astype(jnp.float32)
    gain_mlp = params["gain_mlp"].astype(jnp.float32)
    attn_in = (normed * gain_attn + params["shift_attn"].astype(jnp.float32)).astype(jnp.bfloat16)
    mlp_in = (normed * gain_mlp + params["shift_mlp"].astype(jnp.float32)).astype(jnp.bfloat16)
    qkv_pre = (
        jnp.dot(attn_in, params["weight_qkv"], preferred_element_type=jnp.float32)
        + params["bias_qkv"].astype(jnp.float32)
    ).reshape(local_rows, 3, head_count, HEAD)
    cosine, sine_rows = rotary_tables(positions)
    queries = rotate(qkv_pre[:, 0], cosine, sine_rows).astype(jnp.bfloat16)
    keys_own = rotate(qkv_pre[:, 1], cosine, sine_rows).astype(jnp.bfloat16)
    values_own = qkv_pre[:, 2].astype(jnp.bfloat16)
    key_vals = jnp.stack(
        [keys_own.reshape(local_rows, model_width), values_own.reshape(local_rows, model_width)], 1
    )
    query_slot = lax.axis_index("group") * local_rows + jnp.arange(local_rows, dtype=jnp.int32)

    def split_keys(piece_kv):
        count_keys = piece_kv.shape[0]
        return (
            piece_kv[:, 0].reshape(count_keys, head_count, HEAD),
            piece_kv[:, 1].reshape(count_keys, head_count, HEAD),
        )

    run_max = jnp.full((head_count, local_rows), MASKED, jnp.float32)
    piece_kv = lax.all_gather(key_vals, "group", axis=0, tiled=True)
    piece_seg = lax.all_gather(segment_ids, "group", axis=0, tiled=True)
    piece_keys, piece_values = split_keys(piece_kv)
    key_slot = jnp.arange(piece_seg.shape[0], dtype=jnp.int32)
    scores, allowed = masked_scores(
        queries, piece_keys, segment_ids, piece_seg, query_slot, key_slot
    )
    new_max = jnp.maximum(run_max, jnp.max(scores, -1))
    weights = jnp.where(allowed[None], jnp.exp(scores - new_max[..., None]), 0.0)
    run_sum = jnp.sum(weights, -1)
    run_acc = jnp.einsum(
        "hqk,khd->hqd",
        weights.astype(jnp.bfloat16),
        piece_values,
        preferred_element_type=jnp.float32,
    )
    run_max, run_sum, run_acc = (new_max, run_sum, run_acc)
    log_total = run_max + jnp.log(run_sum)
    context = jnp.transpose(run_acc / run_sum[..., None], (1, 0, 2)).astype(jnp.bfloat16)
    context_flat = context.reshape(local_rows, model_width)
    attn_out = jnp.dot(
        context_flat, params["weight_out"], preferred_element_type=jnp.float32
    ) + params["bias_out"].astype(jnp.float32)
    up_pre = jnp.dot(mlp_in, params["weight_up"], preferred_element_type=jnp.float32) + params[
        "bias_up"
    ].astype(jnp.float32)
    up_act = jax.nn.gelu(up_pre, approximate=False).astype(jnp.bfloat16)
    mlp_out = jnp.dot(up_act, params["weight_down"], preferred_element_type=jnp.float32) + params[
        "bias_down"
    ].astype(jnp.float32)
    block_out = (block_in + attn_out + mlp_out).astype(jnp.bfloat16)
    valid_rows = (jnp.arange(local_rows) < counts[0]).astype(jnp.float32)
    grad_rows = grad_out.astype(jnp.float32) * valid_rows[:, None]
    grad_low = grad_rows.astype(jnp.bfloat16)
    bias_grad = jnp.sum(grad_rows, 0)
    grad_dict = {}
    grad_dict["weight_down"] = jnp.dot(up_act.T, grad_low, preferred_element_type=jnp.float32)
    grad_dict["bias_down"] = bias_grad
    grad_dict["weight_out"] = jnp.dot(context_flat.T, grad_low, preferred_element_type=jnp.float32)
    grad_dict["bias_out"] = bias_grad
    grad_act = jnp.dot(grad_low, params["weight_down"].T, preferred_element_type=jnp.float32)
    grad_pre = (grad_act * gelu_slope(up_pre)).astype(jnp.bfloat16)
    grad_dict["weight_up"] = jnp.dot(mlp_in.T, grad_pre, preferred_element_type=jnp.float32)
    grad_dict["bias_up"] = jnp.sum(grad_pre.astype(jnp.float32), 0)
    grad_mlp_in = jnp.dot(grad_pre, params["weight_up"].T, preferred_element_type=jnp.float32)
    grad_context = jnp.dot(
        grad_low, params["weight_out"].T, preferred_element_type=jnp.float32
    ).astype(jnp.bfloat16)
    grad_context = grad_context.reshape(local_rows, head_count, HEAD)
    row_delta = jnp.einsum(
        "qhd,qhd->hq", grad_context.astype(jnp.float32), context.astype(jnp.float32)
    )
    piece_kv = lax.all_gather(key_vals, "group", axis=0, tiled=True)
    piece_seg = lax.all_gather(segment_ids, "group", axis=0, tiled=True)
    piece_keys, piece_values = split_keys(piece_kv)
    count_keys = piece_seg.shape[0]
    key_slot = jnp.arange(count_keys, dtype=jnp.int32)
    scores, allowed = masked_scores(
        queries, piece_keys, segment_ids, piece_seg, query_slot, key_slot
    )
    probs_low, grad_scores = score_grads(
        scores, allowed, log_total, row_delta, grad_context, piece_values
    )
    grad_queries = jnp.einsum(
        "hqk,khd->qhd", grad_scores, piece_keys, preferred_element_type=jnp.float32
    )
    part_keys = jnp.einsum("hqk,qhd->khd", grad_scores, queries, preferred_element_type=jnp.float32)
    part_values = jnp.einsum(
        "hqk,qhd->khd", probs_low, grad_context, preferred_element_type=jnp.float32
    )
    addition = jnp.stack(
        [part_keys.reshape(count_keys, model_width), part_values.reshape(count_keys, model_width)],
        1,
    )
    grad_kv = addition
    grad_queries, batch_kv = (grad_queries, grad_kv)
    grad_kv = lax.psum_scatter(
        batch_kv.astype(jnp.bfloat16), "group", scatter_dimension=0, tiled=True
    ).astype(jnp.float32)
    grad_keys = grad_kv[:, 0].reshape(local_rows, head_count, HEAD)
    grad_values = grad_kv[:, 1].reshape(local_rows, head_count, HEAD)
    grad_qkv = (
        jnp.stack(
            [
                rotate_back(grad_queries, cosine, sine_rows),
                rotate_back(grad_keys, cosine, sine_rows),
                grad_values,
            ],
            1,
        )
        .reshape(local_rows, 3 * model_width)
        .astype(jnp.bfloat16)
    )
    grad_dict["weight_qkv"] = jnp.dot(attn_in.T, grad_qkv, preferred_element_type=jnp.float32)
    grad_dict["bias_qkv"] = jnp.sum(grad_qkv.astype(jnp.float32), 0)
    grad_attn_in = jnp.dot(grad_qkv, params["weight_qkv"].T, preferred_element_type=jnp.float32)
    grad_dict["gain_attn"] = jnp.sum(grad_attn_in * normed, 0)
    grad_dict["shift_attn"] = jnp.sum(grad_attn_in, 0)
    grad_dict["gain_mlp"] = jnp.sum(grad_mlp_in * normed, 0)
    grad_dict["shift_mlp"] = jnp.sum(grad_mlp_in, 0)
    grad_normed = grad_attn_in * gain_attn + grad_mlp_in * gain_mlp
    grad_in = (grad_rows + norm_backward(grad_normed, normed, inv_std)).astype(jnp.bfloat16)
    dp_count = lax.axis_size("dp")
    group_count = lax.axis_size("group")
    partial_value = pack_grads(grad_dict, model_width, FF, master.shape[0] * dp_count * group_count)
    sectioned_grad = lax.psum_scatter(
        partial_value.reshape(dp_count, group_count, -1).astype(jnp.bfloat16),
        "group",
        scatter_dimension=1,
        tiled=True,
    )
    grad_shard = (
        lax.psum_scatter(sectioned_grad, "dp", scatter_dimension=0, tiled=True)
        .astype(jnp.float32)
        .reshape(-1)
    )
    square_sum = lax.psum(jnp.sum(grad_shard * grad_shard), ("dp", "group"))
    grad_scale = 1.0 / (jnp.sqrt(square_sum) + 1e-06)
    scaled = grad_shard * grad_scale
    new_one = BETA_ONE * moment_one + (1.0 - BETA_ONE) * scaled
    new_two = BETA_TWO * moment_two + (1.0 - BETA_TWO) * scaled * scaled
    correct_one = 1.0 - BETA_ONE**STEP
    correct_two = 1.0 - BETA_TWO**STEP
    new_master = master - LEARN_RATE * (
        new_one / correct_one / (jnp.sqrt(new_two / correct_two) + ADAM_EPS) + DECAY_RATE * master
    )
    return (block_out, grad_in, grad_shard, new_master, new_one, new_two)


def padded(count, step):
    return -(-count // step) * step


@functools.lru_cache(None)
def row_plan(width, hidden, dp_count, group_count, shard_len):
    half = width // 2
    row = width * group_count
    devices = dp_count * group_count
    if hidden != row or (width // HEAD) % group_count or shard_len % half or width % 128:
        return None
    base = [i * shard_len // row for i in range(devices)]
    shift = [i * shard_len % row // half for i in range(devices)]
    span = max(-(-(s * half + shard_len) // row) for s in shift)
    stride = shard_len // row
    starts, at = {}, 0
    for entry_name, entry_shape in param_layout(width, hidden):
        starts[entry_name] = at // width
        at += int(np.prod(entry_shape))
    piece_base = [d * group_count * shard_len // row for d in range(dp_count)]
    spans = all(
        base[i] == piece_base[i // group_count] + stride * (i % group_count) for i in range(devices)
    )
    aligned = (
        starts["weight_up"] % group_count == 0
        and starts["weight_down"] % group_count == 0
        and starts["bias_qkv"] % group_count == 0
        and (starts["weight_out"] + 1) % group_count == 0
        and span == stride + 1
        and spans
        and base == [stride * i + i // (2 * group_count) for i in range(devices)]
        and shift == [i % (2 * group_count) for i in range(devices)]
    )
    if not aligned:
        return None
    row_out = starts["bias_qkv"] // group_count
    return dict(
        base=base,
        shift=shift,
        span=span,
        stride=stride,
        starts=starts,
        piece_base=piece_base,
        row_out=row_out,
        row_up=starts["weight_up"] // group_count,
        row_down=starts["weight_down"] // group_count,
        out_chunk=max(i for i in range(devices) if base[i] <= row_out),
        send_rows=padded(span + 7, TILE_ROWS),
        over=[i for i in range(devices - 1) if base[i + 1] == base[i] + stride],
        period=2 * group_count,
    )


def chunk_place(plan, me):
    period = plan["period"]
    return plan["stride"] * me + me // period, lax.rem(me, period)


def flip(value, bit):
    return value + bit - 2 * bit * ((value // bit) % 2)


def remote(src, dst, send_sem, recv_sem, device):
    return pltpu.make_async_remote_copy(
        src_ref=src,
        dst_ref=dst,
        send_sem=send_sem,
        recv_sem=recv_sem,
        device_id=device,
        device_id_type=MESH,
    )


def greet(devices):
    barrier = pltpu.get_barrier_semaphore()
    for device in devices:
        pl.semaphore_signal(barrier, inc=1, device_id=device, device_id_type=MESH)
    pl.semaphore_wait(barrier, len(devices))


def places(group_count):
    d, z = lax.axis_index("dp"), lax.axis_index("group")
    to = [lax.rem(z + k, group_count) for k in range(group_count)]
    frm = [lax.rem(z - k + group_count, group_count) for k in range(group_count)]
    return d, z, to, frm


def layer_kernel(
    plan, dp_count, group_count, flat, turn_in, unperm, tok, grd, seg, pos, used, grad, block_out, grad_in,
    square_sum, swap_a, swap_b, rs, rr, ls, lr, pad, send, stage, near, obuf, whole, toks, grds, idss, outs, w32, gm32, w_up, w_down,
    w_qkv, w_out, normed, attn_in, mlp_in, slope, act, g_pre, g_low, acc, g_mlp, tabs, qm, km,
    vm, gm, k_all, v_all, ctx, gq, gk, gv, g_qkv, rel_a, rel_b, parts_a, parts_b, gout, held,
    from_core, from_first, from_last, total, gbuf, slabs, back, sq, sqz, sqd, loc, p1s, p1r,
    cs, cr, xs, xr, ys, yr, ts, tr, os, orr, fcs, fcr, fxs, fxr, fys, fyr, zs, zr, gs, gr, bs,
    br, qs, qr, ds, dr,
):
    d, z, to, frm = places(group_count)
    n = group_count
    dc, dx, dy = flip(d, 1), flip(d, 2), flip(d, 4)
    dxy = flip(dx, 4)
    m = dp_count
    turn_to = [lax.rem(d + k, m) for k in range(m)]
    turn_from = [lax.rem(d - k + m, m) for k in range(m)]
    greet([(d, to[k]) for k in range(1, n)] + [(turn_to[k], z) for k in range(1, m)])
    later = []

    def share(j, ref):
        for k in range(1, n):
            copy = remote(ref.at[z], ref.at[z], ts.at[j, k], tr.at[j, k], (d, to[k]))
            copy.start()
            other = remote(ref.at[z], ref.at[frm[k]], ts.at[j, k], tr.at[j, k], (d, to[k]))
            later.append((copy, other))

    def settle():
        for copy, other in later:
            other.wait_recv()
            copy.wait_send()
        later.clear()

    def hop_start(j, ref, s):
        @pl.when((z < n - 1) & (z - s + 1 >= 0))
        def _():
            block = ref.at[z - s + 1]
            remote(block, block, rs.at[j, s], rr.at[j, s], (d, z + 1)).start()

        @pl.when((z > 0) & (z + s - 1 <= n - 1))
        def _():
            block = ref.at[z + s - 1]
            remote(block, block, ls.at[j, s], lr.at[j, s], (d, z - 1)).start()

    def hop_arrived(j, ref, s):
        @pl.when(z - s >= 0)
        def _():
            block = ref.at[z - s]
            remote(block, block, rs.at[j, s], rr.at[j, s], (d, z - 1)).wait_recv()

        @pl.when(z + s <= n - 1)
        def _():
            block = ref.at[z + s]
            remote(block, block, ls.at[j, s], lr.at[j, s], (d, z + 1)).wait_recv()

    def hop_sent(j, ref, s):
        @pl.when((z < n - 1) & (z - s + 1 >= 0))
        def _():
            block = ref.at[z - s + 1]
            remote(block, block, rs.at[j, s], rr.at[j, s], (d, z + 1)).wait_send()

        @pl.when((z > 0) & (z + s - 1 <= n - 1))
        def _():
            block = ref.at[z + s - 1]
            remote(block, block, ls.at[j, s], lr.at[j, s], (d, z - 1)).wait_send()

    def hop_on(j, ref, s):
        hop_arrived(j, ref, s)
        if s < n - 1:
            hop_start(j, ref, s + 1)

    toks[z] = tok[...]
    idss[z] = jnp.concatenate(
        [seg[...], pos[...], jnp.zeros((6, seg.shape[1]), jnp.int32)], 0
    )
    hop_start(0, toks, 1)
    share(0, idss)
    slot = lax.broadcasted_iota(jnp.int32, (tok.shape[0], 1), 0)
    grds[z] = jnp.where(slot < used[0], grd[...].astype(jnp.float32), 0.0).astype(jnp.bfloat16)
    span, stride = plan["span"], plan["stride"]
    send_rows, width = send.shape[1:]
    unit = width // n
    tiles = width // 128
    group = tiles * n
    length = flat.shape[0]
    me = d * n + z
    base, shift = chunk_place(plan, me)
    pad[0:group] = jnp.zeros((group, 128), jnp.float32)
    pad[group : group + length] = flat[...]
    rest = pad.shape[0] - group - length
    pad[group + length :] = jnp.zeros((rest, 128), jnp.float32)
    row = base + lax.broadcasted_iota(jnp.int32, (send_rows, 1), 0)
    whole_lines = ((row >= plan["row_out"]) & (row < plan["row_up"])) | (row >= plan["row_down"])
    up_rows = (row >= plan["row_up"]) & (row < plan["row_down"])
    first_row = group - tiles // 2 * shift
    for b in range(n):
        stage[b] = jnp.concatenate(
            [
                pad[pl.ds(first_row + tiles * b + t, send_rows, stride=group), :]
                for t in range(tiles)
            ],
            1,
        )
    for b in range(n):
        line = stage[b]
        turned = jnp.dot(
            line.astype(jnp.bfloat16), turn_in[...], preferred_element_type=jnp.float32
        )
        near[b] = jnp.where(up_rows, turned, line)
    extra = jnp.concatenate(
        [stage[j % n, stride - 1 + j // n : stride + j // n, :] for j in range(send_rows - span)], 0
    )
    for g in range(n):
        by_column = jnp.concatenate([near[b][:, g * unit : (g + 1) * unit] for b in range(n)], 1)
        value = jnp.where(whole_lines, stage[g], by_column)
        value = jnp.concatenate([value[:stride], jnp.concatenate([value[stride:span], extra], 0)], 0)
        send[g] = value.astype(jnp.bfloat16)
    first = []
    for k in range(1, n):
        copy = remote(send.at[to[k]], whole.at[d, z], p1s.at[k], p1r.at[k], (d, to[k]))
        copy.start()
        first.append(copy)
    whole[d, z] = send[z]
    sent = []

    def push(ref, s, r, device):
        copy = remote(ref, ref, s, r, device)
        copy.start()
        sent.append(copy)

    def arrived(ref, s, r, device):
        remote(ref, ref, s, r, device).wait_recv()

    for k in range(n):
        ref = whole.at[d, frm[k]]
        if k > 0:
            arrived(ref, p1s.at[k], p1r.at[k], (d, to[k]))
        push(ref, xs.at[k], xr.at[k], (dx, z))
        push(ref, ys.at[k], yr.at[k], (dy, z))
        push(ref, cs.at[k], cr.at[k], (dc, z))
    settle()
    hop_on(0, toks, 1)
    for k in range(n):
        by_x, by_y = whole.at[dx, frm[k]], whole.at[dy, frm[k]]
        arrived(by_x, xs.at[k], xr.at[k], (dx, z))
        if k < n // 2:
            push(by_x, ys.at[n + k], yr.at[n + k], (dy, z))
        push(by_x, cs.at[n + k], cr.at[n + k], (dc, z))
        arrived(by_y, ys.at[k], yr.at[k], (dy, z))
        if k >= n // 2:
            push(by_y, xs.at[n + k], xr.at[n + k], (dx, z))
        push(by_y, cs.at[2 * n + k], cr.at[2 * n + k], (dc, z))
    hop_on(0, toks, 2)
    hop_start(1, grds, 1)
    for k in range(n):
        across = whole.at[dxy, frm[k]]
        if k < n // 2:
            arrived(across, ys.at[n + k], yr.at[n + k], (dy, z))
        else:
            arrived(across, xs.at[n + k], xr.at[n + k], (dx, z))
        push(across, cs.at[3 * n + k], cr.at[3 * n + k], (dc, z))
    for j, owner in enumerate((d, dx, dy, dxy)):
        for k in range(n):
            ref = whole.at[flip(owner, 1), frm[k]]
            arrived(ref, cs.at[j * n + k], cr.at[j * n + k], (dc, z))
    hop_on(1, grds, 1)
    for copy in first + sent:
        copy.wait_send()
    chunks = [plan["out_chunk"] + j for j in range(4)]
    chunks = [whole[i // n, i % n].astype(jnp.float32) for i in chunks]
    block = unit // n
    lines = []
    for j in range(1, 4):
        count = min(stride, unit - stride * (j - 1))
        part = chunks[j][:count]
        if j > 1:
            head = chunks[j - 1][stride : stride + 8]
            row8 = lax.broadcasted_iota(jnp.int32, (8, 1), 0)
            part = jnp.concatenate([part[:8] + jnp.where(row8 == 0, head, 0.0), part[8:]], 0)
        lines.append(part)
    lines = jnp.concatenate(lines, 0)
    before = chunks[0][stride : stride + 1]
    moved = pltpu.roll(lines, 1, 0)
    at = lax.broadcasted_iota(jnp.int32, (unit, 1), 0)
    moved = jnp.where(at == 0, before, moved)
    lines = jnp.where(z == n - 1, moved, lines).astype(jnp.bfloat16)
    for g in range(n):
        obuf[g] = lines[g * block : (g + 1) * block]
    outs[z] = obuf[z]
    outs_moving = []
    for k in range(1, n):
        copy = remote(obuf.at[to[k]], outs.at[z], os.at[k], orr.at[k], (d, to[k]))
        copy.start()
        outs_moving.append(
            (copy, remote(obuf.at[to[k]], outs.at[frm[k]], os.at[k], orr.at[k], (d, to[k])))
        )
    f32, bf16 = jnp.float32, jnp.bfloat16
    rows = normed.shape[0]
    local = rows // n
    wide = 256
    heads = unit // HEAD
    bases = plan["base"]
    row_out, row_up, row_down, over = plan["row_out"], plan["row_up"], plan["row_down"], plan["over"]

    def mm(lhs, rhs):
        return jnp.dot(lhs, rhs, preferred_element_type=f32)

    def mm_t(lhs, rhs):
        return lax.dot_general(lhs, rhs, (((1,), (1,)), ((), ())), preferred_element_type=f32)

    def t_mm(lhs, rhs):
        return lax.dot_general(lhs, rhs, (((0,), (0,)), ((), ())), preferred_element_type=f32)

    def chunk(i):
        return whole[i // n, i % n].astype(f32)

    def fill(low, high):
        for i, first in enumerate(bases):
            last = first + (stride if i in over else span)
            lo, hi = max(low, first), min(high, last)
            if lo >= hi:
                continue
            w32[lo - low : hi - low] = chunk(i)[lo - first : hi - first]
            if lo == first and i - 1 in over:
                tail = whole[(i - 1) // n, (i - 1) % n, stride : stride + 8].astype(f32)[:1]
                w32[lo - low : lo - low + 1] = w32[lo - low : lo - low + 1] + tail

    def line(row):
        i = max(i for i in range(len(bases)) if bases[i] <= row)
        return chunk(i)[row - bases[i] : row - bases[i] + 1]

    fill(row_up, row_up + width)
    w_up[...] = w32[:width].astype(bf16)
    fill(row_down, row_down + width)
    w_down[...] = w32[:width].astype(bf16)
    fill(0, row_out)
    third = width // n
    gap = jnp.zeros((third, wide - unit), f32)
    for t in range(tiles):
        rel_a[t, :row_out] = w32[:row_out, t * 128 : (t + 1) * 128]

    def strided_rows(ref, start, step):
        return jnp.concatenate(
            [ref[t, pl.ds(start, third, stride=step), :] for t in range(tiles)], 1
        )

    def put_rows(ref, start, step, value):
        for t in range(tiles):
            ref[t, pl.ds(start, third, stride=step), :] = value[:, t * 128 : (t + 1) * 128]

    planes = [strided_rows(rel_a, p, 3) for p in range(3)]
    for t in range(n):
        blocks = []
        for j in range(3):
            p, b = (3 * t + j) // n, (3 * t + j) % n
            blocks += [planes[p][:, b * unit : (b + 1) * unit], gap]
        put_rows(rel_b, t, n, jnp.concatenate(blocks, 1))
    for t in range(tiles):
        w_qkv[:, t * 128 : (t + 1) * 128] = rel_b[t].astype(bf16)
    bias_up = line(row_up + width)
    vectors = chunk(len(bases) - 1)[span : span + n + 1]
    bias_down, gain_attn, shift_attn, gain_mlp, shift_mlp = (vectors[j : j + 1] for j in range(5))
    is_last = z == n - 1
    bias_rest = jnp.where(is_last, bias_down + line(row_up - 1), 0.0)
    bias_lines = chunk(plan["out_chunk"])[span + n : span + n + 3]
    bias_qkv = []
    for j in range(3):
        mine = jnp.zeros((1, unit), f32)
        for g in range(n):
            mine = jnp.where(z == g, bias_lines[j : j + 1, g * unit : (g + 1) * unit], mine)
        bias_qkv += [mine, jnp.zeros((1, wide - unit), f32)]
    bias_qkv = jnp.concatenate(bias_qkv, 1)

    step = 64
    hop_on(0, toks, 3)
    hop_on(1, grds, 2)

    @pl.loop(0, rows // step)
    def _(i):
        at = pl.ds(i * step, step)
        x = toks[i // (local // step), pl.ds(i % (local // step) * step, step), :].astype(f32)
        centred = x - jnp.mean(x, -1, keepdims=True)
        inv = lax.rsqrt(jnp.mean(centred * centred, -1, keepdims=True) + NORM_EPS)
        value = centred * inv
        normed[at, :] = value
        attn_in[at, :] = (value * gain_attn + shift_attn).astype(bf16)
        mlp_in[at, :] = (value * gain_mlp + shift_mlp).astype(bf16)

    w32[0:8] = jnp.broadcast_to(bias_up, (8, width))
    w32[8:16] = jnp.broadcast_to(bias_qkv, (8, width))

    @pl.loop(0, width // wide)
    def _(i):
        at = pl.ds(pl.multiple_of(i * wide, wide), wide)
        up = mm(mlp_in[...], w_up[:, at]) + w32[0:1, at]
        half = 0.5 * (1.0 + lax.erf(up * 0.7071067811865476))
        act[:, at] = (up * half).astype(bf16)
        slope[:, at] = half + up * jnp.exp(-0.5 * up * up) * 0.3989422804014327

    @pl.loop(0, width // wide)
    def _(i):
        at = pl.ds(pl.multiple_of(i * wide, wide), wide)
        acc[:, at] = mm(act[...], w_down[:, at])

    position = jnp.concatenate([idss[g, 1:2, :] for g in range(n)], 1).astype(f32)
    half_rot = ROT // 2
    at_freq = lax.broadcasted_iota(jnp.int32, (half_rot, 1), 0)
    freq = jnp.zeros((half_rot, 1), f32)
    for i in range(half_rot):
        freq = jnp.where(at_freq == i, float(10000.0 ** (-2.0 * i / ROT)), freq)
    angles = freq * position
    lane = lax.broadcasted_iota(jnp.int32, (half_rot, wide), 1) % HEAD
    same = lane % half_rot == lax.broadcasted_iota(jnp.int32, (half_rot, wide), 0)
    hot = [same & (lane < ROT), same & (lane < half_rot), same & (lane >= half_rot) & (lane < ROT)]

    def expand(table, where):
        return lax.dot_general(
            table,
            where.astype(f32),
            (((0,), (0,)), ((), ())),
            precision=lax.Precision.HIGHEST,
            preferred_element_type=f32,
        )

    cosine, sine = jnp.cos(angles), jnp.sin(angles)
    lane_wide = lax.broadcasted_iota(jnp.int32, (1, wide), 1)
    head_lane = lane_wide % HEAD
    tabs[0] = expand(cosine, hot[0]) + jnp.where(head_lane >= ROT, 1.0, 0.0)
    tabs[1] = expand(sine, hot[1])
    tabs[2] = expand(sine, hot[2])

    def turn(value, at, sign):
        ahead = pltpu.roll(value, wide - half_rot, 1)
        behind = pltpu.roll(value, half_rot, 1)
        return value * tabs[0, at] + sign * (behind * tabs[2, at] - ahead * tabs[1, at])

    def masked(ref, value):
        for h in range(heads):
            ref[h] = jnp.where(lane_wide // HEAD == h, value, 0.0).astype(bf16)

    every = slice(0, rows)
    q32 = turn(mm(attn_in[...], w_qkv[:, :wide]) + w32[8:9, :wide], every, 1.0)
    masked(qm, q32)
    k32 = turn(mm(attn_in[...], w_qkv[:, wide : 2 * wide]) + w32[8:9, wide : 2 * wide], every, 1.0)
    masked(km, k32)
    k_all[...] = k32.astype(bf16)
    v32 = mm(attn_in[...], w_qkv[:, 2 * wide :]) + w32[8:9, 2 * wide :]
    masked(vm, v32)
    v_all[...] = v32.astype(bf16)
    for copy, other in outs_moving:
        other.wait_recv()
        copy.wait_send()
    order = [(t - 1) % n for t in range(n)]
    out_rows = jnp.concatenate([outs[j] for j in order], 0)
    w_out[...] = mm(unperm[...], out_rows).astype(bf16)
    hop_on(1, grds, 3)
    for g in range(n):
        g_low[g * local : (g + 1) * local] = grds[g]
    masked(gm, mm_t(g_low[...], w_out[...]).astype(bf16).astype(f32))

    @pl.loop(0, width // wide)
    def _(i):
        at = pl.ds(pl.multiple_of(i * wide, wide), wide)
        g_pre[:, at] = (mm_t(g_low[...], w_down[at, :]) * slope[:, at]).astype(bf16)

    @pl.loop(0, width // wide)
    def _(i):
        at = pl.ds(pl.multiple_of(i * wide, wide), wide)
        g_mlp[:, at] = mm_t(g_pre[...], w_up[at, :])

    bias_grad = jnp.where(is_last, jnp.sum(g_low[...].astype(f32), 0, keepdims=True), 0.0)

    def swap_start(j, src, dst, b):
        @pl.when(z != b)
        def _():
            remote(src.at[b], dst.at[z], zs.at[j, b], zr.at[j, z], (d, b)).start()

        @pl.when(z == b)
        def _():
            dst[b] = src[b]

    def swap_end(j, src, dst):
        for b in range(n):
            @pl.when(z != b)
            def _():
                remote(src.at[b], dst.at[b], zs.at[j, b], zr.at[j, b], (d, b)).wait_recv()
                remote(src.at[b], dst.at[b], zs.at[j, b], zr.at[j, b], (d, b)).wait_send()

    seg_row = jnp.concatenate([idss[g, 0:1, :] for g in range(n)], 1).astype(f32)
    seg_col = jnp.transpose(jnp.broadcast_to(seg_row, (128, rows)))[:, 0:1]
    ctx[...] = jnp.zeros_like(ctx)
    gq[...] = jnp.zeros_like(gq)
    gk[...] = jnp.zeros_like(gk)
    gv[...] = jnp.zeros_like(gv)
    vecs = [[], [], [], []]
    ends_first = [b for pair in zip(range(n // 2), reversed(range(n))) for b in pair]
    for b in ends_first:
        at = slice(b * local, (b + 1) * local)
        upto = (b + 1) * local
        seen = slice(0, upto)
        earlier = lax.broadcasted_iota(jnp.int32, (local, upto), 1) <= b * local + (
            lax.broadcasted_iota(jnp.int32, (local, upto), 0)
        )
        allowed = (seg_col[at] == seg_row[:, seen]) & earlier

        @pl.loop(0, heads)
        def _(h):
            scores = jnp.where(allowed, mm_t(qm[h, at], k_all[seen]) * SCORE_SCALE, MASKED)
            top = jnp.max(scores, -1, keepdims=True)
            weights = jnp.exp(scores - top)
            probs = weights / jnp.sum(weights, -1, keepdims=True)
            low = probs.astype(bf16)
            context = mm(low, vm[h, seen])
            ctx[at] += context
            kept = context.astype(bf16).astype(f32)
            delta = jnp.sum(gm[h, at].astype(f32) * kept, -1, keepdims=True)
            slanted = (probs * (mm_t(gm[h, at], v_all[seen]) - delta) * SCORE_SCALE).astype(bf16)
            gq[at] += mm(slanted, km[h, seen])
            gk[seen] += t_mm(slanted, qm[h, at])
            gv[seen] += t_mm(low, gm[h, at])

        parts_a[b] = (acc[at] + mm(ctx[at].astype(bf16), w_out[...]) + bias_rest).astype(bf16)
        swap_start(0, parts_a, swap_a, b)

    ctx_low = ctx[...].astype(bf16)
    g_qkv[:, :wide] = turn(gq[...], every, -1.0).astype(bf16)
    g_qkv[:, wide : 2 * wide] = turn(gk[...], every, -1.0).astype(bf16)
    g_qkv[:, 2 * wide :] = gv[...].astype(bf16)
    for i in range(width // wide):
        at = slice(i * wide, (i + 1) * wide)
        g_attn = mm_t(g_qkv[...], w_qkv[at, :])
        g_up = g_mlp[:, at]
        value = (g_attn * gain_attn[:, at] + g_up * gain_mlp[:, at]).astype(bf16)
        for g in range(n):
            parts_b[g, :, at] = value[g * local : (g + 1) * local]
        here = normed[:, at]
        for j, term in enumerate((g_attn * here, g_attn, g_up * here, g_up)):
            vecs[j].append(jnp.sum(term, 0, keepdims=True))
    out_grad = t_mm(ctx_low, g_low[...]).astype(bf16)
    out_grad = t_mm(unperm[...], out_grad).astype(bf16)
    for g in range(n):
        t = (g + 1) % n
        gout[g] = out_grad[t * block : (t + 1) * block]
    gbuf[z] = gout[z]
    trades = []
    for k in range(1, n):
        copy = remote(gout.at[to[k]], gbuf.at[z], gs.at[k], gr.at[k], (d, to[k]))
        copy.start()
        trades.append((copy, remote(gout.at[to[k]], gbuf.at[frm[k]], gs.at[k], gr.at[k], (d, to[k]))))
    for b in range(n):
        swap_start(1, parts_b, swap_b, b)
    for i in range(width // wide):
        at = slice(i * wide, (i + 1) * wide)
        gm32[row_up + i * wide : row_up + (i + 1) * wide] = t_mm(mlp_in[:, at], g_pre[...])
        gm32[row_down + i * wide : row_down + (i + 1) * wide] = t_mm(act[:, at], g_low[...])
    gm32[row_up + width : row_up + width + 1] = jnp.sum(g_pre[...].astype(f32), 0, keepdims=True)
    for i in range(width // wide):
        at = slice(i * wide, (i + 1) * wide)
        value = t_mm(attn_in[:, at], g_qkv[...])
        for t in range(tiles):
            rel_b[t, at] = value[:, t * 128 : (t + 1) * 128]
    columns = [strided_rows(rel_b, t, n) for t in range(n)]
    for p in range(3):
        blocks = []
        for b in range(n):
            t, j = (n * p + b) // 3, (n * p + b) % 3
            blocks.append(columns[t][:, j * wide : j * wide + unit])
        put_rows(rel_a, p, 3, jnp.concatenate(blocks, 1))
    for t in range(tiles):
        gm32[:row_out, t * 128 : (t + 1) * 128] = rel_a[t, :row_out]
    gm32[row_out:row_up] = jnp.zeros((row_up - row_out, width), f32)
    gm32[row_up - 1 : row_up] = bias_grad
    row_end = row_down + width
    gm32[row_end:] = jnp.zeros((gm32.shape[0] - row_end, width), f32)
    sums = jnp.sum(g_qkv[...].astype(f32), 0, keepdims=True)
    sums = jnp.concatenate(
        [sums[:, j * wide : j * wide + unit] for j in range(3)] + [jnp.zeros((1, unit), f32)], 1
    )
    extra = [bias_grad] + [jnp.concatenate(v, 1) for v in vecs] + [sums, jnp.zeros((2, width), f32)]
    body = n * stride
    for e, first in enumerate(plan["piece_base"]):
        held[e, :body] = gm32[first : first + body].astype(bf16)
        last = [gm32[first + body : first + body + 1], jnp.zeros((7, width), f32)] + extra
        held[e, body:] = jnp.concatenate(last, 0).astype(bf16)
    y, x, c = d // 4, lax.rem(d // 2, 2), lax.rem(d, 2)
    rows = total.shape[0]
    cut = padded(rows // 2, TILE_ROWS)
    for copy, other in trades:
        other.wait_recv()
    out_rows = jnp.concatenate([gbuf[g].astype(f32) for g in range(n)], 0)
    at = lax.broadcasted_iota(jnp.int32, (unit, 1), 0)
    moved = jnp.where(at == unit - 1, 0.0, pltpu.roll(out_rows, unit - 1, 0))
    is_last = z == n - 1
    after = plan["out_chunk"] // n + 1
    held[after, :unit] = (
        held[after, :unit].astype(f32) + jnp.where(is_last, moved, out_rows)
    ).astype(bf16)
    at = lax.broadcasted_iota(jnp.int32, (TILE_ROWS, 1), 0)
    first_line = jnp.where((at == 0) & is_last, out_rows[:1], 0.0)
    held[after - 1, body:] = (held[after - 1, body:].astype(f32) + first_line).astype(bf16)

    low, high = pl.ds(0, cut), pl.ds(cut, rows - cut)
    here = 2 * y + x
    quads = [flip(flip(here, 1), 2), flip(here, 1), flip(here, 2), here]
    mine = [held.at[2 * q + c] for q in quads]
    cross = []
    for k in range(4):
        copy = remote(
            held.at[2 * quads[k] + 1 - c], from_core.at[k], fcs.at[k], fcr.at[k], (dc, z)
        )
        copy.start()
        cross.append(copy)

    def add(dst, src):
        dst[...] = (dst[...].astype(f32) + src[...].astype(f32)).astype(dst.dtype)

    sent = []

    def pass_on(src, dst, s, r, device):
        copy = remote(src, dst, s, r, device)
        copy.start()
        sent.append(copy)
        return copy

    by_x, by_y = (dx, z), (dy, z)
    for k in range(4):
        cross[k].wait_recv()
        add(mine[k], from_core.at[k])
        if k == 0:
            x0 = pass_on(mine[0].at[low], from_first.at[0, low], fxs.at[0], fxr.at[0], by_x)
            y0 = pass_on(mine[0].at[high], from_first.at[0, high], fys.at[0], fyr.at[0], by_y)
        elif k == 1:
            x1 = pass_on(mine[1].at[low], from_first.at[1, low], fxs.at[1], fxr.at[1], by_x)
        elif k == 2:
            y1 = pass_on(mine[2].at[high], from_first.at[1, high], fys.at[1], fyr.at[1], by_y)
    x0.wait_recv()
    add(mine[2].at[low], from_first.at[0, low])
    y2 = pass_on(mine[2].at[low], from_last.at[low], fys.at[2], fyr.at[2], by_y)
    y0.wait_recv()
    add(mine[1].at[high], from_first.at[0, high])
    x2 = pass_on(mine[1].at[high], from_last.at[high], fxs.at[2], fxr.at[2], by_x)
    x1.wait_recv()
    add(mine[3].at[low], from_first.at[1, low])
    y1.wait_recv()
    add(mine[3].at[high], from_first.at[1, high])
    y2.wait_recv()
    x2.wait_recv()
    total[...] = (mine[3][...].astype(f32) + from_last[...].astype(f32)).astype(bf16).astype(f32)

    odd = lax.rem(d, 2)
    at = lax.broadcasted_iota(jnp.int32, (rows, 1), 0)
    counted = jnp.where((at >= odd) & (at < body + 1), total[...], 0.0)
    sq[z] = jnp.full(sq.shape[1:], jnp.sum(counted * counted), f32)
    for k in range(1, n):
        copy = remote(sq.at[z], sq.at[z], qs.at[k], qr.at[k], (d, to[k]))
        copy.start()
        sent.append(copy)
    extra = total[body + 8 : body + 14]
    for j in range(n):
        slab = jnp.concatenate(
            [
                total[stride * j : stride * j + stride],
                jnp.concatenate(
                    [total[stride * j + stride : stride * j + span], extra, jnp.zeros((1, width), f32)], 0
                ),
            ],
            0,
        )
        slabs[j] = slab.astype(bf16)
    far = []
    for k in range(1, n):
        copy = remote(slabs.at[to[k]], back.at[z], bs.at[k], br.at[k], (d, to[k]))
        copy.start()
        far.append((copy, remote(slabs.at[to[k]], back.at[frm[k]], bs.at[k], br.at[k], (d, to[k]))))
    back[z] = slabs[z]
    for k in range(1, n):
        remote(sq.at[z], sq.at[frm[k]], qs.at[k], qr.at[k], (d, to[k])).wait_recv()
    sqz[...] = sq[0] + sq[1] + sq[2] + sq[3]
    sqd[d] = sqz[...]
    for k in range(1, m):
        copy = remote(sqz, sqd.at[d], ds.at[k], dr.at[k], (turn_to[k], z))
        copy.start()
        sent.append(copy)
    swap_end(0, parts_a, swap_a)
    swap_end(1, parts_b, swap_b)
    x = toks[z].astype(f32)
    value = x
    for g in range(n):
        value = value + swap_a[g].astype(f32)
    block_out[...] = value.astype(bf16)
    centred = x - jnp.mean(x, -1, keepdims=True)
    inv = lax.rsqrt(jnp.mean(centred * centred, -1, keepdims=True) + NORM_EPS)
    own_normed = centred * inv
    value = swap_b[0].astype(f32)
    for g in range(1, n):
        value = value + swap_b[g].astype(f32)
    value = norm_backward(value, own_normed, inv)
    grad_in[...] = (grds[z].astype(f32) + value).astype(bf16)
    for copy, other in far:
        other.wait_recv()

    for g in range(n):
        stage[g] = back[g].astype(f32)
    vec = stage[0, stride : stride + 8]
    for g in range(1, n):
        vec = vec + stage[g, stride : stride + 8]
    vec = vec[1:6]
    bias_rows = [stage[g, span + 5 : span + 6] for g in range(n)]
    squares = jnp.sum(vec * vec)
    for g in range(n):
        squares = squares + jnp.sum(bias_rows[g] * bias_rows[g])
    row_end = plan["row_down"] + width
    for b in range(n):
        part = slice(b * unit, (b + 1) * unit)
        by_column = jnp.concatenate([stage[g, :, part] for g in range(n)], 1)
        unturned = lax.dot_general(
            by_column.astype(bf16), turn_in[...], (((1,), (1,)), ((), ())), preferred_element_type=f32
        )
        value = jnp.where(up_rows, unturned, by_column)
        value = jnp.where(whole_lines, stage[b], value)
        if b < 3:
            bias_line = jnp.concatenate([bias_rows[g][:, part] for g in range(n)], 1)
            value = jnp.where(row == plan["row_out"], bias_line, value)
        value = jnp.where(row == row_end, vec[b : b + 1], value)
        if b == 0:
            value = jnp.where(row == row_end + 1, vec[n : n + 1], value)
        for t in range(tiles):
            pad[pl.ds(first_row + tiles * b + t, send_rows, stride=group), :] = value[
                :, t * 128 : (t + 1) * 128
            ]
    grad[...] = pad[group : group + grad.shape[0]]
    for k in range(1, m):
        remote(sqz, sqd.at[turn_from[k]], ds.at[k], dr.at[k], (turn_to[k], z)).wait_recv()
    result = sqd[0]
    for k in range(1, m):
        result = result + sqd[k]
    square_sum[...] = result + squares
    for copy in cross + sent:
        copy.wait_send()
    hop_tensors = ((0, toks), (1, grds))
    for j, ref in hop_tensors:
        for k in range(1, n):
            hop_sent(j, ref, k)
    for copy, other in trades + far:
        copy.wait_send()


def layer_call(plan, dp_count, group_count, flat, turn_in, unperm, tok, grd, seg, pos, used):
    n, m = group_count, dp_count
    local, width = tok.shape
    rows = local * n
    f32, bf16 = jnp.float32, jnp.bfloat16
    wide, heads = 256, width // n // HEAD
    block = width // n // n
    send_rows = plan["send_rows"]
    group = width // 128 * n
    pad_rows = padded(2 * group + group * send_rows, 8)
    row_end = plan["row_down"] + width
    piece = n * plan["stride"] + TILE_ROWS

    def fl(*shape):
        return pltpu.VMEM(shape, f32)

    def bf(*shape):
        return pltpu.VMEM(shape, bf16)

    return pl.pallas_call(
        functools.partial(layer_kernel, plan, m, n),
        out_shape=[
            jax.ShapeDtypeStruct(flat.shape, f32),
            jax.ShapeDtypeStruct((local, width), bf16),
            jax.ShapeDtypeStruct((local, width), bf16),
            jax.ShapeDtypeStruct((8, 128), f32),
        ],
        in_specs=[INVMEM] * 7 + [pl.BlockSpec(memory_space=pltpu.SMEM)],
        out_specs=[INVMEM] * 4,
        scratch_shapes=[
            bf(n, local, width),
            bf(n, local, width),
            DMA((2, n)), DMA((2, n)), DMA((2, n)), DMA((2, n)),
            fl(pad_rows, 128),
            bf(n, send_rows, width),
            fl(n, send_rows, width),
            fl(n, send_rows, width),
            bf(n, block, width),
            bf(m, n, send_rows, width),
            bf(n, local, width),
            bf(n, local, width),
            pltpu.VMEM((n, 8) + seg.shape[1:], jnp.int32),
            bf(n, block, width),
            fl(width + 8, width),
            fl(padded(row_end + 8, 8), width),
            bf(width, width),
            bf(width, width),
            bf(width, 3 * wide),
            bf(wide, width),
            fl(rows, width),
            bf(rows, width),
            bf(rows, width),
            fl(rows, width),
            bf(rows, width),
            bf(rows, width),
            bf(rows, width),
            fl(rows, width),
            fl(rows, width),
            fl(3, rows, wide),
            bf(heads, rows, wide),
            bf(heads, rows, wide),
            bf(heads, rows, wide),
            bf(heads, rows, wide),
            bf(rows, wide),
            bf(rows, wide),
            fl(rows, wide),
            fl(rows, wide),
            fl(rows, wide),
            fl(rows, wide),
            bf(rows, 3 * wide),
            fl(width // 128, width, 128),
            fl(width // 128, width, 128),
            bf(n, local, width),
            bf(n, local, width),
            bf(n, block, width),
            bf(m, piece, width),
            bf(4, piece, width),
            bf(2, piece, width),
            bf(piece, width),
            fl(piece, width),
            bf(n, block, width),
            bf(n, send_rows, width),
            bf(n, send_rows, width),
            fl(n, 8, 128),
            fl(8, 128),
            fl(m, 8, 128),
            DMA((8,)),
            DMA((n,)),
            DMA((n,)),
            DMA((4 * n,)),
            DMA((4 * n,)),
            DMA((2 * n,)),
            DMA((2 * n,)),
            DMA((2 * n,)),
            DMA((2 * n,)),
            DMA((3, n)),
            DMA((3, n)),
            DMA((n,)),
            DMA((n,)),
            DMA((4,)),
            DMA((4,)),
            DMA((3,)),
            DMA((3,)),
            DMA((3,)),
            DMA((3,)),
            DMA((2, n)),
            DMA((2, n)),
            DMA((n,)),
            DMA((n,)),
            DMA((n,)),
            DMA((n,)),
            DMA((n,)),
            DMA((n,)),
            DMA((m,)),
            DMA((m,)),
        ],
        compiler_params=pltpu.CompilerParams(
            collective_id=1, has_side_effects=True, vmem_limit_bytes=62 * 2**20
        ),
        name="layer_parts",
    )(flat, turn_in, unperm, tok, grd, seg, pos, used)


def one_hot(size, natural):
    return (np.arange(size)[:, None] == np.asarray(natural)[None, :]).astype(np.float32)


def strided(size, step):
    each = size // step
    column = np.arange(size)
    return one_hot(size, (column % each) * step + column // each)


def on_device_split(tokens, grad_out, segment_ids, positions, counts, master, moment_one, moment_two):
    bf16 = jnp.bfloat16
    dp_count, group_count = lax.axis_size("dp"), lax.axis_size("group")
    width = tokens.shape[1]
    n = group_count
    plan = row_plan(width, FF, dp_count, n, master.shape[0])
    turn_in = jnp.asarray(strided(width, n), bf16)
    unit = width // n
    unperm = jnp.asarray(np.pad(strided(unit, n), ((0, 256 - unit), (0, 0))), bf16)

    flat = master.reshape(-1, 128)
    seg, pos = segment_ids.reshape(1, -1), positions.reshape(1, -1)
    grad_rows, block_out, grad_in, squares = layer_call(
        plan, dp_count, n, flat, turn_in, unperm, tokens, grad_out, seg, pos, counts
    )
    grad_shard = grad_rows.reshape(-1)
    return (block_out, grad_in) + update(grad_shard, squares[0, 0], master, moment_one, moment_two)


def update(grad_shard, square_sum, master, moment_one, moment_two):
    grad_scale = 1.0 / (jnp.sqrt(square_sum) + 1e-06)
    scaled = grad_shard * grad_scale
    new_one = BETA_ONE * moment_one + (1.0 - BETA_ONE) * scaled
    new_two = BETA_TWO * moment_two + (1.0 - BETA_TWO) * scaled * scaled
    correct_one = 1.0 - BETA_ONE**STEP
    correct_two = 1.0 - BETA_TWO**STEP
    new_master = master - LEARN_RATE * (
        new_one / correct_one / (jnp.sqrt(new_two / correct_two) + ADAM_EPS) + DECAY_RATE * master
    )
    return (grad_shard, new_master, new_one, new_two)


def on_device(tokens, grad_out, segment_ids, positions, counts, master, moment_one, moment_two):
    dp_count, group_count = lax.axis_size("dp"), lax.axis_size("group")
    width = tokens.shape[1]
    splits = (
        (dp_count, group_count) == (8, 4)
        and tokens.shape[0] == 128
        and width // group_count <= 256
        and row_plan(width, FF, dp_count, group_count, master.shape[0]) is not None
    )
    body = on_device_split if splits else on_device_gathered
    return body(tokens, grad_out, segment_ids, positions, counts, master, moment_one, moment_two)


def solution(mesh):
    placed = (
        P(("dp", "group"), None),
        P(("dp", "group"), None),
        P(("dp", "group")),
        P(("dp", "group")),
        P(("dp", "group")),
        P(("dp", "group")),
        P(("dp", "group")),
        P(("dp", "group")),
    )
    return jax.shard_map(
        on_device,
        mesh=mesh,
        in_specs=placed,
        out_specs=(
            P(("dp", "group"), None),
            P(("dp", "group"), None),
            P(("dp", "group")),
            P(("dp", "group")),
            P(("dp", "group")),
            P(("dp", "group")),
        ),
        check_vma=False,
    )
```
